128 devices in a mesh: req: 32 (over x, z, core), tp: 4 (over y).
Axes of the slice: x: 4, y: 4, z: 4, core: 2. Of those that a mesh axis runs over, the one named last changes fastest.
Arguments:
- tokens: bfloat16 [65536, 1024], P('req'), may hold values from -6 to 6
- attn_gain: bfloat16 [1024], replicated, may hold values from 0.5 to 1.5
- w_query: bfloat16 [1024, 1024], P(None, 'tp'), may hold values from -1 to 1
- w_key: bfloat16 [1024, 1024], P(None, 'tp'), may hold values from -1 to 1
- w_value: bfloat16 [1024, 1024], P(None, 'tp'), may hold values from -0.1875 to 0.1875
- persist_key: bfloat16 [16, 1024], P(None, 'tp'), may hold values from -250 to 250
- persist_value: bfloat16 [16, 1024], P(None, 'tp'), may hold values from -6 to 6
- log_forget: float32 [65536, 8], P('req', 'tp'), may hold values from -0.75 to 0
- mem_gain: float32 [1024], P('tp'), may hold values from 0.5 to 1.5
- w_out: bfloat16 [1024, 1024], P('tp'), may hold values from -0.1875 to 0.1875
- ffn_gain: bfloat16 [1024], replicated, may hold values from 0.5 to 1.5
- w_gate: bfloat16 [1024, 2816], P(None, 'tp'), may hold values from -0.1875 to 0.1875
- w_up: bfloat16 [1024, 2816], P(None, 'tp'), may hold values from -0.1875 to 0.1875
- w_down: bfloat16 [2816, 1024], P('tp'), may hold values from -0.109375 to 0.109375
- doc_ids: int32 [65536], P('req'), may hold values from 0 to 512, never falling along the last dimension, each value on 1 to 32768 neighbouring positions
- page_owner: int32 [512], P('req'), may hold values from 0 to 31, as said below
- page_slot: int32 [512], P('req'), may hold values from 0 to 15
Outputs:
- layer_out: bfloat16 [65536, 1024], P('req')
- kv_cache: bfloat16 [512, 128, 2048], P('req', None, 'tp')
The draws below stay inside these ranges and needn't reach their ends.
Inputs may be any that keep to these rules, and one draw needn't show every extreme that they name: `page_owner`: the pages of one index of req going to one owner number at most 1, and every owner receives exactly 16 pages, one for each of its slots.
All inputs are finite; a program needn't handle non-finite values.
Results may differ from the reference program's by a relative error of at most 0.015.
Values may be sent and summed in bfloat16 or wider, within the bound.
No kernel may reach another device: no remote copies, remote signals or barrier semaphores. Data moves between devices by JAX's collectives and lax.ppermute only.
A program may use at most 128 MiB of HBM per device.

```python
import math
import jax
import jax.numpy as jnp
import numpy as np
from jax import lax

D = 1024
ATTN_HEADS = 8
HEAD_DIM = 128
FF = 2816
PERSIST = 16
SEG = 1024
PAGE = 128
PACKED_ITEMS = 65536
DOCS = 513
PAGES_DEV = 16
PAGES = 512
N_REQ = 32


def page_table(key):
    first_key, second_key = jax.random.split(jax.random.fold_in(key, 11))
    order = jax.random.permutation(first_key, N_REQ)
    place = jnp.arange(PAGES)
    source = place // PAGES_DEV
    local = place % PAGES_DEV
    owner = order[(source + local) % N_REQ]
    scores = jax.random.randint(second_key, (N_REQ, PAGES_DEV), 0, 1 << 20) * PAGES_DEV + jnp.arange(PAGES_DEV)[None, :]
    ranking = jnp.argsort(scores, axis=1)
    slot = ranking[owner, local]
    return (owner.astype(jnp.int32), slot.astype(jnp.int32))


def draw_page_owner(key, part):
    return page_table(key)[0]


def draw_page_slot(key, part):
    return page_table(key)[1]


def projection(key, label):
    matrix = jnp.clip(jax.random.normal(jax.random.fold_in(key, label), (D, ATTN_HEADS * HEAD_DIM), jnp.float32), -6.0, 6.0) * (1.0 / math.sqrt(D))
    return matrix.astype(jnp.bfloat16)


def draw_w_query(key, part):
    return projection(key, 41)


def draw_w_key(key, part):
    return projection(key, 43)


def draw_tokens(key, part):
    first_key = jax.random.fold_in(jax.random.fold_in(key, 13), 0)
    values = jnp.clip(jax.random.normal(first_key, (PACKED_ITEMS, D), jnp.float32), -6.0, 6.0)
    return values.astype(jnp.bfloat16)


def draw_log_forget(key, part):
    first_key, second_key, stochastic_seed_third, fourth_key = jax.random.split(jax.random.fold_in(key, 5), 4)
    share = 0.5
    quick = jax.random.uniform(first_key, (1, ATTN_HEADS), jnp.float32) < share
    speed_numbers = jnp.where(quick, -1.0 / 40.0, -0.5 / PACKED_ITEMS)
    stochastic_wobble = jnp.exp(jax.random.uniform(second_key, (PACKED_ITEMS, ATTN_HEADS), jnp.float32, -math.log(2.0), math.log(2.0)))
    spell_spans = jax.random.uniform(stochastic_seed_third, (PACKED_ITEMS, ATTN_HEADS), jnp.float32) < 3.0 / PACKED_ITEMS
    objective_numbers = jax.random.uniform(fourth_key, (PACKED_ITEMS, ATTN_HEADS), jnp.float32, math.log(0.5), math.log(0.8))
    return (speed_numbers * stochastic_wobble + jnp.where(spell_spans, objective_numbers, 0.0)).astype(jnp.float32)


def draw_persist_key(key, part):
    first_key = jax.random.fold_in(jax.random.fold_in(key, 7), 0)
    width = ATTN_HEADS * HEAD_DIM
    values = jnp.clip(jax.random.normal(first_key, (PERSIST, width), jnp.float32), -6.0, 6.0)
    return values.astype(jnp.bfloat16)


def shard_levels(stream_key, shape, cuts, least, largest):
    level, own = 1.0, jax.random.fold_in(stream_key, 6)
    for axis_at, blocks in cuts:
        draws = jnp.exp(jax.random.uniform(jax.random.fold_in(own, axis_at), (blocks,), jnp.float32, least / len(cuts), largest / len(cuts)))
        level = level * jnp.repeat(draws, shape[axis_at] // blocks).reshape([-1 if axis == axis_at else 1 for axis in range(len(shape))])
    return level


def split_up(amount, total, most, lean):
    portions = [(1 << 20) // math.isqrt(standing ** lean) + 1 for standing in range(2, amount + 1)]
    surplus, counts = total - most - (amount - 1), [1] * (amount - 1)
    while surplus > 0:
        free = [i for i in range(amount - 1) if counts[i] < most]
        whole, remaining = sum([portions[i] for i in free]), surplus
        for i in free:
            more = min(most - counts[i], max(1, remaining * portions[i] // whole), surplus)
            counts[i] = counts[i] + more
            surplus = surplus - more
    return np.array([most] + counts)


def ragged_sizes(rng, amount, total, bound, lean):
    if amount == 2:
        one = jax.random.randint(rng, (), max(1, total - bound), min(bound, total - 1) + 1)
        return jnp.stack([one, total - one])
    tallies = jnp.asarray(split_up(amount, total, bound, lean), jnp.int32)
    twos = (amount - 1) // 2
    giver, receiver = tallies[1:1 + 2 * twos:2], tallies[2:2 + 2 * twos:2]
    margin = jnp.minimum(giver - 1, bound - receiver)
    shifted = jax.random.randint(jax.random.fold_in(rng, 1), (twos,), 0, 1 << 20) % (margin + 1)
    tallies = tallies.at[1:1 + 2 * twos:2].set(giver - shifted).at[2:2 + 2 * twos:2].set(receiver + shifted)
    return tallies[jax.random.permutation(jax.random.fold_in(rng, 2), amount)]


def gaussian(stream_key, extent, deviation, most, pieces=(), kind=jnp.bfloat16):
    factor_of = shard_levels(stream_key, extent, pieces, -0.22, 0.18) if pieces else 1.0
    entries = jax.random.normal(stream_key, extent, jnp.float32) * deviation * factor_of
    return jnp.minimum(jnp.maximum(entries, -most), most).astype(kind)


def setup_inputs(seed: int = 0) -> dict:
    splits = jax.random.split(jax.random.key(seed), 18)
    return {
        "tokens": draw_tokens(jax.random.fold_in(splits[17], 71), 0),
        "attn_gain": jnp.clip(1.0 + 0.1 * jax.random.normal(splits[1], (D,), jnp.float32), 0.5, 1.5).astype(jnp.bfloat16),
        "w_query": draw_w_query(jax.random.fold_in(splits[17], 71), 0),
        "w_key": draw_w_key(jax.random.fold_in(splits[17], 71), 0),
        "w_value": gaussian(splits[4], (D, ATTN_HEADS * HEAD_DIM), D ** -0.5, 0.1875, ((1, 4),)),
        "persist_key": draw_persist_key(jax.random.fold_in(splits[17], 71), 0),
        "persist_value": gaussian(splits[6], (PERSIST, ATTN_HEADS * HEAD_DIM), 1.0, 6.0, ((1, 4),)),
        "log_forget": draw_log_forget(jax.random.fold_in(splits[17], 71), 0),
        "mem_gain": jnp.clip(1.0 + 0.1 * jax.random.normal(splits[8], (ATTN_HEADS * HEAD_DIM,), jnp.float32), 0.5, 1.5),
        "w_out": gaussian(splits[9], (ATTN_HEADS * HEAD_DIM, D), (ATTN_HEADS * HEAD_DIM) ** -0.5, 0.1875, ((0, 4),)),
        "ffn_gain": jnp.clip(1.0 + 0.1 * jax.random.normal(splits[10], (D,), jnp.float32), 0.5, 1.5).astype(jnp.bfloat16),
        "w_gate": gaussian(splits[11], (D, FF), D ** -0.5, 0.1875, ((1, 4),)),
        "w_up": gaussian(splits[12], (D, FF), D ** -0.5, 0.1875, ((1, 4),)),
        "w_down": gaussian(splits[13], (FF, D), FF ** -0.5, 0.109375, ((0, 4),)),
        "doc_ids": jnp.searchsorted(jnp.cumsum(ragged_sizes(splits[14], DOCS, PACKED_ITEMS, PACKED_ITEMS // 2, 0)), jnp.arange(PACKED_ITEMS), side="right").astype(jnp.int32),
        "page_owner": draw_page_owner(jax.random.fold_in(splits[17], 71), 0),
        "page_slot": draw_page_slot(jax.random.fold_in(splits[17], 71), 0),
    }


norm_eps = 1e-05
unit_eps = 1e-06
big_negative = -1e+30

def rms_scale(values, gain):
    wide = values.astype(jnp.float32)
    return wide * lax.rsqrt(lax.optimization_barrier(jnp.mean(wide * wide, axis=-1, keepdims=True)) + norm_eps) * gain.astype(jnp.float32)

def unit_rows(values):
    wide = values.astype(jnp.float32)
    return wide * lax.rsqrt(lax.optimization_barrier(jnp.mean(wide * wide, axis=-1, keepdims=True)) + unit_eps) / math.sqrt(wide.shape[-1])

def attend(queries, key_rows, value_rows, docs, persist_keys, persist_values):
    scale = 1.0 / math.sqrt(queries.shape[-1])
    query_wide = queries.astype(jnp.float32)
    local = jnp.einsum('thd,shd->hts', query_wide, key_rows.astype(jnp.float32)) * scale
    count = docs.shape[0]
    order = jnp.arange(count)
    allowed = (order[None, :] <= order[:, None]) & (docs[None, :] == docs[:, None])
    local = jnp.where(allowed[None], local, big_negative)
    persist = jnp.einsum('thd,phd->htp', query_wide, persist_keys.astype(jnp.float32)) * scale
    peak = jnp.maximum(lax.optimization_barrier(jnp.max(persist, axis=-1)), lax.optimization_barrier(jnp.max(local, axis=-1)))
    weight_persist = jnp.exp(persist - peak[..., None])
    weight_local = jnp.exp(local - peak[..., None])
    total = lax.optimization_barrier(jnp.sum(weight_persist, axis=-1)) + lax.optimization_barrier(jnp.sum(weight_local, axis=-1))
    probs_persist = (weight_persist / total[..., None]).astype(jnp.bfloat16)
    probs_local = (weight_local / total[..., None]).astype(jnp.bfloat16)
    return jnp.einsum('htp,phd->thd', probs_persist.astype(jnp.float32), persist_values.astype(jnp.float32)) + jnp.einsum('hts,shd->thd', probs_local.astype(jnp.float32), value_rows.astype(jnp.float32))

def memory_block(carry, inputs):
    state, carried = carry
    q_unit, k_unit, value_rows, decay_log, docs = inputs
    value_wide = value_rows.astype(jnp.float32)
    cumul = jnp.cumsum(decay_log, axis=0)
    diff = cumul[:, None, :] - cumul[None, :, :]
    order = jnp.arange(docs.shape[0])
    allowed = ((order[None, :] <= order[:, None]) & (docs[None, :] == docs[:, None]))[:, :, None]
    decay = jnp.where(allowed, jnp.exp(jnp.where(allowed, diff, 0.0)), 0.0)
    inner = jnp.einsum('thd,shd->tsh', q_unit, k_unit, precision=lax.Precision.HIGHEST) * decay
    recall = jnp.einsum('tsh,shd->thd', inner, value_wide, precision=lax.Precision.HIGHEST)
    continues = (docs == carried).astype(jnp.float32)
    reach = jnp.exp(cumul) * continues[:, None]
    recall = recall + jnp.einsum('thd,hde->the', q_unit, state, precision=lax.Precision.HIGHEST) * reach[:, :, None]
    last_doc = docs[-1]
    keep = jnp.exp(cumul[-1][None, :] - cumul) * (docs == last_doc).astype(jnp.float32)[:, None]
    kept = jnp.exp(cumul[-1]) * (last_doc == carried).astype(jnp.float32)
    state_next = jnp.einsum('shd,she->hde', k_unit * keep[:, :, None], value_wide, precision=lax.Precision.HIGHEST) + state * kept[:, None, None]
    return ((state_next, last_doc), recall)

def reference(tokens, attn_gain, w_query, w_key, w_value, persist_key, persist_value, log_forget, mem_gain, w_out, ffn_gain, w_gate, w_up, w_down, doc_ids, page_owner, page_slot):
    normed = rms_scale(tokens, attn_gain).astype(jnp.bfloat16)
    queries = jnp.dot(normed, w_query, preferred_element_type=jnp.float32).astype(jnp.bfloat16)
    key_rows = jnp.dot(normed, w_key, preferred_element_type=jnp.float32).astype(jnp.bfloat16)
    value_rows = jnp.dot(normed, w_value, preferred_element_type=jnp.float32).astype(jnp.bfloat16)
    shape3 = (PACKED_ITEMS, ATTN_HEADS, HEAD_DIM)
    pages = jnp.stack([key_rows.reshape(shape3), value_rows.reshape(shape3)], axis=2).reshape(PAGES, PAGE, ATTN_HEADS * 2 * HEAD_DIM)
    place = (page_owner * PAGES_DEV + page_slot).astype(jnp.int32)
    kv_cache = jnp.zeros_like(pages).at[place].set(pages)
    blocks = PACKED_ITEMS // SEG
    shape4 = (blocks, SEG, ATTN_HEADS, HEAD_DIM)
    q_unit = unit_rows(queries.reshape(shape3)).reshape(shape4)
    k_unit = unit_rows(key_rows.reshape(shape3)).reshape(shape4)
    query_blocks = queries.reshape(shape4)
    key_blocks = key_rows.reshape(shape4)
    value_blocks = value_rows.reshape(shape4)
    doc_blocks = doc_ids.reshape(blocks, SEG)
    decay_blocks = log_forget.reshape(blocks, SEG, ATTN_HEADS)
    start = (jnp.zeros((ATTN_HEADS, HEAD_DIM, HEAD_DIM), jnp.float32), jnp.int32(-1))
    _, recall = lax.scan(memory_block, start, (q_unit, k_unit, value_blocks, decay_blocks, doc_blocks))
    persist_keys = persist_key.reshape(PERSIST, ATTN_HEADS, HEAD_DIM)
    persist_values = persist_value.reshape(PERSIST, ATTN_HEADS, HEAD_DIM)

    def attend_block(parts):
        return attend(parts[0], parts[1], parts[2], parts[3], persist_keys, persist_values)
    attended = lax.map(attend_block, (query_blocks, key_blocks, value_blocks, doc_blocks))
    memory_out = rms_scale(recall, mem_gain.reshape(ATTN_HEADS, HEAD_DIM))
    heads_out = (attended + memory_out).astype(jnp.bfloat16).reshape(PACKED_ITEMS, ATTN_HEADS * HEAD_DIM)
    resid = (tokens.astype(jnp.float32) + jnp.dot(heads_out, w_out, preferred_element_type=jnp.float32)).astype(jnp.bfloat16)
    normed_ffn = rms_scale(resid, ffn_gain).astype(jnp.bfloat16)
    gate_proj = jnp.dot(normed_ffn, w_gate, preferred_element_type=jnp.float32)
    up_proj = jnp.dot(normed_ffn, w_up, preferred_element_type=jnp.float32)
    hidden = (jax.nn.silu(gate_proj) * up_proj).astype(jnp.bfloat16)
    layer_out = (resid.astype(jnp.float32) + jnp.dot(hidden, w_down, preferred_element_type=jnp.float32)).astype(jnp.bfloat16)
    return (layer_out, kv_cache)
```

```python
import math

import jax
import jax.numpy as jnp
from jax import lax
from jax.experimental import pallas as pl
from jax.experimental.pallas import tpu as pltpu
from jax.sharding import PartitionSpec as P

HD = 128
SEG = 1024
PAGE = 128
CH = 256
ROWS = 256
F32 = jnp.float32
BF = jnp.bfloat16
HI = lax.Precision.HIGHEST
ANY = pl.ANY


def rms(x, eps):
    return x * lax.rsqrt(jnp.mean(x * x, axis=-1, keepdims=True) + eps)


def dot(a, b):
    return jnp.dot(a, b, preferred_element_type=F32)


def dot_t(a, b):
    return lax.dot_general(a, b, (((1,), (1,)), ((), ())), preferred_element_type=F32)


def dot_l(a, b):
    return lax.dot_general(a, b, (((0,), (0,)), ((), ())), preferred_element_type=F32)


def tri(n, lower=True):
    r = lax.broadcasted_iota(jnp.int32, (n, n), 0)
    c = lax.broadcasted_iota(jnp.int32, (n, n), 1)
    return (r >= c) if lower else (r <= c)


def split3(x):
    hi = x.astype(BF).astype(F32)
    mid = (x - hi).astype(BF).astype(F32)
    return hi, mid, x - hi - mid


def project_kernel(tok, gain, wq, wk, wv, col, q_out, kv_out, ku_out, min_out, pay_out, st, misc):
    i = pl.program_id(0)

    @pl.when(i == 0)
    def _():
        st[...] = jnp.zeros_like(st)
        misc[...] = jnp.full_like(misc, -1.0)
        misc[0:2, :] = jnp.zeros((2, 128), F32)

    n = (rms(tok[...].astype(F32), 1e-5) * gain[...].astype(F32)).astype(BF)
    q_out[...] = dot(n, wq[...]).astype(BF)
    k = dot(n, wk[...]).astype(BF)
    v = dot(n, wv[...]).astype(BF)
    mask = tri(CH).astype(F32)
    for h in range(2):
        s = slice(h * HD, (h + 1) * HD)
        kv_out[:, 2 * h * HD : (2 * h + 1) * HD] = k[:, s]
        kv_out[:, (2 * h + 1) * HD : (2 * h + 2) * HD] = v[:, s]
    for j in range(tok.shape[0] // CH):
        r = slice(j * CH, (j + 1) * CH)
        info = col[r, :]
        cum = jnp.dot(mask, info, precision=HI, preferred_element_type=F32)
        end = cum[CH - 1 : CH, :]
        doc = info[:, 0:1]
        last = info[CH - 1 : CH, 0:1]
        same = (doc == last).astype(F32)
        last_row = jnp.broadcast_to(last, (1, 128))
        cont = (last_row == misc[2:3, :]).astype(F32)
        for h in range(2):
            s = slice(h * HD, (h + 1) * HD)
            ku = rms(k[r, s].astype(F32), 1e-6) * (1.0 / math.sqrt(HD))
            ku_out[r, s] = ku.astype(BF)
            end_h = end[:, 1 + h : 2 + h]
            w = jnp.exp(end_h - cum[:, 1 + h : 2 + h]) * same
            add = dot_l((ku * w).astype(BF), v[r, s])
            end_row = jnp.broadcast_to(end_h, (1, 128))
            old = st[h]
            min_out[j, h] = old
            st[h] = old * (jnp.exp(end_row) * cont) + add
            misc[h : h + 1, :] = misc[h : h + 1, :] + end_row
        misc[2:3, :] = last_row

    @pl.when(i == pl.num_programs(0) - 1)
    def _():
        write_payload(pay_out, st, misc[0:1, :], misc[1:2, :], misc[2:3, :])


def write_payload(out, st, l0, l1, last):
    for h in range(2):
        out[h * HD : (h + 1) * HD, :] = st[h].astype(BF)
    hi = jnp.floor(last * (1.0 / 256.0))
    rows = [*split3(l0), *split3(l1), hi, last - hi * 256.0]
    out[2 * HD : 2 * HD + 8, :] = jnp.concatenate(rows, axis=0).astype(BF)


def read_payload(ref, j):
    s = ref[j, 2 * HD : 2 * HD + 8, :].astype(F32)
    l0 = s[0:1] + s[1:2] + s[2:3]
    l1 = s[3:4] + s[4:5] + s[5:6]
    return l0, l1, s[6:7] * 256.0 + s[7:8]


def project(tokens, gain, wq, wk, wv, col):
    t, d = tokens.shape
    tile = 512
    n = t // tile
    c = tile // CH
    full = lambda a: pl.BlockSpec(a.shape, lambda i: (0, 0))
    row = lambda w: pl.BlockSpec((tile, w), lambda i: (i, 0))
    return pl.pallas_call(
        project_kernel,
        grid=(n,),
        in_specs=[row(d), full(gain), full(wq), full(wk), full(wv), row(8)],
        out_specs=[
            row(256),
            row(512),
            row(256),
            pl.BlockSpec((c, 2, HD, HD), lambda i: (i, 0, 0, 0)),
            pl.BlockSpec((264, 128), lambda i: (0, 0)),
        ],
        out_shape=[
            jax.ShapeDtypeStruct((t, 256), BF),
            jax.ShapeDtypeStruct((t, 512), BF),
            jax.ShapeDtypeStruct((t, 256), BF),
            jax.ShapeDtypeStruct((t // CH, 2, HD, HD), F32),
            jax.ShapeDtypeStruct((264, 128), BF),
        ],
        scratch_shapes=[pltpu.VMEM((2, HD, HD), F32), pltpu.VMEM((8, 128), F32)],
        name="project",
    )(tokens, gain, wq, wk, wv, col)


def combine_kernel(place, got, e_out, info_out, pay_out, st):
    g = place[0]
    st[...] = jnp.zeros_like(st)
    e_out[...] = jnp.zeros_like(e_out)
    cur = jnp.full((1, 128), -1.0, F32)
    t0 = t1 = jnp.zeros((1, 128), F32)
    i0, i1, il = t0, t1, cur
    for j in range(8):
        @pl.when(g == j)
        def _():
            e_out[...] = st[...]

        here = g == j
        i0, i1, il = jnp.where(here, t0, i0), jnp.where(here, t1, i1), jnp.where(here, cur, il)
        l0, l1, last = read_payload(got, j)
        cont = (cur == last).astype(F32)
        for h, l in ((0, l0), (1, l1)):
            st[h] = st[h] * (jnp.exp(l) * cont) + got[j, h * HD : (h + 1) * HD, :].astype(F32)
        t0, t1, cur = t0 + l0, t1 + l1, last
    info_out[...] = jnp.concatenate([i0, i1, il, jnp.zeros((5, 128), F32)], axis=0)
    write_payload(pay_out, st, t0, t1, cur)


def combine(place, got):
    vm = pl.BlockSpec(memory_space=pltpu.VMEM)
    return pl.pallas_call(
        combine_kernel,
        in_specs=[pl.BlockSpec(memory_space=pltpu.SMEM), vm],
        out_specs=[vm, vm, vm],
        out_shape=[
            jax.ShapeDtypeStruct((2, HD, HD), F32),
            jax.ShapeDtypeStruct((8, 128), F32),
            jax.ShapeDtypeStruct((264, 128), BF),
        ],
        scratch_shapes=[pltpu.VMEM((2, HD, HD), F32)],
        name="combine",
    )(place, got)


def attend_kernel(q, k, v, pk, pv, col, row, out):
    scale = 1.0 / math.sqrt(HD)
    c = scale * math.log2(math.e)
    mask = tri(CH)
    for i in range(SEG // CH):
        r = slice(i * CH, (i + 1) * CH)
        qi = q[r, :]
        doc = col[r, 0:1]
        sp = dot_t(qi, pk[...])
        sd = dot_t(qi, k[r, :])
        sd = jnp.where(mask & (doc == row[0:1, r]), sd, -1e30)
        m = jnp.maximum(jnp.max(sp, axis=-1, keepdims=True), jnp.max(sd, axis=-1, keepdims=True))
        if i:
            e = slice(0, i * CH)
            so = dot_t(qi, k[e, :])
            so = jnp.where(doc == row[0:1, e], so, -1e30)
            m = jnp.maximum(m, jnp.max(so, axis=-1, keepdims=True))
        wp = jnp.exp2((sp - m) * c)
        wd = jnp.exp2((sd - m) * c)
        total = jnp.sum(wp, axis=-1, keepdims=True) + jnp.sum(wd, axis=-1, keepdims=True)
        acc = dot(wp.astype(BF), pv[...]) + dot(wd.astype(BF), v[r, :])
        if i:
            wo = jnp.exp2((so - m) * c)
            total = total + jnp.sum(wo, axis=-1, keepdims=True)
            acc = acc + dot(wo.astype(BF), v[e, :])
        out[r, :] = acc / total


def attend(q, kv, pk, pv, col, row, seg):
    return pl.pallas_call(
        attend_kernel,
        grid=(2,),
        in_specs=[
            pl.BlockSpec((SEG, HD), lambda h: (seg, h)),
            pl.BlockSpec((SEG, HD), lambda h: (seg, 2 * h)),
            pl.BlockSpec((SEG, HD), lambda h: (seg, 2 * h + 1)),
            pl.BlockSpec((16, HD), lambda h: (0, h)),
            pl.BlockSpec((16, HD), lambda h: (0, h)),
            pl.BlockSpec((SEG, 8), lambda h: (seg, 0)),
            pl.BlockSpec((8, SEG), lambda h: (0, seg)),
        ],
        out_specs=pl.BlockSpec((SEG, HD), lambda h: (0, h)),
        out_shape=jax.ShapeDtypeStruct((SEG, 2 * HD), F32),
        name="attend",
    )(q, kv, kv, pk, pv, col, row)


def recall_kernel(half, place, bound, q, ku, kv, mi, e1, info, got, col, row, rows, at0, at1, gain, out, pst, pdoc):
    b = pl.program_id(0)
    chunk = 2 * b + half

    @pl.when(b == 0)
    def _():
        x, g = place[1], place[0]
        st = [jnp.zeros((HD, HD), F32)] * 2
        cur = jnp.full((1, 128), -1.0, F32)
        pst[...] = jnp.zeros_like(pst)
        il = cur
        for j in range(4):
            here = x == j
            il = jnp.where(here, cur, il)
            for h in range(2):
                pst[h] = jnp.where(here, st[h], pst[h])
            l0, l1, last = read_payload(got, j)
            cont = (cur == last).astype(F32)
            for h, l in ((0, l0), (1, l1)):
                st[h] = st[h] * (jnp.exp(l) * cont) + got[j, h * HD : (h + 1) * HD, :].astype(F32)
            cur = last
        glast = info[2:3, :]
        first = g == 0
        ok = jnp.where(first, 1.0, (il == glast).astype(F32))
        for h in range(2):
            pst[h] = pst[h] * (jnp.exp(info[h : h + 1, :]) * ok) + e1[h]
        pdoc[0:1, :] = jnp.where(first, il, glast)

    mask = tri(CH)
    c_col = jnp.dot(mask.astype(F32), col[...], precision=HI, preferred_element_type=F32)
    c_row = jnp.dot(row[...], tri(CH, False).astype(F32), precision=HI, preferred_element_type=F32)
    pos = lax.broadcasted_iota(jnp.int32, rows.shape, 1)
    pre = jnp.sum(jnp.where(pos < chunk * CH, rows[...], 0.0), axis=1, keepdims=True)
    doc = col[:, 0:1]
    pdoc_row = pdoc[0:1, :]
    carried = jnp.where(chunk == 0, pdoc_row, bound[chunk])
    joined = (carried == pdoc_row).astype(F32)
    live = (doc == carried[:, 0:1]).astype(F32)
    ok = mask & (doc == row[0:1, :])
    for h in range(2):
        s = slice(h * HD, (h + 1) * HD)
        qh = q[:, s]
        cc = c_col[:, 1 + h : 2 + h]
        dec = jnp.exp(jnp.where(ok, cc - c_row[1 + h : 2 + h, :], -1e30))
        inner = (dot_t(qh, ku[:, s]) * dec).astype(BF)
        rec = dot(inner, kv[:, (2 * h + 1) * HD : (2 * h + 2) * HD])
        f = jnp.exp(jnp.broadcast_to(pre[1 + h : 2 + h, :], (1, 128))) * joined
        m = mi[0, h] + pst[h] * f
        rec = rec + dot(qh, m.astype(BF)) * (jnp.exp(cc) * live)
        qw = qh.astype(F32)
        rec = rec * (lax.rsqrt(jnp.mean(qw * qw, axis=-1, keepdims=True) + 1e-6) * (1.0 / math.sqrt(HD)))
        at = jnp.where(chunk < SEG // CH, at0[:, s], at1[:, s])
        out[0, :, s] = (at + rms(rec, 1e-5) * gain[:, s]).astype(BF)


def recall(half, place, bound, q, ku, kv, mi, e1, info, got, col, row, at0, at1, gain):
    import functools

    ch = lambda w: pl.BlockSpec((CH, w), lambda b, p, d: (2 * b + half, 0))
    full = lambda a: pl.BlockSpec(a.shape, lambda b, p, d: (0,) * a.ndim)
    per = SEG // CH
    gs = pltpu.PrefetchScalarGridSpec(
        num_scalar_prefetch=2,
        grid=(4,),
        in_specs=[
            ch(256),
            ch(256),
            ch(512),
            pl.BlockSpec((1, 2, HD, HD), lambda b, p, d: (2 * b + half, 0, 0, 0)),
            full(e1),
            full(info),
            full(got),
            ch(8),
            pl.BlockSpec((8, CH), lambda b, p, d: (0, 2 * b + half)),
            full(row),
            pl.BlockSpec((CH, 256), lambda b, p, d: (jnp.minimum(2 * b + half, per - 1), 0)),
            pl.BlockSpec((CH, 256), lambda b, p, d: (jnp.maximum(2 * b + half - per, 0), 0)),
            full(gain),
        ],
        out_specs=pl.BlockSpec((1, CH, 256), lambda b, p, d: (lax.rem(b - p[2] + 4, 4), 0, 0)),
        scratch_shapes=[pltpu.VMEM((2, HD, HD), F32), pltpu.VMEM((8, 128), F32)],
    )
    return pl.pallas_call(
        functools.partial(recall_kernel, half),
        grid_spec=gs,
        out_shape=jax.ShapeDtypeStruct((4, CH, 256), BF),
        name="recall",
    )(place, bound, q, ku, kv, mi, e1, info, got, col, row, row, at0, at1, gain)


def ffn_kernel(place, tok, gain, h0, h1, h2, h3, *rest):
    own = rest[0:4]
    gu = (rest[4:7], rest[7:10])
    do = (rest[10:13], rest[13:16])
    out, wg, wu, wd, wo, sem = rest[16:]
    core = place[3]
    copies = []

    def copy(src, dst):
        c = pltpu.make_async_copy(src, dst, sem.at[len(copies)])
        c.start()
        copies.append(c)
        return c

    outs, ups, downs = [], [], []
    hh, hd, ho = 512, 352, 128
    outs.append([copy(own[3], wo.at[0])])
    for d in range(3):
        outs.append([copy(do[p][d].at[pl.ds(hd, ho), :], wo.at[d + 1, pl.ds((core if p == 0 else 1 - core) * ho, ho), :]) for p in range(2)])
    for d in range(4):
        if d == 0:
            ups.append([copy(own[0], wg.at[0]), copy(own[1], wu.at[0])])
            downs.append([copy(own[2], wd.at[0])])
            continue
        u, w = [], []
        for p in range(2):
            at = core if p == 0 else 1 - core
            u.append(copy(gu[p][d - 1].at[0], wg.at[d, pl.ds(at * hh, hh), :]))
            u.append(copy(gu[p][d - 1].at[1], wu.at[d, pl.ds(at * hh, hh), :]))
            w.append(copy(do[p][d - 1].at[pl.ds(0, hd), :], wd.at[d, pl.ds(at * hd, hd), :]))
        ups.append(u)
        downs.append(w)
    acc = tok[...].astype(F32)
    for d, h in enumerate((h0, h1, h2, h3)):
        for c in outs[d]:
            c.wait()
        acc = acc + dot(h[...], wo[d])
    resid = acc.astype(BF).astype(F32)
    n = (rms(resid, 1e-5) * gain[...].astype(F32)).astype(BF)
    acc = resid
    for d in range(4):
        for c in ups[d]:
            c.wait()
        g = dot(n, wg[d])
        u = dot(n, wu[d])
        hid = (g / (1.0 + jnp.exp(-g)) * u).astype(BF)
        for c in downs[d]:
            c.wait()
        acc = acc + dot(hid, wd[d])
    out[...] = acc.astype(BF)


def ffn(half, place, tokens, gain, heads, own, gu, gux, do, dox):
    d = tokens.shape[1]
    full = lambda a: pl.BlockSpec(a.shape, lambda i, p: (0,) * a.ndim)
    anys = pl.BlockSpec(memory_space=ANY)
    ws = [*own, *gu, *gux, *do, *dox]
    gs = pltpu.PrefetchScalarGridSpec(
        num_scalar_prefetch=1,
        grid=(1,),
        in_specs=[pl.BlockSpec((ROWS, d), lambda i, p: (2 * p[2] + half, 0)), full(gain)]
        + [full(h) for h in heads]
        + [anys] * len(ws),
        out_specs=pl.BlockSpec((ROWS, d), lambda i, p: (0, 0)),
        scratch_shapes=[
            pltpu.VMEM((4, 1024, 704), BF),
            pltpu.VMEM((4, 1024, 704), BF),
            pltpu.VMEM((4, 704, 1024), BF),
            pltpu.VMEM((4, 256, 1024), BF),
            pltpu.SemaphoreType.DMA((28,)),
        ],
    )
    return pl.pallas_call(
        ffn_kernel,
        grid_spec=gs,
        out_shape=jax.ShapeDtypeStruct((ROWS, d), BF),
        name="ffn",
    )(place, tokens, gain, *heads, *ws)


def dispatch_kernel(owner, pages, codes, out, sem):
    copies = []
    n = pages.shape[0]
    for p in range(n):
        copies.append(pltpu.make_async_copy(pages.at[p], out.at[owner[p], pl.ds(0, PAGE), :], sem.at[p]))
    for o in range(out.shape[0]):
        copies.append(pltpu.make_async_copy(codes.at[o], out.at[o, pl.ds(PAGE, 8), :], sem.at[n + o]))
    for c in copies:
        c.start()
    for c in copies:
        c.wait()


def dispatch(owner, pages, codes, count):
    anys = pl.BlockSpec(memory_space=ANY)
    return pl.pallas_call(
        dispatch_kernel,
        in_specs=[pl.BlockSpec(memory_space=pltpu.SMEM), anys, anys],
        out_specs=anys,
        out_shape=jax.ShapeDtypeStruct((count, PAGE + 8, pages.shape[2]), BF),
        scratch_shapes=[pltpu.SemaphoreType.DMA((pages.shape[0] + count,))],
        name="dispatch",
    )(owner, pages, codes)


def place_kernel(source, got, out, sem):
    copies = [
        pltpu.make_async_copy(got.at[source[s], pl.ds(0, PAGE), :], out.at[s], sem.at[s])
        for s in range(out.shape[0])
    ]
    for c in copies:
        c.start()
    for c in copies:
        c.wait()


def place_pages(source, got, count):
    anys = pl.BlockSpec(memory_space=ANY)
    return pl.pallas_call(
        place_kernel,
        in_specs=[pl.BlockSpec(memory_space=pltpu.SMEM), anys],
        out_specs=anys,
        out_shape=jax.ShapeDtypeStruct((count, PAGE, got.shape[2]), BF),
        scratch_shapes=[pltpu.SemaphoreType.DMA((count,))],
        name="place",
    )(source, got)


def join_kernel(place, *refs):
    pieces, out, sem = refs[:10], refs[10], refs[11]
    y = place[2]
    copies = []
    for half in range(2):
        own, a, b, lo, hi = pieces[5 * half : 5 * half + 5]
        for src, d, off, n in ((own, 0, 0, ROWS), (a, 3, 0, ROWS), (b, 1, 0, ROWS), (lo, 2, 0, ROWS // 2), (hi, 2, ROWS // 2, ROWS // 2)):
            at = lax.rem(y + d, 4) * (2 * ROWS) + half * ROWS + off
            copies.append(pltpu.make_async_copy(src, out.at[pl.ds(at, n), :], sem.at[len(copies)]))
    for c in copies:
        c.start()
    for c in copies:
        c.wait()


def join(place, pieces):
    anys = pl.BlockSpec(memory_space=ANY)
    return pl.pallas_call(
        join_kernel,
        in_specs=[pl.BlockSpec(memory_space=pltpu.SMEM)] + [anys] * 10,
        out_specs=anys,
        out_shape=jax.ShapeDtypeStruct((8 * ROWS, pieces[0].shape[1]), BF),
        scratch_shapes=[pltpu.SemaphoreType.DMA((10,))],
        name="join",
    )(place, *pieces)


def on_device(
    tokens, attn_gain, w_query, w_key, w_value, persist_key, persist_value, log_forget, mem_gain,
    w_out, ffn_gain, w_gate, w_up, w_down, doc_ids, page_owner, page_slot,
):
    count = tokens.shape[0]
    reqs = lax.axis_size("req")
    req, y = lax.axis_index("req"), lax.axis_index("tp")
    core = req % 2
    place = jnp.stack([req % 8, req // 8, y, core]).astype(jnp.int32)
    shift = lambda a, d: lax.ppermute(a, "tp", [(i, (i + d) % 4) for i in range(4)])
    swap = lambda a: lax.ppermute(a, "req", [(i, i ^ 1) for i in range(reqs)])

    cut = lambda w: lax.dynamic_slice_in_dim(w, core * (w.shape[0] // 2), w.shape[0] // 2, 0)
    gu_half = jnp.stack([cut(w_gate), cut(w_up)])
    do_half = jnp.concatenate([cut(w_down), cut(w_out)])
    do = [shift(do_half, d) for d in (1, 2, 3)]
    gu = [shift(gu_half, d) for d in (1, 2, 3)]

    doc = doc_ids.astype(F32)
    row = jnp.concatenate([doc[None], log_forget.T, jnp.zeros((5, count), F32)])
    col = jnp.concatenate([doc[:, None], log_forget, jnp.zeros((count, 5), F32)], axis=1)
    bound = jnp.concatenate([jnp.full((1,), -1.0, F32), doc[CH - 1 : -1 : CH]])

    q, kv, ku, mi, pay = project(tokens, attn_gain[None], w_query, w_key, w_value, col)

    group8 = [[x * 8 + k for k in range(8)] for x in range(reqs // 8)]
    group4 = [[x * 8 + k for x in range(reqs // 8)] for k in range(8)]
    spread = lambda a, n, g: lax.all_to_all(
        jnp.broadcast_to(a[None], (n, *a.shape)), "req", 0, 0, tiled=True, axis_index_groups=g
    )
    got8 = spread(pay, 8, group8)

    at0 = attend(q, kv, persist_key, persist_value, col, row, 0)
    e1, info, pay4 = combine(place, got8)
    got4 = spread(pay4, 4, group4)
    at1 = attend(q, kv, persist_key, persist_value, col, row, 1)

    pages = kv.reshape(count // PAGE, PAGE, 512)
    hit = page_owner[None, :] == jnp.arange(reqs)[:, None]
    code = jnp.sum(jnp.where(hit, page_slot[None, :] + 1, 0), axis=1).astype(BF)
    codes = jnp.broadcast_to(code[:, None, None], (reqs, 8, 512))
    outgoing = dispatch(page_owner, pages, codes, reqs)
    arrived = lax.all_to_all(outgoing, "req", 0, 0, tiled=True)

    gux = [swap(a) for a in gu]
    dox = [swap(a) for a in do]
    gain = mem_gain[None]
    pieces = []
    for half in range(2):
        out = recall(half, place, bound, q, ku, kv, mi, e1, info, got4, col, row, at0, at1, gain)
        heads = [out[0]] + [shift(out[d], d) for d in (1, 2, 3)]
        own = ffn(half, place, tokens, ffn_gain[None], heads, (w_gate, w_up, w_down, w_out), gu, gux, do, dox)
        a, b = shift(own, 1), shift(own, -1)
        lo = shift(a[: ROWS // 2], 1)
        hi = shift(b[ROWS // 2 :], -1)
        pieces += [own, a, b, lo, hi]
    layer_out = join(place, pieces)

    slots = arrived[:, PAGE, 0].astype(F32)
    wanted = slots[None, :] == (jnp.arange(count // PAGE) + 1).astype(F32)[:, None]
    source = jnp.sum(jnp.where(wanted, jnp.arange(reqs)[None, :], 0), axis=1).astype(jnp.int32)
    kv_cache = place_pages(source, arrived, count // PAGE)
    return layer_out, kv_cache


def solution(mesh):
    return jax.shard_map(
        on_device,
        mesh=mesh,
        in_specs=(
            P("req", None), P(), P(None, "tp"), P(None, "tp"), P(None, "tp"), P(None, "tp"), P(None, "tp"),
            P("req", "tp"), P("tp"), P("tp", None), P(), P(None, "tp"), P(None, "tp"), P("tp", None),
            P("req"), P("req"), P("req"),
        ),
        out_specs=(P("req", None), P("req", None, "tp")),
        check_vma=False,
    )
```

```python
import functools
import math

import jax
import jax.numpy as jnp
from jax import lax
from jax.experimental import pallas as pl
from jax.experimental.pallas import tpu as pltpu
from jax.sharding import PartitionSpec as P

HD = 128
SEG = 1024
PAGE = 128
CH = 256
ROWS = 256
F32 = jnp.float32
BF = jnp.bfloat16
ANY = pl.ANY


def rms(x, eps):
    return x * lax.rsqrt(jnp.mean(x * x, axis=-1, keepdims=True) + eps)


def dot(a, b):
    return jnp.dot(a, b, preferred_element_type=F32)


def dot_t(a, b):
    return lax.dot_general(a, b, (((1,), (1,)), ((), ())), preferred_element_type=F32)


def dot_l(a, b):
    return lax.dot_general(a, b, (((0,), (0,)), ((), ())), preferred_element_type=F32)


def tri(n, lower=True):
    r = lax.broadcasted_iota(jnp.int32, (n, n), 0)
    c = lax.broadcasted_iota(jnp.int32, (n, n), 1)
    return (r >= c) if lower else (r <= c)


def split3(x):
    hi = x.astype(BF).astype(F32)
    mid = (x - hi).astype(BF).astype(F32)
    return hi, mid, x - hi - mid


def running(info):
    parts = jnp.concatenate(split3(info), axis=0).astype(BF)
    c = dot(parts, tri(info.shape[1], False).astype(F32).astype(BF))
    c = c[0:8] + c[8:16] + c[16:24]
    return jnp.where(lax.broadcasted_iota(jnp.int32, info.shape, 0) == 0, info, c)


def normed(tok, gain, out):
    g = gain[...].astype(F32)
    for b in range(CH // 32):
        r = slice(b * 32, (b + 1) * 32)
        out[r, :] = (rms(tok[r, :].astype(F32), 1e-5) * g).astype(BF)


def project_kernel(owner, tok0, tok1, tok2, gain, wq, wk, wv, row, codes, q_out, kv_out, ku_out, min_out, pay_out, cr_out, cc_out, sent, st, misc, buf, n0, n1, sem):
    i = pl.program_id(0)
    here = CH // PAGE
    last_sem = 2 * here

    @pl.when(i == 0)
    def _():
        st[...] = jnp.zeros_like(st)
        misc[...] = jnp.full_like(misc, -1.0)
        misc[0:2, :] = jnp.zeros((2, 128), F32)
        pltpu.make_async_copy(codes, sent.at[:, pl.ds(PAGE, 8), :], sem.at[last_sem]).start()
        normed(tok0, gain, n0)

    copies = []
    for j, (now, tok, later) in enumerate(((n0, tok1, n1), (n1, tok2, n0))):
        r = slice(j * CH, (j + 1) * CH)
        n = now[...]
        k = dot(n, wk[...]).astype(BF)
        v = dot(n, wv[...]).astype(BF)
        q_out[r, :] = dot(n, wq[...]).astype(BF)
        for h in range(2):
            s = slice(h * HD, (h + 1) * HD)
            kv_out[r, 2 * h * HD : (2 * h + 1) * HD] = k[:, s]
            kv_out[r, (2 * h + 1) * HD : (2 * h + 2) * HD] = v[:, s]
            for p in range(here):
                w = slice(p * PAGE, (p + 1) * PAGE)
                buf[j * here + p, :, 2 * h * HD : (2 * h + 1) * HD] = k[w, s]
                buf[j * here + p, :, (2 * h + 1) * HD : (2 * h + 2) * HD] = v[w, s]
        for p in range(here):
            m = j * here + p
            c = pltpu.make_async_copy(buf.at[m], sent.at[owner[i * 2 * here + m], pl.ds(0, PAGE), :], sem.at[m])
            c.start()
            copies.append(c)
        normed(tok, gain, later)
        cr = running(row[:, r])
        cc = cr.T
        cr_out[:, r] = cr
        cc_out[r, :] = cc
        last = cr[0:1, CH - 1 : CH]
        same = (cc[:, 0:1] == last).astype(F32)
        last_row = jnp.broadcast_to(last, (1, 128))
        cont = (last_row == misc[2:3, :]).astype(F32)
        for h in range(2):
            s = slice(h * HD, (h + 1) * HD)
            ku = rms(k[:, s].astype(F32), 1e-6) * (1.0 / math.sqrt(HD))
            ku_out[r, s] = ku.astype(BF)
            end_h = cr[1 + h : 2 + h, CH - 1 : CH]
            w = jnp.exp(end_h - cc[:, 1 + h : 2 + h]) * same
            add = dot_l((ku * w).astype(BF), v[:, s])
            end_row = jnp.broadcast_to(end_h, (1, 128))
            old = st[h]
            min_out[j, h] = old
            st[h] = old * (jnp.exp(end_row) * cont) + add
            misc[h : h + 1, :] = misc[h : h + 1, :] + end_row
        misc[2:3, :] = last_row

    @pl.when(i == pl.num_programs(0) - 1)
    def _():
        write_payload(pay_out, st, misc[0:1, :], misc[1:2, :], misc[2:3, :])
        pltpu.make_async_copy(codes, sent.at[:, pl.ds(PAGE, 8), :], sem.at[last_sem]).wait()

    for c in copies:
        c.wait()


def write_payload(out, st, l0, l1, last):
    hi = jnp.floor(last * (1.0 / 256.0))
    rows = [*split3(l0), *split3(l1), hi, last - hi * 256.0]
    tail = jnp.concatenate(rows, axis=0).astype(BF)
    for i in range(out.shape[0]):
        for h in range(2):
            out[i, h * HD : (h + 1) * HD, :] = st[h].astype(BF)
        out[i, 2 * HD : 2 * HD + 8, :] = tail


def read_payload(ref, j):
    s = ref[j, 2 * HD : 2 * HD + 8, :].astype(F32)
    l0 = s[0:1] + s[1:2] + s[2:3]
    l1 = s[3:4] + s[4:5] + s[5:6]
    return l0, l1, s[6:7] * 256.0 + s[7:8]


def project(owner, tokens, gain, wq, wk, wv, row, codes):
    t, d = tokens.shape
    tile = 512
    n = t // tile
    c = tile // CH
    full = lambda a: pl.BlockSpec(a.shape, lambda i, o: (0,) * a.ndim)
    rows = lambda w: pl.BlockSpec((tile, w), lambda i, o: (i, 0))
    lanes = pl.BlockSpec((8, tile), lambda i, o: (0, i))
    gs = pltpu.PrefetchScalarGridSpec(
        num_scalar_prefetch=1,
        grid=(n,),
        in_specs=[
            pl.BlockSpec((CH, d), lambda i, o: (0, 0)),
            pl.BlockSpec((CH, d), lambda i, o: (2 * i + 1, 0)),
            pl.BlockSpec((CH, d), lambda i, o: (jnp.minimum(2 * i + 2, 2 * n - 1), 0)),
            full(gain), full(wq), full(wk), full(wv), lanes, full(codes),
        ],
        out_specs=[
            rows(256),
            rows(512),
            rows(256),
            pl.BlockSpec((c, 2, HD, HD), lambda i, o: (i, 0, 0, 0)),
            pl.BlockSpec((8, 264, 128), lambda i, o: (0, 0, 0)),
            lanes,
            rows(8),
            pl.BlockSpec(memory_space=ANY),
        ],
        scratch_shapes=[
            pltpu.VMEM((2, HD, HD), F32),
            pltpu.VMEM((8, 128), F32),
            pltpu.VMEM((tile // PAGE, PAGE, 512), BF),
            pltpu.VMEM((CH, d), BF),
            pltpu.VMEM((CH, d), BF),
            pltpu.SemaphoreType.DMA((tile // PAGE + 1,)),
        ],
    )
    return pl.pallas_call(
        project_kernel,
        grid_spec=gs,
        out_shape=[
            jax.ShapeDtypeStruct((t, 256), BF),
            jax.ShapeDtypeStruct((t, 512), BF),
            jax.ShapeDtypeStruct((t, 256), BF),
            jax.ShapeDtypeStruct((t // CH, 2, HD, HD), F32),
            jax.ShapeDtypeStruct((8, 264, 128), BF),
            jax.ShapeDtypeStruct((8, t), F32),
            jax.ShapeDtypeStruct((t, 8), F32),
            jax.ShapeDtypeStruct((codes.shape[0], PAGE + 8, 512), BF),
        ],
        name="project",
    )(owner, tokens, tokens, tokens, gain, wq, wk, wv, row, codes)


def combine_kernel(place, got, e_out, info_out, pay_out, st):
    g = place[0]
    st[...] = jnp.zeros_like(st)
    e_out[...] = jnp.zeros_like(e_out)
    cur = jnp.full((1, 128), -1.0, F32)
    t0 = t1 = jnp.zeros((1, 128), F32)
    i0, i1, il = t0, t1, cur
    for j in range(8):
        @pl.when(g == j)
        def _():
            e_out[...] = st[...]

        here = g == j
        i0, i1, il = jnp.where(here, t0, i0), jnp.where(here, t1, i1), jnp.where(here, cur, il)
        l0, l1, last = read_payload(got, j)
        cont = (cur == last).astype(F32)
        for h, l in ((0, l0), (1, l1)):
            st[h] = st[h] * (jnp.exp(l) * cont) + got[j, h * HD : (h + 1) * HD, :].astype(F32)
        t0, t1, cur = t0 + l0, t1 + l1, last
    info_out[...] = jnp.concatenate([i0, i1, il, jnp.zeros((5, 128), F32)], axis=0)
    write_payload(pay_out, st, t0, t1, cur)


def combine(place, got):
    vm = pl.BlockSpec(memory_space=pltpu.VMEM)
    return pl.pallas_call(
        combine_kernel,
        in_specs=[pl.BlockSpec(memory_space=pltpu.SMEM), vm],
        out_specs=[vm, vm, vm],
        out_shape=[
            jax.ShapeDtypeStruct((2, HD, HD), F32),
            jax.ShapeDtypeStruct((8, 128), F32),
            jax.ShapeDtypeStruct((4, 264, 128), BF),
        ],
        scratch_shapes=[pltpu.VMEM((2, HD, HD), F32)],
        name="combine",
    )(place, got)


def attend_kernel(q, k, v, pk, pv, col, row, out):
    scale = 1.0 / math.sqrt(HD)
    c = scale * math.log2(math.e)
    mask = tri(CH)
    for i in range(SEG // CH):
        r = slice(i * CH, (i + 1) * CH)
        qi = q[r, :]
        doc = col[r, 0:1]
        sp = dot_t(qi, pk[...])
        sd = dot_t(qi, k[r, :])
        sd = jnp.where(mask & (doc == row[0:1, r]), sd, -1e30)
        m = jnp.maximum(jnp.max(sp, axis=-1, keepdims=True), jnp.max(sd, axis=-1, keepdims=True))
        if i:
            e = slice(0, i * CH)
            so = dot_t(qi, k[e, :])
            so = jnp.where(doc == row[0:1, e], so, -1e30)
            m = jnp.maximum(m, jnp.max(so, axis=-1, keepdims=True))
        wp = jnp.exp2((sp - m) * c)
        wd = jnp.exp2((sd - m) * c)
        total = jnp.sum(wp, axis=-1, keepdims=True) + jnp.sum(wd, axis=-1, keepdims=True)
        acc = dot(wp.astype(BF), pv[...]) + dot(wd.astype(BF), v[r, :])
        if i:
            wo = jnp.exp2((so - m) * c)
            total = total + jnp.sum(wo, axis=-1, keepdims=True)
            acc = acc + dot(wo.astype(BF), v[e, :])
        out[r, :] = acc / total


def attend(q, kv, pk, pv, col, row, seg, h0=0, heads=2):
    return pl.pallas_call(
        attend_kernel,
        grid=(heads,),
        in_specs=[
            pl.BlockSpec((SEG, HD), lambda h: (seg, h + h0)),
            pl.BlockSpec((SEG, HD), lambda h: (seg, 2 * (h + h0))),
            pl.BlockSpec((SEG, HD), lambda h: (seg, 2 * (h + h0) + 1)),
            pl.BlockSpec((16, HD), lambda h: (0, h + h0)),
            pl.BlockSpec((16, HD), lambda h: (0, h + h0)),
            pl.BlockSpec((SEG, 8), lambda h: (seg, 0)),
            pl.BlockSpec((8, SEG), lambda h: (0, seg)),
        ],
        out_specs=pl.BlockSpec((SEG, HD), lambda h: (0, h)),
        out_shape=jax.ShapeDtypeStruct((SEG, heads * HD), F32),
        name="attend",
        cost_estimate=pl.CostEstimate(flops=700_000_000 * heads, transcendentals=0, bytes_accessed=2_000_000 * heads),
    )(q, kv, kv, pk, pv, col, row)


def recall_kernel(half, place, bound, q, ku, kv, mi, e1, info, got, col, row, rows, at0, at1, gain, out, pst, pdoc):
    b = pl.program_id(0)
    chunk = 2 * b + half

    @pl.when(b == 0)
    def _():
        x, g = place[1], place[0]
        st = [jnp.zeros((HD, HD), F32)] * 2
        cur = jnp.full((1, 128), -1.0, F32)
        pst[...] = jnp.zeros_like(pst)
        il = cur
        for j in range(4):
            here = x == j
            il = jnp.where(here, cur, il)
            for h in range(2):
                pst[h] = jnp.where(here, st[h], pst[h])
            l0, l1, last = read_payload(got, j)
            cont = (cur == last).astype(F32)
            for h, l in ((0, l0), (1, l1)):
                st[h] = st[h] * (jnp.exp(l) * cont) + got[j, h * HD : (h + 1) * HD, :].astype(F32)
            cur = last
        glast = info[2:3, :]
        first = g == 0
        ok = jnp.where(first, 1.0, (il == glast).astype(F32))
        for h in range(2):
            pst[h] = pst[h] * (jnp.exp(info[h : h + 1, :]) * ok) + e1[h]
        pdoc[0:1, :] = jnp.where(first, il, glast)

    mask = tri(CH)
    pos = lax.broadcasted_iota(jnp.int32, rows.shape, 1)
    ends = (pos < chunk * CH) & (lax.rem(pos, CH) == CH - 1)
    pre = jnp.sum(jnp.where(ends, rows[...], 0.0), axis=1, keepdims=True)
    doc = col[:, 0:1]
    pdoc_row = pdoc[0:1, :]
    carried = jnp.where(chunk == 0, pdoc_row, bound[chunk])
    joined = (carried == pdoc_row).astype(F32)
    live = (doc == carried[:, 0:1]).astype(F32)
    ok = mask & (doc == row[0:1, :])
    for h in range(2):
        s = slice(h * HD, (h + 1) * HD)
        qh = q[:, s]
        cc = col[:, 1 + h : 2 + h]
        dec = jnp.exp(jnp.where(ok, cc - row[1 + h : 2 + h, :], -1e30))
        inner = (dot_t(qh, ku[:, s]) * dec).astype(BF)
        rec = dot(inner, kv[:, (2 * h + 1) * HD : (2 * h + 2) * HD])
        f = jnp.exp(jnp.broadcast_to(pre[1 + h : 2 + h, :], (1, 128))) * joined
        m = mi[0, h] + pst[h] * f
        rec = rec + dot(qh, m.astype(BF)) * (jnp.exp(cc) * live)
        qw = qh.astype(F32)
        rec = rec * (lax.rsqrt(jnp.mean(qw * qw, axis=-1, keepdims=True) + 1e-6) * (1.0 / math.sqrt(HD)))
        at = jnp.where(chunk < SEG // CH, at0[:, s], at1[:, s])
        out[0, :, s] = (at + rms(rec, 1e-5) * gain[:, s]).astype(BF)


def recall(half, place, bound, q, ku, kv, mi, e1, info, got, col, row, at0, at1, gain):
    ch = lambda w: pl.BlockSpec((CH, w), lambda b, p, d: (2 * b + half, 0))
    full = lambda a: pl.BlockSpec(a.shape, lambda b, p, d: (0,) * a.ndim)
    per = SEG // CH
    gs = pltpu.PrefetchScalarGridSpec(
        num_scalar_prefetch=2,
        grid=(4,),
        in_specs=[
            ch(256),
            ch(256),
            ch(512),
            pl.BlockSpec((1, 2, HD, HD), lambda b, p, d: (2 * b + half, 0, 0, 0)),
            full(e1),
            full(info),
            full(got),
            ch(8),
            pl.BlockSpec((8, CH), lambda b, p, d: (0, 2 * b + half)),
            full(row),
            pl.BlockSpec((CH, 256), lambda b, p, d: (jnp.minimum(2 * b + half, per - 1), 0)),
            pl.BlockSpec((CH, 256), lambda b, p, d: (jnp.maximum(2 * b + half - per, 0), 0)),
            full(gain),
        ],
        out_specs=pl.BlockSpec((1, CH, 256), lambda b, p, d: (lax.rem(b - p[2] + 4, 4), 0, 0)),
        scratch_shapes=[pltpu.VMEM((2, HD, HD), F32), pltpu.VMEM((8, 128), F32)],
    )
    return pl.pallas_call(
        functools.partial(recall_kernel, half),
        grid_spec=gs,
        out_shape=jax.ShapeDtypeStruct((4, CH, 256), BF),
        name="recall",
        cost_estimate=pl.CostEstimate(flops=400_000_000, transcendentals=0, bytes_accessed=4_000_000),
    )(place, bound, q, ku, kv, mi, e1, info, got, col, row, row, at0, at1, gain)


def ffn_kernel(place, tok, gain, h0, h1, h2, h3, *rest):
    own = rest[0:4]
    gu = (rest[4:8], rest[8:12])
    do = (rest[12:15], rest[15:18])
    out, wgu, wd, wo, norm, acc, sem = rest[18:]
    core = place[3]
    count = [0]
    waits = {}

    def copy(key, src, dst):
        c = pltpu.make_async_copy(src, dst, sem.at[count[0]])
        count[0] += 1
        waits.setdefault(key, []).append(c)
        c.start()

    def fetch(kind, group):
        key = (kind, group)
        if group == 0:
            if kind == "out":
                copy(key, own[3], wo.at[0])
            elif kind == "up":
                copy(key, own[0], wgu.at[0, 0])
                copy(key, own[1], wgu.at[1, 0])
            else:
                copy(key, own[2], wd.at[0])
            return
        spots = (1, 2) if group == 1 else (3,)
        for which in range(2):
            at = core if which == 0 else 1 - core
            if kind == "up":
                pos = jnp.where(at == 0, place[1], place[4])
                span = pl.ds(spots[0], len(spots))
                for i, hop in enumerate((0, 3, 1, 2)):
                    p = lax.rem(pos + hop, 4)
                    copy(key, gu[which][i].at[pl.ds(spots[0] - 1, len(spots))], wgu.at[at, span, pl.ds(p * 176, 176), :])
                continue
            for i in spots:
                if kind == "down":
                    copy(key, do[which][i - 1].at[pl.ds(0, 352), :], wd.at[i, pl.ds(at * 352, 352), :])
                else:
                    copy(key, do[which][i - 1].at[pl.ds(352, 128), :], wo.at[i, pl.ds(at * 128, 128), :])

    def ready(kind, group):
        for c in waits[(kind, group)]:
            c.wait()

    for group in range(3):
        fetch("out", group)
    fetch("up", 0)
    fetch("down", 0)
    total = tok[...].astype(F32)
    for i, (h, group) in enumerate(((h0, 0), (h1, 1), (h3, None), (h2, 2))):
        if group is not None:
            ready("out", group)
        total = total + dot(h[...], wo[i])
    for group in (1, 2):
        fetch("up", group)
        fetch("down", group)
    resid = total.astype(BF).astype(F32)
    acc[...] = resid
    norm[...] = (rms(resid, 1e-5) * gain[...].astype(F32)).astype(BF)

    def step(i, carry):
        for index, group in ((0, 0), (1, 1), (3, 2)):
            @pl.when(i == index)
            def _():
                ready("up", group)
                ready("down", group)

        n = norm[...]
        g = dot_t(n, wgu[0, i])
        u = dot_t(n, wgu[1, i])
        hid = (g / (1.0 + jnp.exp(-g)) * u).astype(BF)
        acc[...] += dot(hid, wd[i])
        return carry

    lax.fori_loop(0, 4, step, 0)
    out[...] = acc[...].astype(BF)


def ffn(half, place, tokens, gain, heads, own, gu, gux, do, dox):
    d = tokens.shape[1]
    full = lambda a: pl.BlockSpec(a.shape, lambda i, p: (0,) * a.ndim)
    anys = pl.BlockSpec(memory_space=ANY)
    ws = [*own, *gu, *gux, *do, *dox]
    gs = pltpu.PrefetchScalarGridSpec(
        num_scalar_prefetch=1,
        grid=(1,),
        in_specs=[pl.BlockSpec((ROWS, d), lambda i, p: (2 * p[2] + half, 0)), full(gain)]
        + [full(h) for h in heads]
        + [anys] * len(ws),
        out_specs=pl.BlockSpec((ROWS, d), lambda i, p: (0, 0)),
        scratch_shapes=[
            pltpu.VMEM((2, 4, 704, 1024), BF),
            pltpu.VMEM((4, 704, 1024), BF),
            pltpu.VMEM((4, 256, 1024), BF),
            pltpu.VMEM((ROWS, d), BF),
            pltpu.VMEM((ROWS, d), F32),
            pltpu.SemaphoreType.DMA((32,)),
        ],
    )
    return pl.pallas_call(
        ffn_kernel,
        grid_spec=gs,
        out_shape=jax.ShapeDtypeStruct((ROWS, d), BF),
        name="ffn",
    )(place, tokens, gain, *heads, *ws)


def staged(ins, bufs, outs, sem):
    n = len(ins)
    first = [pltpu.make_async_copy(ins[i], bufs[i], sem.at[i]) for i in range(n)]
    second = [pltpu.make_async_copy(bufs[i], outs[i], sem.at[n + i]) for i in range(n)]
    for c in first:
        c.start()
    for a, b in zip(first, second):
        a.wait()
        b.start()
    for c in second:
        c.wait()


def place_kernel(source, got, out, buf, sem):
    n = out.shape[0]
    staged(
        [got.at[source[s], pl.ds(0, PAGE), :] for s in range(n)],
        [buf.at[s] for s in range(n)],
        [out.at[s] for s in range(n)],
        sem,
    )


def place_pages(source, got, count):
    anys = pl.BlockSpec(memory_space=ANY)
    shape = (count, PAGE, got.shape[2])
    return pl.pallas_call(
        place_kernel,
        in_specs=[pl.BlockSpec(memory_space=pltpu.SMEM), anys],
        out_specs=anys,
        out_shape=jax.ShapeDtypeStruct(shape, BF),
        scratch_shapes=[pltpu.VMEM(shape, BF), pltpu.SemaphoreType.DMA((2 * count,))],
        name="place",
    )(source, got)


def join_kernel(spots, place, *refs):
    pieces, out, bufs, sem = refs[: len(spots)], refs[-2 - len(spots)], refs[-1 - len(spots) : -1], refs[-1]
    y = place[2]
    outs = []
    for d, row, n in spots:
        outs.append(out.at[pl.ds(lax.rem(y + d, 4) * (2 * ROWS) + row, n), :])
    staged(pieces, bufs, outs, sem)


def join(place, pieces, spots, into=None):
    anys = pl.BlockSpec(memory_space=ANY)
    rest = [] if into is None else [into]
    width = pieces[0].shape[1]
    return pl.pallas_call(
        functools.partial(join_kernel, spots),
        in_specs=[pl.BlockSpec(memory_space=pltpu.SMEM)] + [anys] * (len(pieces) + len(rest)),
        out_specs=anys,
        out_shape=jax.ShapeDtypeStruct((8 * ROWS, width), BF),
        scratch_shapes=[pltpu.VMEM(p.shape, BF) for p in pieces] + [pltpu.SemaphoreType.DMA((2 * len(pieces),))],
        input_output_aliases={} if into is None else {1 + len(pieces): 0},
        name="join",
    )(place, *pieces, *rest)


def on_device(
    tokens, attn_gain, w_query, w_key, w_value, persist_key, persist_value, log_forget, mem_gain,
    w_out, ffn_gain, w_gate, w_up, w_down, doc_ids, page_owner, page_slot,
):
    count = tokens.shape[0]
    reqs = lax.axis_size("req")
    req, y = lax.axis_index("req"), lax.axis_index("tp")
    core, x, z = req % 2, req // 8, (req // 2) % 4
    place = jnp.stack([req % 8, x, y, core, z]).astype(jnp.int32)
    shift = lambda a, d: lax.ppermute(a, "tp", [(i, (i + d) % 4) for i in range(4)])
    swap = lambda a: lax.ppermute(a, "req", [(i, i ^ 1) for i in range(reqs)])
    tie = lambda *a: lax.optimization_barrier(a)

    def around(a, d):
        def to(i):
            xx, zz, c = i // 8, (i // 2) % 4, i % 2
            if c == 0:
                xx = (xx + d) % 4
            else:
                zz = (zz + d) % 4
            return xx * 8 + zz * 2 + c

        return lax.ppermute(a, "req", [(i, to(i)) for i in range(reqs)])

    gate, up = w_gate.T, w_up.T
    at = jnp.where(core == 0, x, z)
    cut = lambda w, i, n: lax.dynamic_slice_in_dim(w, i * n, n, 0)
    piece = jnp.where(core == 0, cut(gate, at, 176), cut(up, at, 176))
    s1, s3, s2 = [shift(piece, d) for d in (1, 3, 2)]
    half_do = jnp.concatenate([cut(w_down, core, 352), cut(w_out, core, 128)])
    do1, do3, do2 = [shift(half_do, d) for d in (1, 3, 2)]

    doc = doc_ids.astype(F32)
    row = jnp.concatenate([doc[None], log_forget.T, jnp.zeros((5, count), F32)])
    bound = jnp.concatenate([jnp.full((1,), -1.0, F32), doc[CH - 1 : -1 : CH]])

    hit = page_owner[None, :] == jnp.arange(reqs)[:, None]
    code = jnp.sum(jnp.where(hit, page_slot[None, :] + 1, 0), axis=1).astype(BF)
    codes = jnp.broadcast_to(code[:, None, None], (reqs, 8, 512))
    q, kv, ku, mi, pay, row, col, outgoing = project(
        page_owner, tokens, attn_gain[None], w_query, w_key, w_value, row, codes
    )

    group8 = [[i * 8 + k for k in range(8)] for i in range(reqs // 8)]
    group4 = [[i * 8 + k for i in range(reqs // 8)] for k in range(8)]
    spread = lambda a, g: lax.all_to_all(a, "req", 0, 0, tiled=True, axis_index_groups=g)
    got8 = spread(pay, group8)

    at0 = attend(q, kv, persist_key, persist_value, col, row, 0)
    at0, got8 = tie(at0, got8)
    e1, info, pay4 = combine(place, got8)
    got4 = spread(pay4, group4)
    q1, at0, s1, s2, s3, _ = tie(q, at0, s1, s2, s3, pay4)
    at1 = attend(q1, kv, persist_key, persist_value, col, row, 1)
    at1, got4, s1, s2, s3, do1, do3 = tie(at1, got4, s1, s2, s3, do1, do3)
    near = jnp.stack([s1, s3, s2])
    far = [around(near, d) for d in (1, 3, 2)]

    gain = mem_gain[None]
    own_w = (gate, up, w_down, w_out)
    mem = lambda half: recall(half, place, bound, q, ku, kv, mi, e1, info, got4, col, row, at0, at1, gain)
    send = lambda out: [out[0]] + [shift(out[d], d) for d in (1, 3, 2)]
    out0 = mem(0)
    heads0 = send(out0)
    out1 = mem(1)
    out1, do2, *heads0 = tie(out1, do2, *heads0)
    heads1 = send(out1)
    outgoing, near, out1, *far = tie(outgoing, near, out1, *far)
    arrived = lax.all_to_all(outgoing, "req", 0, 0, tiled=True)
    gu, do = [near, *far], [do1, do3, do2]
    gux, dox = [swap(a) for a in gu], [swap(a) for a in do]
    slots = arrived[:, PAGE, 0].astype(F32)
    wanted = slots[None, :] == (jnp.arange(count // PAGE) + 1).astype(F32)[:, None]
    source = jnp.sum(jnp.where(wanted, jnp.arange(reqs)[None, :], 0), axis=1).astype(jnp.int32)
    kv_cache = place_pages(jnp.clip(source, 0, reqs - 1), arrived, count // PAGE)

    feed = lambda half, heads: ffn(
        half, place, tokens, ffn_gain[None], (heads[0], heads[1], heads[3], heads[2]), own_w, gu, gux, do, dox
    )
    R, H = ROWS, ROWS // 2
    own0 = feed(0, heads0)
    own0, *heads1 = tie(own0, *heads1)
    a0, b0 = shift(own0, 1), shift(own0, -1)
    own1 = feed(1, heads1)
    a1, b1 = shift(own1, 1), shift(own1, -1)
    lo0, hi0 = shift(a0[:H], 1), shift(b0[H:], -1)
    joined = join(place, [own0, a0, b0, own1], ((0, 0, R), (3, 0, R), (1, 0, R), (0, R, R)))
    a1, b1, joined, kv_cache = tie(a1, b1, joined, kv_cache)
    lo1, hi1 = shift(a1[:H], 1), shift(b1[H:], -1)
    joined = join(place, [a1, b1, lo0, hi0], ((3, R, R), (1, R, R), (2, 0, H), (2, H, H)), joined)
    lo1, hi1, joined = tie(lo1, hi1, joined)
    layer_out = join(place, [lo1, hi1], ((2, R, H), (2, R + H, H)), joined)
    return layer_out, kv_cache


def solution(mesh):
    return jax.shard_map(
        on_device,
        mesh=mesh,
        in_specs=(
            P("req", None), P(), P(None, "tp"), P(None, "tp"), P(None, "tp"), P(None, "tp"), P(None, "tp"),
            P("req", "tp"), P("tp"), P("tp", None), P(), P(None, "tp"), P(None, "tp"), P("tp", None),
            P("req"), P("req"), P("req"),
        ),
        out_specs=(P("req", None), P("req", None, "tp")),
        check_vma=False,
    )
```

```python
import functools
import math

import jax
import jax.numpy as jnp
from jax import lax
from jax.experimental import pallas as pl
from jax.experimental.pallas import tpu as pltpu
from jax.sharding import PartitionSpec as P

HD = 128
SEG = 1024
PAGE = 128
CH = 256
ROWS = 256
F32 = jnp.float32
BF = jnp.bfloat16
ANY = pl.ANY


def rms(x, eps):
    return x * lax.rsqrt(jnp.mean(x * x, axis=-1, keepdims=True) + eps)


def dot(a, b):
    return jnp.dot(a, b, preferred_element_type=F32)


def dot_t(a, b):
    return lax.dot_general(a, b, (((1,), (1,)), ((), ())), preferred_element_type=F32)


def dot_l(a, b):
    return lax.dot_general(a, b, (((0,), (0,)), ((), ())), preferred_element_type=F32)


def tri(n, lower=True):
    r = lax.broadcasted_iota(jnp.int32, (n, n), 0)
    c = lax.broadcasted_iota(jnp.int32, (n, n), 1)
    return (r >= c) if lower else (r <= c)


def split3(x):
    hi = x.astype(BF).astype(F32)
    mid = (x - hi).astype(BF).astype(F32)
    return hi, mid, x - hi - mid


def running(info):
    parts = jnp.concatenate(split3(info), axis=0).astype(BF)
    c = dot(parts, tri(info.shape[1], False).astype(F32).astype(BF))
    c = c[0:8] + c[8:16] + c[16:24]
    return jnp.where(lax.broadcasted_iota(jnp.int32, info.shape, 0) == 0, info, c)


def normed(tok, gain, out):
    g = gain[...].astype(F32)
    for b in range(CH // 32):
        r = slice(b * 32, (b + 1) * 32)
        out[r, :] = (rms(tok[r, :].astype(F32), 1e-5) * g).astype(BF)


def project_kernel(owner, slot, tok0, tok1, tok2, gain, wq, wk, wv, row, q_out, kv_out, ku_out, min_out, pay_out, cr_out, cc_out, sent, st, misc, buf, n0, n1, codes, sem):
    i = pl.program_id(0)
    here = CH // PAGE
    last_sem = 2 * here

    @pl.when(i == 0)
    def _():
        st[...] = jnp.zeros_like(st)
        misc[...] = jnp.full_like(misc, -1.0)
        misc[0:2, :] = jnp.zeros((2, 128), F32)
        codes[...] = jnp.zeros_like(codes)
        for p in range(owner.shape[0]):
            codes[owner[p]] = jnp.broadcast_to((slot[p] + 1).astype(F32), codes.shape[1:]).astype(BF)
        pltpu.make_async_copy(codes, sent.at[:, pl.ds(PAGE, 8), :], sem.at[last_sem]).start()
        normed(tok0, gain, n0)

    copies = []
    for j, (now, tok, later) in enumerate(((n0, tok1, n1), (n1, tok2, n0))):
        r = slice(j * CH, (j + 1) * CH)
        n = now[...]
        k = dot(n, wk[...]).astype(BF)
        v = dot(n, wv[...]).astype(BF)
        q_out[r, :] = dot(n, wq[...]).astype(BF)
        for h in range(2):
            s = slice(h * HD, (h + 1) * HD)
            kv_out[r, 2 * h * HD : (2 * h + 1) * HD] = k[:, s]
            kv_out[r, (2 * h + 1) * HD : (2 * h + 2) * HD] = v[:, s]
            for p in range(here):
                w = slice(p * PAGE, (p + 1) * PAGE)
                buf[j * here + p, :, 2 * h * HD : (2 * h + 1) * HD] = k[w, s]
                buf[j * here + p, :, (2 * h + 1) * HD : (2 * h + 2) * HD] = v[w, s]
        for p in range(here):
            m = j * here + p
            c = pltpu.make_async_copy(buf.at[m], sent.at[owner[i * 2 * here + m], pl.ds(0, PAGE), :], sem.at[m])
            c.start()
            copies.append(c)
        normed(tok, gain, later)
        cr = running(row[:, r])
        cc = cr.T
        cr_out[:, r] = cr
        cc_out[r, :] = cc
        last = cr[0:1, CH - 1 : CH]
        same = (cc[:, 0:1] == last).astype(F32)
        last_row = jnp.broadcast_to(last, (1, 128))
        cont = (last_row == misc[2:3, :]).astype(F32)
        for h in range(2):
            s = slice(h * HD, (h + 1) * HD)
            ku = rms(k[:, s].astype(F32), 1e-6) * (1.0 / math.sqrt(HD))
            ku_out[r, s] = ku.astype(BF)
            end_h = cr[1 + h : 2 + h, CH - 1 : CH]
            w = jnp.exp(end_h - cc[:, 1 + h : 2 + h]) * same
            add = dot_l((ku * w).astype(BF), v[:, s])
            end_row = jnp.broadcast_to(end_h, (1, 128))
            old = st[h]
            min_out[j, h] = old
            st[h] = old * (jnp.exp(end_row) * cont) + add
            misc[h : h + 1, :] = misc[h : h + 1, :] + end_row
        misc[2:3, :] = last_row

    @pl.when(i == pl.num_programs(0) - 1)
    def _():
        write_payload(pay_out, st, misc[0:1, :], misc[1:2, :], misc[2:3, :])
        pltpu.make_async_copy(codes, sent.at[:, pl.ds(PAGE, 8), :], sem.at[last_sem]).wait()

    for c in copies:
        c.wait()


def write_payload(out, st, l0, l1, last):
    hi = jnp.floor(last * (1.0 / 256.0))
    rows = [*split3(l0), *split3(l1), hi, last - hi * 256.0]
    tail = jnp.concatenate(rows, axis=0).astype(BF)
    for i in range(out.shape[0]):
        for h in range(2):
            out[i, h * HD : (h + 1) * HD, :] = st[h].astype(BF)
        out[i, 2 * HD : 2 * HD + 8, :] = tail


def read_payload(ref, j):
    s = ref[j, 2 * HD : 2 * HD + 8, :].astype(F32)
    l0 = s[0:1] + s[1:2] + s[2:3]
    l1 = s[3:4] + s[4:5] + s[5:6]
    return l0, l1, s[6:7] * 256.0 + s[7:8]


def project(owner, slot, tokens, gain, wq, wk, wv, row, reqs):
    t, d = tokens.shape
    tile = 512
    n = t // tile
    c = tile // CH
    full = lambda a: pl.BlockSpec(a.shape, lambda i, o, l: (0,) * a.ndim)
    rows = lambda w: pl.BlockSpec((tile, w), lambda i, o, l: (i, 0))
    lanes = pl.BlockSpec((8, tile), lambda i, o, l: (0, i))
    gs = pltpu.PrefetchScalarGridSpec(
        num_scalar_prefetch=2,
        grid=(n,),
        in_specs=[
            pl.BlockSpec((CH, d), lambda i, o, l: (0, 0)),
            pl.BlockSpec((CH, d), lambda i, o, l: (2 * i + 1, 0)),
            pl.BlockSpec((CH, d), lambda i, o, l: (jnp.minimum(2 * i + 2, 2 * n - 1), 0)),
            full(gain), full(wq), full(wk), full(wv), lanes,
        ],
        out_specs=[
            rows(256),
            rows(512),
            rows(256),
            pl.BlockSpec((c, 2, HD, HD), lambda i, o, l: (i, 0, 0, 0)),
            pl.BlockSpec((8, 264, 128), lambda i, o, l: (0, 0, 0)),
            lanes,
            rows(8),
            pl.BlockSpec(memory_space=ANY),
        ],
        scratch_shapes=[
            pltpu.VMEM((2, HD, HD), F32),
            pltpu.VMEM((8, 128), F32),
            pltpu.VMEM((tile // PAGE, PAGE, 512), BF),
            pltpu.VMEM((CH, d), BF),
            pltpu.VMEM((CH, d), BF),
            pltpu.VMEM((reqs, 8, 512), BF),
            pltpu.SemaphoreType.DMA((tile // PAGE + 1,)),
        ],
    )
    return pl.pallas_call(
        project_kernel,
        grid_spec=gs,
        out_shape=[
            jax.ShapeDtypeStruct((t, 256), BF),
            jax.ShapeDtypeStruct((t, 512), BF),
            jax.ShapeDtypeStruct((t, 256), BF),
            jax.ShapeDtypeStruct((t // CH, 2, HD, HD), F32),
            jax.ShapeDtypeStruct((8, 264, 128), BF),
            jax.ShapeDtypeStruct((8, t), F32),
            jax.ShapeDtypeStruct((t, 8), F32),
            jax.ShapeDtypeStruct((reqs, PAGE + 8, 512), BF),
        ],
        name="project",
    )(owner, slot, tokens, tokens, tokens, gain, wq, wk, wv, row)


def combine_kernel(place, got, e_out, info_out, pay_out, st):
    g = place[0]
    st[...] = jnp.zeros_like(st)
    e_out[...] = jnp.zeros_like(e_out)
    cur = jnp.full((1, 128), -1.0, F32)
    t0 = t1 = jnp.zeros((1, 128), F32)
    i0, i1, il = t0, t1, cur
    for j in range(8):
        @pl.when(g == j)
        def _():
            e_out[...] = st[...]

        here = g == j
        i0, i1, il = jnp.where(here, t0, i0), jnp.where(here, t1, i1), jnp.where(here, cur, il)
        l0, l1, last = read_payload(got, j)
        cont = (cur == last).astype(F32)
        for h, l in ((0, l0), (1, l1)):
            st[h] = st[h] * (jnp.exp(l) * cont) + got[j, h * HD : (h + 1) * HD, :].astype(F32)
        t0, t1, cur = t0 + l0, t1 + l1, last
    info_out[...] = jnp.concatenate([i0, i1, il, jnp.zeros((5, 128), F32)], axis=0)
    write_payload(pay_out, st, t0, t1, cur)


def combine(place, got):
    vm = pl.BlockSpec(memory_space=pltpu.VMEM)
    return pl.pallas_call(
        combine_kernel,
        in_specs=[pl.BlockSpec(memory_space=pltpu.SMEM), vm],
        out_specs=[vm, vm, vm],
        out_shape=[
            jax.ShapeDtypeStruct((2, HD, HD), F32),
            jax.ShapeDtypeStruct((8, 128), F32),
            jax.ShapeDtypeStruct((4, 264, 128), BF),
        ],
        scratch_shapes=[pltpu.VMEM((2, HD, HD), F32)],
        name="combine",
    )(place, got)


def attend_kernel(q, k, v, pk, pv, col, row, out):
    scale = 1.0 / math.sqrt(HD)
    c = scale * math.log2(math.e)
    mask = tri(CH)
    for i in range(SEG // CH):
        r = slice(i * CH, (i + 1) * CH)
        qi = q[r, :]
        doc = col[r, 0:1]
        sp = dot_t(qi, pk[...])
        sd = dot_t(qi, k[r, :])
        sd = jnp.where(mask & (doc == row[0:1, r]), sd, -1e30)
        m = jnp.maximum(jnp.max(sp, axis=-1, keepdims=True), jnp.max(sd, axis=-1, keepdims=True))
        if i:
            e = slice(0, i * CH)
            so = dot_t(qi, k[e, :])
            so = jnp.where(doc == row[0:1, e], so, -1e30)
            m = jnp.maximum(m, jnp.max(so, axis=-1, keepdims=True))
        wp = jnp.exp2((sp - m) * c)
        wd = jnp.exp2((sd - m) * c)
        total = jnp.sum(wp, axis=-1, keepdims=True) + jnp.sum(wd, axis=-1, keepdims=True)
        acc = dot(wp.astype(BF), pv[...]) + dot(wd.astype(BF), v[r, :])
        if i:
            wo = jnp.exp2((so - m) * c)
            total = total + jnp.sum(wo, axis=-1, keepdims=True)
            acc = acc + dot(wo.astype(BF), v[e, :])
        out[r, :] = acc / total


def attend(q, kv, pk, pv, col, row, seg, h0=0, heads=2):
    return pl.pallas_call(
        attend_kernel,
        grid=(heads,),
        in_specs=[
            pl.BlockSpec((SEG, HD), lambda h: (seg, h + h0)),
            pl.BlockSpec((SEG, HD), lambda h: (seg, 2 * (h + h0))),
            pl.BlockSpec((SEG, HD), lambda h: (seg, 2 * (h + h0) + 1)),
            pl.BlockSpec((16, HD), lambda h: (0, h + h0)),
            pl.BlockSpec((16, HD), lambda h: (0, h + h0)),
            pl.BlockSpec((SEG, 8), lambda h: (seg, 0)),
            pl.BlockSpec((8, SEG), lambda h: (0, seg)),
        ],
        out_specs=pl.BlockSpec((SEG, HD), lambda h: (0, h)),
        out_shape=jax.ShapeDtypeStruct((SEG, heads * HD), F32),
        name="attend",
        cost_estimate=pl.CostEstimate(flops=700_000_000 * heads, transcendentals=0, bytes_accessed=2_000_000 * heads),
    )(q, kv, kv, pk, pv, col, row)


def recall_kernel(half, place, bound, q, ku, kv, mi, e1, info, got, col, row, rows, at0, at1, gain, out, pst, pdoc):
    b = pl.program_id(0)
    chunk = 2 * b + half

    @pl.when(b == 0)
    def _():
        x, g = place[1], place[0]
        st = [jnp.zeros((HD, HD), F32)] * 2
        cur = jnp.full((1, 128), -1.0, F32)
        pst[...] = jnp.zeros_like(pst)
        il = cur
        for j in range(4):
            here = x == j
            il = jnp.where(here, cur, il)
            for h in range(2):
                pst[h] = jnp.where(here, st[h], pst[h])
            l0, l1, last = read_payload(got, j)
            cont = (cur == last).astype(F32)
            for h, l in ((0, l0), (1, l1)):
                st[h] = st[h] * (jnp.exp(l) * cont) + got[j, h * HD : (h + 1) * HD, :].astype(F32)
            cur = last
        glast = info[2:3, :]
        first = g == 0
        ok = jnp.where(first, 1.0, (il == glast).astype(F32))
        for h in range(2):
            pst[h] = pst[h] * (jnp.exp(info[h : h + 1, :]) * ok) + e1[h]
        pdoc[0:1, :] = jnp.where(first, il, glast)

    mask = tri(CH)
    pos = lax.broadcasted_iota(jnp.int32, rows.shape, 1)
    ends = (pos < chunk * CH) & (lax.rem(pos, CH) == CH - 1)
    pre = jnp.sum(jnp.where(ends, rows[...], 0.0), axis=1, keepdims=True)
    doc = col[:, 0:1]
    pdoc_row = pdoc[0:1, :]
    carried = jnp.where(chunk == 0, pdoc_row, bound[chunk])
    joined = (carried == pdoc_row).astype(F32)
    live = (doc == carried[:, 0:1]).astype(F32)
    ok = mask & (doc == row[0:1, :])
    for h in range(2):
        s = slice(h * HD, (h + 1) * HD)
        qh = q[:, s]
        cc = col[:, 1 + h : 2 + h]
        dec = jnp.exp(jnp.where(ok, cc - row[1 + h : 2 + h, :], -1e30))
        inner = (dot_t(qh, ku[:, s]) * dec).astype(BF)
        rec = dot(inner, kv[:, (2 * h + 1) * HD : (2 * h + 2) * HD])
        f = jnp.exp(jnp.broadcast_to(pre[1 + h : 2 + h, :], (1, 128))) * joined
        m = mi[0, h] + pst[h] * f
        rec = rec + dot(qh, m.astype(BF)) * (jnp.exp(cc) * live)
        qw = qh.astype(F32)
        rec = rec * (lax.rsqrt(jnp.mean(qw * qw, axis=-1, keepdims=True) + 1e-6) * (1.0 / math.sqrt(HD)))
        at = jnp.where(chunk < SEG // CH, at0[:, s], at1[:, s])
        out[0, :, s] = (at + rms(rec, 1e-5) * gain[:, s]).astype(BF)


def recall(half, place, bound, q, ku, kv, mi, e1, info, got, col, row, at0, at1, gain):
    ch = lambda w: pl.BlockSpec((CH, w), lambda b, p, d: (2 * b + half, 0))
    full = lambda a: pl.BlockSpec(a.shape, lambda b, p, d: (0,) * a.ndim)
    per = SEG // CH
    gs = pltpu.PrefetchScalarGridSpec(
        num_scalar_prefetch=2,
        grid=(4,),
        in_specs=[
            ch(256),
            ch(256),
            ch(512),
            pl.BlockSpec((1, 2, HD, HD), lambda b, p, d: (2 * b + half, 0, 0, 0)),
            full(e1),
            full(info),
            full(got),
            ch(8),
            pl.BlockSpec((8, CH), lambda b, p, d: (0, 2 * b + half)),
            full(row),
            pl.BlockSpec((CH, 256), lambda b, p, d: (jnp.minimum(2 * b + half, per - 1), 0)),
            pl.BlockSpec((CH, 256), lambda b, p, d: (jnp.maximum(2 * b + half - per, 0), 0)),
            full(gain),
        ],
        out_specs=pl.BlockSpec((1, CH, 256), lambda b, p, d: (b if half == 0 else lax.rem(b - p[2] + 4, 4), 0, 0)),
        scratch_shapes=[pltpu.VMEM((2, HD, HD), F32), pltpu.VMEM((8, 128), F32)],
    )
    return pl.pallas_call(
        functools.partial(recall_kernel, half),
        grid_spec=gs,
        out_shape=jax.ShapeDtypeStruct((4, CH, 256), BF),
        name="recall",
        cost_estimate=pl.CostEstimate(flops=400_000_000, transcendentals=0, bytes_accessed=4_000_000),
    )(place, bound, q, ku, kv, mi, e1, info, got, col, row, row, at0, at1, gain)


def ffn_kernel(half, place, gain, tokens, *rest):
    y = place[2]
    if half == 0:
        heads = [rest[0].at[lax.rem(y - d + 4, 4)] for d in (0, 1, 3, 2)]
    else:
        heads = rest[0:4]
    rest = rest[1:] if half == 0 else rest[4:]
    own = rest[0:4]
    gu = (rest[4:8], rest[8:12])
    do = (rest[12:15], rest[15:18])
    out, tok, hv, wgu, wd, wo, norm, acc, sem = rest[18:]
    core = place[3]
    count = [0]
    waits = {}

    def copy(key, src, dst):
        c = pltpu.make_async_copy(src, dst, sem.at[count[0]])
        count[0] += 1
        waits.setdefault(key, []).append(c)
        c.start()

    def fetch(kind, group):
        key = (kind, group)
        if group == 0:
            if kind == "out":
                copy(key, own[3], wo.at[0])
            elif kind == "up":
                copy(key, own[0], wgu.at[0, 0])
                copy(key, own[1], wgu.at[1, 0])
            else:
                copy(key, own[2], wd.at[0])
            return
        spots = (1, 2) if group == 1 else (3,)
        for which in range(2):
            at = core if which == 0 else 1 - core
            if kind == "up":
                pos = jnp.where(at == 0, place[1], place[4])
                span = pl.ds(spots[0], len(spots))
                for i, hop in enumerate((0, 3, 1, 2)):
                    p = lax.rem(pos + hop, 4)
                    copy(key, gu[which][i].at[pl.ds(spots[0] - 1, len(spots))], wgu.at[at, span, pl.ds(p * 176, 176), :])
                continue
            for i in spots:
                if kind == "down":
                    copy(key, do[which][i - 1].at[pl.ds(0, 352), :], wd.at[i, pl.ds(at * 352, 352), :])
                else:
                    copy(key, do[which][i - 1].at[pl.ds(352, 128), :], wo.at[i, pl.ds(at * 128, 128), :])

    def ready(kind, group):
        for c in waits[(kind, group)]:
            c.wait()

    copy(("in", 0), tokens.at[pl.ds((2 * y + half) * ROWS, ROWS), :], tok)
    for i in range(4):
        copy(("in", 0), heads[i], hv.at[i])
    for group in range(3):
        fetch("out", group)
    fetch("up", 0)
    fetch("down", 0)
    ready("in", 0)
    total = tok[...].astype(F32)
    for i, group in enumerate((0, 1, None, 2)):
        if group is not None:
            ready("out", group)
        total = total + dot(hv[i], wo[i])
    for group in (1, 2):
        fetch("up", group)
        fetch("down", group)
    resid = total.astype(BF).astype(F32)
    acc[...] = resid
    norm[...] = (rms(resid, 1e-5) * gain[...].astype(F32)).astype(BF)

    def step(i, carry):
        for index, group in ((0, 0), (1, 1), (3, 2)):
            @pl.when(i == index)
            def _():
                ready("up", group)
                ready("down", group)

        n = norm[...]
        g = dot_t(n, wgu[0, i])
        u = dot_t(n, wgu[1, i])
        hid = (g / (1.0 + jnp.exp(-g)) * u).astype(BF)
        acc[...] += dot(hid, wd[i])
        return carry

    lax.fori_loop(0, 4, step, 0)
    out[...] = acc[...].astype(BF)


def ffn(half, place, tokens, gain, heads, own, gu, gux, do, dox):
    d = tokens.shape[1]
    full = lambda a: pl.BlockSpec(a.shape, lambda i, p: (0,) * a.ndim)
    anys = pl.BlockSpec(memory_space=ANY)
    ws = [*own, *gu, *gux, *do, *dox]
    gs = pltpu.PrefetchScalarGridSpec(
        num_scalar_prefetch=1,
        grid=(1,),
        in_specs=[full(gain)] + [anys] * (1 + len(heads) + len(ws)),
        out_specs=pl.BlockSpec((ROWS, d), lambda i, p: (0, 0)),
        scratch_shapes=[
            pltpu.VMEM((ROWS, d), BF),
            pltpu.VMEM((4, ROWS, 256), BF),
            pltpu.VMEM((2, 4, 704, 1024), BF),
            pltpu.VMEM((4, 704, 1024), BF),
            pltpu.VMEM((4, 256, 1024), BF),
            pltpu.VMEM((ROWS, d), BF),
            pltpu.VMEM((ROWS, d), F32),
            pltpu.SemaphoreType.DMA((37,)),
        ],
    )
    return pl.pallas_call(
        functools.partial(ffn_kernel, half),
        grid_spec=gs,
        out_shape=jax.ShapeDtypeStruct((ROWS, d), BF),
        name="ffn",
    )(place, gain, tokens, *heads, *ws)


def staged(ins, bufs, outs, sem):
    n = len(ins)
    first = [pltpu.make_async_copy(ins[i], bufs[i], sem.at[i]) for i in range(n)]
    second = [pltpu.make_async_copy(bufs[i], outs[i], sem.at[n + i]) for i in range(n)]
    for c in first:
        c.start()
    for a, b in zip(first, second):
        a.wait()
        b.start()
    for c in second:
        c.wait()


def place_kernel(source, got, out, buf, sem):
    n = out.shape[0]
    staged(
        [got.at[source[s], pl.ds(0, PAGE), :] for s in range(n)],
        [buf.at[s] for s in range(n)],
        [out.at[s] for s in range(n)],
        sem,
    )


def place_pages(source, got, count):
    anys = pl.BlockSpec(memory_space=ANY)
    shape = (count, PAGE, got.shape[2])
    return pl.pallas_call(
        place_kernel,
        in_specs=[pl.BlockSpec(memory_space=pltpu.SMEM), anys],
        out_specs=anys,
        out_shape=jax.ShapeDtypeStruct(shape, BF),
        scratch_shapes=[pltpu.VMEM(shape, BF), pltpu.SemaphoreType.DMA((2 * count,))],
        name="place",
    )(source, got)


def join_kernel(spots, place, *refs):
    pieces, out, bufs, sem = refs[: len(spots)], refs[-2 - len(spots)], refs[-1 - len(spots) : -1], refs[-1]
    y = place[2]
    outs = []
    for d, row, n in spots:
        outs.append(out.at[pl.ds(lax.rem(y + d, 4) * (2 * ROWS) + row, n), :])
    staged(pieces, bufs, outs, sem)


def join(place, pieces, spots, into=None):
    anys = pl.BlockSpec(memory_space=ANY)
    rest = [] if into is None else [into]
    width = pieces[0].shape[1]
    return pl.pallas_call(
        functools.partial(join_kernel, spots),
        in_specs=[pl.BlockSpec(memory_space=pltpu.SMEM)] + [anys] * (len(pieces) + len(rest)),
        out_specs=anys,
        out_shape=jax.ShapeDtypeStruct((8 * ROWS, width), BF),
        scratch_shapes=[pltpu.VMEM(p.shape, BF) for p in pieces] + [pltpu.SemaphoreType.DMA((2 * len(pieces),))],
        input_output_aliases={} if into is None else {1 + len(pieces): 0},
        name="join",
    )(place, *pieces, *rest)


def cut_kernel(place, gate, up, down, last, piece, both, sem):
    core = place[3]
    at = jnp.where(core == 0, place[1], place[4])
    rows = pl.ds(at * 176, 176)
    from_gate = pltpu.make_async_copy(gate.at[rows, :], piece, sem.at[0])
    from_up = pltpu.make_async_copy(up.at[rows, :], piece, sem.at[0])
    rest = [
        pltpu.make_async_copy(down.at[pl.ds(core * 352, 352), :], both.at[pl.ds(0, 352), :], sem.at[1]),
        pltpu.make_async_copy(last.at[pl.ds(core * 128, 128), :], both.at[pl.ds(352, 128), :], sem.at[2]),
    ]

    @pl.when(core == 0)
    def _():
        from_gate.start()

    @pl.when(core != 0)
    def _():
        from_up.start()

    for c in rest:
        c.start()
    from_gate.wait()
    for c in rest:
        c.wait()


def cut_weights(place, gate, up, down, last):
    anys = pl.BlockSpec(memory_space=ANY)
    vm = pl.BlockSpec(memory_space=pltpu.VMEM)
    width = gate.shape[1]
    return pl.pallas_call(
        cut_kernel,
        in_specs=[pl.BlockSpec(memory_space=pltpu.SMEM)] + [anys] * 4,
        out_specs=[vm, vm],
        out_shape=[jax.ShapeDtypeStruct((176, width), BF), jax.ShapeDtypeStruct((480, width), BF)],
        scratch_shapes=[pltpu.SemaphoreType.DMA((3,))],
        name="cut_weights",
    )(place, gate, up, down, last)


def on_device(
    tokens, attn_gain, w_query, w_key, w_value, persist_key, persist_value, log_forget, mem_gain,
    w_out, ffn_gain, w_gate, w_up, w_down, doc_ids, page_owner, page_slot,
):
    count = tokens.shape[0]
    reqs = lax.axis_size("req")
    req, y = lax.axis_index("req"), lax.axis_index("tp")
    core, x, z = req % 2, req // 8, (req // 2) % 4
    place = jnp.stack([req % 8, x, y, core, z]).astype(jnp.int32)
    shift = lambda a, d: lax.ppermute(a, "tp", [(i, (i + d) % 4) for i in range(4)])
    swap = lambda a: lax.ppermute(a, "req", [(i, i ^ 1) for i in range(reqs)])
    tie = lambda *a: lax.optimization_barrier(a)

    def around(a, d):
        def to(i):
            xx, zz, c = i // 8, (i // 2) % 4, i % 2
            if c == 0:
                xx = (xx + d) % 4
            else:
                zz = (zz + d) % 4
            return xx * 8 + zz * 2 + c

        return lax.ppermute(a, "req", [(i, to(i)) for i in range(reqs)])

    gate, up = w_gate.T, w_up.T
    piece, half_do = cut_weights(place, gate, up, w_down, w_out)
    s1, s3, s2 = [shift(piece, d) for d in (1, 3, 2)]
    do1, do3, do2 = [shift(half_do, d) for d in (1, 3, 2)]

    doc = doc_ids.astype(F32)
    row = jnp.concatenate([doc[None], log_forget.T, jnp.zeros((5, count), F32)])
    bound = jnp.concatenate([jnp.full((1,), -1.0, F32), doc[CH - 1 : -1 : CH]])

    q, kv, ku, mi, pay, row, col, outgoing = project(
        page_owner, page_slot, tokens, attn_gain[None], w_query, w_key, w_value, row, reqs
    )

    group8 = [[i * 8 + k for k in range(8)] for i in range(reqs // 8)]
    group4 = [[i * 8 + k for i in range(reqs // 8)] for k in range(8)]
    spread = lambda a, g: lax.all_to_all(a, "req", 0, 0, tiled=True, axis_index_groups=g)
    got8 = spread(pay, group8)

    q, s1, s2, s3 = tie(q, s1, s2, s3)
    at0 = attend(q, kv, persist_key, persist_value, col, row, 0)
    at0, got8 = tie(at0, got8)
    e1, info, pay4 = combine(place, got8)
    got4 = spread(pay4, group4)
    q1, at0, _ = tie(q, at0, pay4)
    at1 = attend(q1, kv, persist_key, persist_value, col, row, 1)
    at1, got4, s1, s2, s3, do1, do3 = tie(at1, got4, s1, s2, s3, do1, do3)
    near = jnp.stack([s1, s3, s2])
    far = [around(near, d) for d in (1, 3, 2)]

    gain = mem_gain[None]
    own_w = (gate, up, w_down, w_out)
    mem = lambda half: recall(half, place, bound, q, ku, kv, mi, e1, info, got4, col, row, at0, at1, gain)
    do1x = swap(do1)
    out0 = mem(0)
    out0, do1x, do2 = tie(out0, do1x, do2)
    heads0 = [lax.all_to_all(out0, "tp", 0, 0, tiled=True)]
    do3x = swap(do3)
    out1 = mem(1)
    out1, do3x, heads0[0] = tie(out1, do3x, heads0[0])
    heads1 = [out1[0]] + [shift(out1[d], d) for d in (1, 3, 2)]
    near, outgoing, _, *far = tie(near, outgoing, out1, *far)
    nearx, do2x, *farx = [swap(a) for a in (near, do2, *far)]
    outgoing, farx[0] = tie(outgoing, farx[0])
    arrived = lax.all_to_all(outgoing, "req", 0, 0, tiled=True)
    gu, do = [near, *far], [do1, do3, do2]
    gux, dox = [nearx, *farx], [do1x, do3x, do2x]

    slots = arrived[:, PAGE, 0].astype(F32)
    wanted = slots[None, :] == (jnp.arange(count // PAGE) + 1).astype(F32)[:, None]
    source = jnp.sum(jnp.where(wanted, jnp.arange(reqs)[None, :], 0), axis=1).astype(jnp.int32)
    kv_cache = place_pages(jnp.clip(source, 0, reqs - 1), arrived, count // PAGE)

    feed = lambda half, heads: ffn(
        half, place, tokens, ffn_gain[None], heads, own_w, gu, gux, do, dox
    )
    R, H = ROWS, ROWS // 2
    own0 = feed(0, heads0)
    own0, *heads1 = tie(own0, *heads1)
    a0, b0 = shift(own0, 1), shift(own0, -1)
    own1 = feed(1, heads1)
    a1, b1 = shift(own1, 1), shift(own1, -1)
    lo0, hi0 = shift(a0[:H], 1), shift(b0[H:], -1)
    joined = join(place, [own0, a0, b0, own1], ((0, 0, R), (3, 0, R), (1, 0, R), (0, R, R)))
    a1, b1, joined, kv_cache = tie(a1, b1, joined, kv_cache)
    lo1, hi1 = shift(a1[:H], 1), shift(b1[H:], -1)
    joined = join(place, [a1, b1, lo0, hi0], ((3, R, R), (1, R, R), (2, 0, H), (2, H, H)), joined)
    lo1, hi1, joined = tie(lo1, hi1, joined)
    layer_out = join(place, [lo1, hi1], ((2, R, H), (2, R + H, H)), joined)
    return layer_out, kv_cache


def solution(mesh):
    return jax.shard_map(
        on_device,
        mesh=mesh,
        in_specs=(
            P("req", None), P(), P(None, "tp"), P(None, "tp"), P(None, "tp"), P(None, "tp"), P(None, "tp"),
            P("req", "tp"), P("tp"), P("tp", None), P(), P(None, "tp"), P(None, "tp"), P("tp", None),
            P("req"), P("req"), P("req"),
        ),
        out_specs=(P("req", None), P("req", None, "tp")),
        check_vma=False,
    )
```

```python
import functools
import math

import jax
import jax.numpy as jnp
from jax import lax
from jax.experimental import pallas as pl
from jax.experimental.pallas import tpu as pltpu
from jax.sharding import PartitionSpec as P

HD = 128
SEG = 1024
PAGE = 128
CH = 256
ROWS = 256
F32 = jnp.float32
BF = jnp.bfloat16
ANY = pl.ANY


def rms(x, eps):
    return x * lax.rsqrt(jnp.mean(x * x, axis=-1, keepdims=True) + eps)


def dot(a, b):
    return jnp.dot(a, b, preferred_element_type=F32)


def dot_t(a, b):
    return lax.dot_general(a, b, (((1,), (1,)), ((), ())), preferred_element_type=F32)


def dot_l(a, b):
    return lax.dot_general(a, b, (((0,), (0,)), ((), ())), preferred_element_type=F32)


def tri(n, lower=True):
    r = lax.broadcasted_iota(jnp.int32, (n, n), 0)
    c = lax.broadcasted_iota(jnp.int32, (n, n), 1)
    return (r >= c) if lower else (r <= c)


def split3(x):
    hi = x.astype(BF).astype(F32)
    mid = (x - hi).astype(BF).astype(F32)
    return hi, mid, x - hi - mid


def running(info):
    parts = jnp.concatenate(split3(info), axis=0).astype(BF)
    c = dot(parts, tri(info.shape[1], False).astype(F32).astype(BF))
    c = c[0:8] + c[8:16] + c[16:24]
    return jnp.where(lax.broadcasted_iota(jnp.int32, info.shape, 0) == 0, info, c)


def normed(tok, gain, out):
    g = gain[...].astype(F32)
    for b in range(CH // 32):
        r = slice(b * 32, (b + 1) * 32)
        out[r, :] = (rms(tok[r, :].astype(F32), 1e-5) * g).astype(BF)


def project_kernel(owner, slot, tok0, tok1, tok2, gain, wq, wk, wv, row, q_out, kv_out, ku_out, min_out, pay_out, cr_out, cc_out, sent, st, misc, buf, n0, n1, codes, sem):
    i = pl.program_id(0)
    here = CH // PAGE
    last_sem = 2 * here

    @pl.when(i == 0)
    def _():
        st[...] = jnp.zeros_like(st)
        misc[...] = jnp.full_like(misc, -1.0)
        misc[0:2, :] = jnp.zeros((2, 128), F32)
        codes[...] = jnp.zeros_like(codes)
        for p in range(owner.shape[0]):
            codes[owner[p]] = jnp.broadcast_to((slot[p] + 1).astype(F32), codes.shape[1:]).astype(BF)
        pltpu.make_async_copy(codes, sent.at[:, pl.ds(PAGE, 8), :], sem.at[last_sem]).start()
        normed(tok0, gain, n0)

    copies = []
    for j, (now, tok, later) in enumerate(((n0, tok1, n1), (n1, tok2, n0))):
        r = slice(j * CH, (j + 1) * CH)
        n = now[...]
        k = dot(n, wk[...]).astype(BF)
        v = dot(n, wv[...]).astype(BF)
        q_out[r, :] = dot(n, wq[...]).astype(BF)
        for h in range(2):
            s = slice(h * HD, (h + 1) * HD)
            kv_out[r, 2 * h * HD : (2 * h + 1) * HD] = k[:, s]
            kv_out[r, (2 * h + 1) * HD : (2 * h + 2) * HD] = v[:, s]
            for p in range(here):
                w = slice(p * PAGE, (p + 1) * PAGE)
                buf[j * here + p, :, 2 * h * HD : (2 * h + 1) * HD] = k[w, s]
                buf[j * here + p, :, (2 * h + 1) * HD : (2 * h + 2) * HD] = v[w, s]
        for p in range(here):
            m = j * here + p
            c = pltpu.make_async_copy(buf.at[m], sent.at[owner[i * 2 * here + m], pl.ds(0, PAGE), :], sem.at[m])
            c.start()
            copies.append(c)
        normed(tok, gain, later)
        cr = running(row[:, r])
        cc = cr.T
        cr_out[:, r] = cr
        cc_out[r, :] = cc
        last = cr[0:1, CH - 1 : CH]
        same = (cc[:, 0:1] == last).astype(F32)
        last_row = jnp.broadcast_to(last, (1, 128))
        cont = (last_row == misc[2:3, :]).astype(F32)
        for h in range(2):
            s = slice(h * HD, (h + 1) * HD)
            ku = rms(k[:, s].astype(F32), 1e-6) * (1.0 / math.sqrt(HD))
            ku_out[r, s] = ku.astype(BF)
            end_h = cr[1 + h : 2 + h, CH - 1 : CH]
            w = jnp.exp(end_h - cc[:, 1 + h : 2 + h]) * same
            add = dot_l((ku * w).astype(BF), v[:, s])
            end_row = jnp.broadcast_to(end_h, (1, 128))
            old = st[h]
            min_out[j, h] = old
            st[h] = old * (jnp.exp(end_row) * cont) + add
            misc[h : h + 1, :] = misc[h : h + 1, :] + end_row
        misc[2:3, :] = last_row

    @pl.when(i == pl.num_programs(0) - 1)
    def _():
        write_payload(pay_out, st, misc[0:1, :], misc[1:2, :], misc[2:3, :])
        pltpu.make_async_copy(codes, sent.at[:, pl.ds(PAGE, 8), :], sem.at[last_sem]).wait()

    for c in copies:
        c.wait()


def write_payload(out, st, l0, l1, last):
    hi = jnp.floor(last * (1.0 / 256.0))
    rows = [*split3(l0), *split3(l1), hi, last - hi * 256.0]
    tail = jnp.concatenate(rows, axis=0).astype(BF)
    for i in range(out.shape[0]):
        for h in range(2):
            out[i, h * HD : (h + 1) * HD, :] = st[h].astype(BF)
        out[i, 2 * HD : 2 * HD + 8, :] = tail


def read_payload(ref, j):
    s = ref[j, 2 * HD : 2 * HD + 8, :].astype(F32)
    l0 = s[0:1] + s[1:2] + s[2:3]
    l1 = s[3:4] + s[4:5] + s[5:6]
    return l0, l1, s[6:7] * 256.0 + s[7:8]


def project(owner, slot, tokens, gain, wq, wk, wv, row, reqs):
    t, d = tokens.shape
    tile = 512
    n = t // tile
    c = tile // CH
    full = lambda a: pl.BlockSpec(a.shape, lambda i, o, l: (0,) * a.ndim)
    rows = lambda w: pl.BlockSpec((tile, w), lambda i, o, l: (i, 0))
    lanes = pl.BlockSpec((8, tile), lambda i, o, l: (0, i))
    gs = pltpu.PrefetchScalarGridSpec(
        num_scalar_prefetch=2,
        grid=(n,),
        in_specs=[
            pl.BlockSpec((CH, d), lambda i, o, l: (0, 0)),
            pl.BlockSpec((CH, d), lambda i, o, l: (2 * i + 1, 0)),
            pl.BlockSpec((CH, d), lambda i, o, l: (jnp.minimum(2 * i + 2, 2 * n - 1), 0)),
            full(gain), full(wq), full(wk), full(wv), lanes,
        ],
        out_specs=[
            rows(256),
            rows(512),
            rows(256),
            pl.BlockSpec((c, 2, HD, HD), lambda i, o, l: (i, 0, 0, 0)),
            pl.BlockSpec((8, 264, 128), lambda i, o, l: (0, 0, 0)),
            lanes,
            rows(8),
            pl.BlockSpec(memory_space=ANY),
        ],
        scratch_shapes=[
            pltpu.VMEM((2, HD, HD), F32),
            pltpu.VMEM((8, 128), F32),
            pltpu.VMEM((tile // PAGE, PAGE, 512), BF),
            pltpu.VMEM((CH, d), BF),
            pltpu.VMEM((CH, d), BF),
            pltpu.VMEM((reqs, 8, 512), BF),
            pltpu.SemaphoreType.DMA((tile // PAGE + 1,)),
        ],
    )
    return pl.pallas_call(
        project_kernel,
        grid_spec=gs,
        out_shape=[
            jax.ShapeDtypeStruct((t, 256), BF),
            jax.ShapeDtypeStruct((t, 512), BF),
            jax.ShapeDtypeStruct((t, 256), BF),
            jax.ShapeDtypeStruct((t // CH, 2, HD, HD), F32),
            jax.ShapeDtypeStruct((8, 264, 128), BF),
            jax.ShapeDtypeStruct((8, t), F32),
            jax.ShapeDtypeStruct((t, 8), F32),
            jax.ShapeDtypeStruct((reqs, PAGE + 8, 512), BF),
        ],
        name="project",
    )(owner, slot, tokens, tokens, tokens, gain, wq, wk, wv, row)


def combine_kernel(place, got, e_out, info_out, pay_out, st):
    g = place[0]
    st[...] = jnp.zeros_like(st)
    e_out[...] = jnp.zeros_like(e_out)
    cur = jnp.full((1, 128), -1.0, F32)
    t0 = t1 = jnp.zeros((1, 128), F32)
    i0, i1, il = t0, t1, cur
    for j in range(8):
        @pl.when(g == j)
        def _():
            e_out[...] = st[...]

        here = g == j
        i0, i1, il = jnp.where(here, t0, i0), jnp.where(here, t1, i1), jnp.where(here, cur, il)
        l0, l1, last = read_payload(got, j)
        cont = (cur == last).astype(F32)
        for h, l in ((0, l0), (1, l1)):
            st[h] = st[h] * (jnp.exp(l) * cont) + got[j, h * HD : (h + 1) * HD, :].astype(F32)
        t0, t1, cur = t0 + l0, t1 + l1, last
    info_out[...] = jnp.concatenate([i0, i1, il, jnp.zeros((5, 128), F32)], axis=0)
    write_payload(pay_out, st, t0, t1, cur)


def combine(place, got):
    vm = pl.BlockSpec(memory_space=pltpu.VMEM)
    return pl.pallas_call(
        combine_kernel,
        in_specs=[pl.BlockSpec(memory_space=pltpu.SMEM), vm],
        out_specs=[vm, vm, vm],
        out_shape=[
            jax.ShapeDtypeStruct((2, HD, HD), F32),
            jax.ShapeDtypeStruct((8, 128), F32),
            jax.ShapeDtypeStruct((4, 264, 128), BF),
        ],
        scratch_shapes=[pltpu.VMEM((2, HD, HD), F32)],
        name="combine",
    )(place, got)


def attend_kernel(q, k, v, pk, pv, col, row, out):
    scale = 1.0 / math.sqrt(HD)
    c = scale * math.log2(math.e)
    mask = tri(CH)
    for i in range(SEG // CH):
        r = slice(i * CH, (i + 1) * CH)
        qi = q[r, :]
        doc = col[r, 0:1]
        sp = dot_t(qi, pk[...])
        sd = dot_t(qi, k[r, :])
        sd = jnp.where(mask & (doc == row[0:1, r]), sd, -1e30)
        m = jnp.maximum(jnp.max(sp, axis=-1, keepdims=True), jnp.max(sd, axis=-1, keepdims=True))
        if i:
            e = slice(0, i * CH)
            so = dot_t(qi, k[e, :])
            so = jnp.where(doc == row[0:1, e], so, -1e30)
            m = jnp.maximum(m, jnp.max(so, axis=-1, keepdims=True))
        wp = jnp.exp2((sp - m) * c)
        wd = jnp.exp2((sd - m) * c)
        total = jnp.sum(wp, axis=-1, keepdims=True) + jnp.sum(wd, axis=-1, keepdims=True)
        acc = dot(wp.astype(BF), pv[...]) + dot(wd.astype(BF), v[r, :])
        if i:
            wo = jnp.exp2((so - m) * c)
            total = total + jnp.sum(wo, axis=-1, keepdims=True)
            acc = acc + dot(wo.astype(BF), v[e, :])
        out[r, :] = acc / total


def attend(q, kv, pk, pv, col, row, seg, h0=0, heads=2):
    return pl.pallas_call(
        attend_kernel,
        grid=(heads,),
        in_specs=[
            pl.BlockSpec((SEG, HD), lambda h: (seg, h + h0)),
            pl.BlockSpec((SEG, HD), lambda h: (seg, 2 * (h + h0))),
            pl.BlockSpec((SEG, HD), lambda h: (seg, 2 * (h + h0) + 1)),
            pl.BlockSpec((16, HD), lambda h: (0, h + h0)),
            pl.BlockSpec((16, HD), lambda h: (0, h + h0)),
            pl.BlockSpec((SEG, 8), lambda h: (seg, 0)),
            pl.BlockSpec((8, SEG), lambda h: (0, seg)),
        ],
        out_specs=pl.BlockSpec((SEG, HD), lambda h: (0, h)),
        out_shape=jax.ShapeDtypeStruct((SEG, heads * HD), F32),
        name="attend",
        cost_estimate=pl.CostEstimate(flops=700_000_000 * heads, transcendentals=0, bytes_accessed=2_000_000 * heads),
    )(q, kv, kv, pk, pv, col, row)


def recall_kernel(half, place, bound, q, ku, kv, mi, e1, info, got, col, row, rows, at0, at1, gain, o0, o1, o2, o3, pst, pdoc):
    b = pl.program_id(0)
    chunk = 2 * b + half

    @pl.when(b == 0)
    def _():
        x, g = place[1], place[0]
        st = [jnp.zeros((HD, HD), F32)] * 2
        cur = jnp.full((1, 128), -1.0, F32)
        pst[...] = jnp.zeros_like(pst)
        il = cur
        for j in range(4):
            here = x == j
            il = jnp.where(here, cur, il)
            for h in range(2):
                pst[h] = jnp.where(here, st[h], pst[h])
            l0, l1, last = read_payload(got, j)
            cont = (cur == last).astype(F32)
            for h, l in ((0, l0), (1, l1)):
                st[h] = st[h] * (jnp.exp(l) * cont) + got[j, h * HD : (h + 1) * HD, :].astype(F32)
            cur = last
        glast = info[2:3, :]
        first = g == 0
        ok = jnp.where(first, 1.0, (il == glast).astype(F32))
        for h in range(2):
            pst[h] = pst[h] * (jnp.exp(info[h : h + 1, :]) * ok) + e1[h]
        pdoc[0:1, :] = jnp.where(first, il, glast)

    mask = tri(CH)
    pos = lax.broadcasted_iota(jnp.int32, rows.shape, 1)
    ends = (pos < chunk * CH) & (lax.rem(pos, CH) == CH - 1)
    pre = jnp.sum(jnp.where(ends, rows[...], 0.0), axis=1, keepdims=True)
    doc = col[:, 0:1]
    pdoc_row = pdoc[0:1, :]
    carried = jnp.where(chunk == 0, pdoc_row, bound[chunk])
    joined = (carried == pdoc_row).astype(F32)
    live = (doc == carried[:, 0:1]).astype(F32)
    ok = mask & (doc == row[0:1, :])
    for h in range(2):
        s = slice(h * HD, (h + 1) * HD)
        qh = q[:, s]
        cc = col[:, 1 + h : 2 + h]
        dec = jnp.exp(jnp.where(ok, cc - row[1 + h : 2 + h, :], -1e30))
        inner = (dot_t(qh, ku[:, s]) * dec).astype(BF)
        rec = dot(inner, kv[:, (2 * h + 1) * HD : (2 * h + 2) * HD])
        f = jnp.exp(jnp.broadcast_to(pre[1 + h : 2 + h, :], (1, 128))) * joined
        m = mi[0, h] + pst[h] * f
        rec = rec + dot(qh, m.astype(BF)) * (jnp.exp(cc) * live)
        qw = qh.astype(F32)
        rec = rec * (lax.rsqrt(jnp.mean(qw * qw, axis=-1, keepdims=True) + 1e-6) * (1.0 / math.sqrt(HD)))
        at = jnp.where(chunk < SEG // CH, at0[:, s], at1[:, s])
        val = (at + rms(rec, 1e-5) * gain[:, s]).astype(BF)
        for d, out in enumerate((o0, o1, o2, o3)):
            @pl.when(lax.rem(b - place[2] + 4, 4) == d)
            def _():
                out[:, s] = val


def recall(half, place, bound, q, ku, kv, mi, e1, info, got, col, row, at0, at1, gain):
    ch = lambda w: pl.BlockSpec((CH, w), lambda b, p, d: (2 * b + half, 0))
    full = lambda a: pl.BlockSpec(a.shape, lambda b, p, d: (0,) * a.ndim)
    per = SEG // CH
    gs = pltpu.PrefetchScalarGridSpec(
        num_scalar_prefetch=2,
        grid=(4,),
        in_specs=[
            ch(256),
            ch(256),
            ch(512),
            pl.BlockSpec((1, 2, HD, HD), lambda b, p, d: (2 * b + half, 0, 0, 0)),
            full(e1),
            full(info),
            full(got),
            ch(8),
            pl.BlockSpec((8, CH), lambda b, p, d: (0, 2 * b + half)),
            full(row),
            pl.BlockSpec((CH, 256), lambda b, p, d: (jnp.minimum(2 * b + half, per - 1), 0)),
            pl.BlockSpec((CH, 256), lambda b, p, d: (jnp.maximum(2 * b + half - per, 0), 0)),
            full(gain),
        ],
        out_specs=[pl.BlockSpec((CH, 256), lambda b, p, d: (0, 0))] * 4,
        scratch_shapes=[pltpu.VMEM((2, HD, HD), F32), pltpu.VMEM((8, 128), F32)],
    )
    return pl.pallas_call(
        functools.partial(recall_kernel, half),
        grid_spec=gs,
        out_shape=[jax.ShapeDtypeStruct((CH, 256), BF)] * 4,
        name="recall",
        cost_estimate=pl.CostEstimate(flops=400_000_000, transcendentals=0, bytes_accessed=4_000_000),
    )(place, bound, q, ku, kv, mi, e1, info, got, col, row, row, at0, at1, gain)


def ffn_kernel(half, place, gain, tokens, *rest):
    y = place[2]
    heads, own = rest[0:4], rest[4:8]
    sets = (rest[8:14], rest[14:20])
    out, tok, hv, wgu, wd, wo, norm, acc, sem = rest[20:]
    core = place[3]
    count = [0]
    waits = {}

    def copy(key, src, dst):
        c = pltpu.make_async_copy(src, dst, sem.at[count[0]])
        count[0] += 1
        waits.setdefault(key, []).append(c)
        c.start()

    def fetch(kind, i):
        key = (kind, i)
        if i == 0:
            if kind == "out":
                copy(key, own[3], wo.at[0])
            elif kind == "up":
                copy(key, own[0], wgu.at[0, 0])
                copy(key, own[1], wgu.at[1, 0])
            else:
                copy(key, own[2], wd.at[0])
            return
        for which in range(2):
            at = core if which == 0 else 1 - core
            p, q = sets[which][2 * i - 2], sets[which][2 * i - 1]
            if kind == "up":
                copy(key, p.at[pl.ds(0, 352), :], wgu.at[0, i, pl.ds(at * 352, 352), :])
                copy(key, p.at[pl.ds(352, 240), :], wgu.at[1, i, pl.ds(at * 352, 240), :])
                copy(key, q.at[pl.ds(0, 112), :], wgu.at[1, i, pl.ds(at * 352 + 240, 112), :])
            elif kind == "down":
                copy(key, q.at[pl.ds(112, 352), :], wd.at[i, pl.ds(at * 352, 352), :])
            else:
                copy(key, q.at[pl.ds(464, 128), :], wo.at[i, pl.ds(at * 128, 128), :])

    def ready(kind, group):
        for c in waits[(kind, group)]:
            c.wait()

    copy(("in", 0), tokens.at[pl.ds((2 * y + half) * ROWS, ROWS), :], tok)
    for i in range(4):
        copy(("in", 0), heads[i], hv.at[i])
    for i in range(4):
        fetch("out", i)
    fetch("up", 0)
    fetch("down", 0)
    ready("in", 0)
    total = tok[...].astype(F32)
    for i in range(4):
        ready("out", i)
        total = total + dot(hv[i], wo[i])
    for i in (1, 2, 3):
        fetch("up", i)
        fetch("down", i)
    resid = total.astype(BF).astype(F32)
    acc[...] = resid
    norm[...] = (rms(resid, 1e-5) * gain[...].astype(F32)).astype(BF)

    def step(i, carry):
        for index in range(4):
            @pl.when(i == index)
            def _():
                ready("up", index)
                ready("down", index)

        n = norm[...]
        g = dot_t(n, wgu[0, i])
        u = dot_t(n, wgu[1, i])
        hid = (g / (1.0 + jnp.exp(-g)) * u).astype(BF)
        acc[...] += dot(hid, wd[i])
        return carry

    lax.fori_loop(0, 4, step, 0)
    out[...] = acc[...].astype(BF)


def ffn(half, place, tokens, gain, heads, own, mine, other):
    d = tokens.shape[1]
    full = lambda a: pl.BlockSpec(a.shape, lambda i, p: (0,) * a.ndim)
    anys = pl.BlockSpec(memory_space=ANY)
    ws = [*own, *mine, *other]
    gs = pltpu.PrefetchScalarGridSpec(
        num_scalar_prefetch=1,
        grid=(1,),
        in_specs=[full(gain)] + [anys] * (1 + len(heads) + len(ws)),
        out_specs=pl.BlockSpec((ROWS, d), lambda i, p: (0, 0)),
        scratch_shapes=[
            pltpu.VMEM((ROWS, d), BF),
            pltpu.VMEM((4, ROWS, 256), BF),
            pltpu.VMEM((2, 4, 704, 1024), BF),
            pltpu.VMEM((4, 704, 1024), BF),
            pltpu.VMEM((4, 256, 1024), BF),
            pltpu.VMEM((ROWS, d), BF),
            pltpu.VMEM((ROWS, d), F32),
            pltpu.SemaphoreType.DMA((39,)),
        ],
    )
    return pl.pallas_call(
        functools.partial(ffn_kernel, half),
        grid_spec=gs,
        out_shape=jax.ShapeDtypeStruct((ROWS, d), BF),
        name="ffn",
    )(place, gain, tokens, *heads, *ws)


def staged(ins, bufs, outs, sem):
    n = len(ins)
    first = [pltpu.make_async_copy(ins[i], bufs[i], sem.at[i]) for i in range(n)]
    second = [pltpu.make_async_copy(bufs[i], outs[i], sem.at[n + i]) for i in range(n)]
    for c in first:
        c.start()
    for a, b in zip(first, second):
        a.wait()
        b.start()
    for c in second:
        c.wait()


def place_kernel(source, got, out, buf, sem):
    n = out.shape[0]
    staged(
        [got.at[source[s], pl.ds(0, PAGE), :] for s in range(n)],
        [buf.at[s] for s in range(n)],
        [out.at[s] for s in range(n)],
        sem,
    )


def place_pages(source, got, count):
    anys = pl.BlockSpec(memory_space=ANY)
    shape = (count, PAGE, got.shape[2])
    return pl.pallas_call(
        place_kernel,
        in_specs=[pl.BlockSpec(memory_space=pltpu.SMEM), anys],
        out_specs=anys,
        out_shape=jax.ShapeDtypeStruct(shape, BF),
        scratch_shapes=[pltpu.VMEM(shape, BF), pltpu.SemaphoreType.DMA((2 * count,))],
        name="place",
    )(source, got)


def join_kernel(spots, place, *refs):
    pieces, out, bufs, sem = refs[: len(spots)], refs[-2 - len(spots)], refs[-1 - len(spots) : -1], refs[-1]
    y = place[2]
    outs = []
    for d, row, n in spots:
        outs.append(out.at[pl.ds(lax.rem(y + d, 4) * (2 * ROWS) + row, n), :])
    staged(pieces, bufs, outs, sem)


def join(place, pieces, spots, into=None):
    anys = pl.BlockSpec(memory_space=ANY)
    rest = [] if into is None else [into]
    width = pieces[0].shape[1]
    return pl.pallas_call(
        functools.partial(join_kernel, spots),
        in_specs=[pl.BlockSpec(memory_space=pltpu.SMEM)] + [anys] * (len(pieces) + len(rest)),
        out_specs=anys,
        out_shape=jax.ShapeDtypeStruct((8 * ROWS, width), BF),
        scratch_shapes=[pltpu.VMEM(p.shape, BF) for p in pieces] + [pltpu.SemaphoreType.DMA((2 * len(pieces),))],
        input_output_aliases={} if into is None else {1 + len(pieces): 0},
        name="join",
    )(place, *pieces, *rest)


def cut_kernel(place, gate, up, down, last, p, q, sem):
    core = place[3]
    copies = [
        pltpu.make_async_copy(gate.at[pl.ds(core * 352, 352), :], p.at[pl.ds(0, 352), :], sem.at[0]),
        pltpu.make_async_copy(up.at[pl.ds(core * 352, 240), :], p.at[pl.ds(352, 240), :], sem.at[1]),
        pltpu.make_async_copy(up.at[pl.ds(core * 352 + 240, 112), :], q.at[pl.ds(0, 112), :], sem.at[2]),
        pltpu.make_async_copy(down.at[pl.ds(core * 352, 352), :], q.at[pl.ds(112, 352), :], sem.at[3]),
        pltpu.make_async_copy(last.at[pl.ds(core * 128, 128), :], q.at[pl.ds(464, 128), :], sem.at[4]),
    ]
    for c in copies:
        c.start()
    for c in copies:
        c.wait()


def cut_weights(place, gate, up, down, last):
    anys = pl.BlockSpec(memory_space=ANY)
    vm = pl.BlockSpec(memory_space=pltpu.VMEM)
    shape = jax.ShapeDtypeStruct((592, gate.shape[1]), BF)
    return pl.pallas_call(
        cut_kernel,
        in_specs=[pl.BlockSpec(memory_space=pltpu.SMEM)] + [anys] * 4,
        out_specs=[vm, vm],
        out_shape=[shape, shape],
        scratch_shapes=[pltpu.SemaphoreType.DMA((5,))],
        name="cut_weights",
    )(place, gate, up, down, last)


def on_device(
    tokens, attn_gain, w_query, w_key, w_value, persist_key, persist_value, log_forget, mem_gain,
    w_out, ffn_gain, w_gate, w_up, w_down, doc_ids, page_owner, page_slot,
):
    count = tokens.shape[0]
    reqs = lax.axis_size("req")
    req, y = lax.axis_index("req"), lax.axis_index("tp")
    core, x, z = req % 2, req // 8, (req // 2) % 4
    place = jnp.stack([req % 8, x, y, core, z]).astype(jnp.int32)
    shift = lambda a, d: lax.ppermute(a, "tp", [(i, (i + d) % 4) for i in range(4)])
    swap = lambda a: lax.ppermute(a, "req", [(i, i ^ 1) for i in range(reqs)])
    tie = lambda *a: lax.optimization_barrier(a)

    gate, up = w_gate.T, w_up.T
    p, qq = cut_weights(place, gate, up, w_down, w_out)
    p1, q3, q1w, p3 = shift(p, 1), shift(qq, -1), shift(qq, 1), shift(p, -1)

    doc = doc_ids.astype(F32)
    row = jnp.concatenate([doc[None], log_forget.T, jnp.zeros((5, count), F32)])
    bound = jnp.concatenate([jnp.full((1,), -1.0, F32), doc[CH - 1 : -1 : CH]])

    q, kv, ku, mi, pay, row, col, outgoing = project(
        page_owner, page_slot, tokens, attn_gain[None], w_query, w_key, w_value, row, reqs
    )

    group8 = [[i * 8 + k for k in range(8)] for i in range(reqs // 8)]
    group4 = [[i * 8 + k for i in range(reqs // 8)] for k in range(8)]
    spread = lambda a, g: lax.all_to_all(a, "req", 0, 0, tiled=True, axis_index_groups=g)
    got8 = spread(pay, group8)

    at0 = attend(q, kv, persist_key, persist_value, col, row, 0)
    at0, got8 = tie(at0, got8)
    e1, info, pay4 = combine(place, got8)
    got4 = spread(pay4, group4)
    q1, at0, _ = tie(q, at0, pay4)
    at1 = attend(q1, kv, persist_key, persist_value, col, row, 1)
    at1, got4, outgoing = tie(at1, got4, outgoing)
    arrived = lax.all_to_all(outgoing, "req", 0, 0, tiled=True)
    at1, p1, q3, q1w, p3 = tie(at1, p1, q3, q1w, p3)
    p2, q2 = shift(p1, 1), shift(q3, -1)

    gain = mem_gain[None]
    own_w = (gate, up, w_down, w_out)
    mem = lambda half: recall(half, place, bound, q, ku, kv, mi, e1, info, got4, col, row, at0, at1, gain)
    send = lambda out: [out[0]] + [shift(out[d], d) for d in (1, 3, 2)]
    p1x, q3x, q1x, p3x = swap(p1), swap(q3), swap(q1w), swap(p3)
    out0 = mem(0)
    tied = tie(*out0, p1x, q3x, q1x, p3x)
    out0, (p1x, q3x, q1x, p3x) = tied[:4], tied[4:]
    heads0 = send(out0)
    out1 = mem(1)
    tied = tie(*out1, *heads0)
    out1, heads0 = tied[:4], tied[4:]
    heads1 = send(out1)
    p2, q2, _ = tie(p2, q2, out1[0])
    p2x, q2x = swap(p2), swap(q2)
    mine, other = [p1, q1w, p3, q3, p2, q2], [p1x, q1x, p3x, q3x, p2x, q2x]

    slots = arrived[:, PAGE, 0].astype(F32)
    wanted = slots[None, :] == (jnp.arange(count // PAGE) + 1).astype(F32)[:, None]
    source = jnp.sum(jnp.where(wanted, jnp.arange(reqs)[None, :], 0), axis=1).astype(jnp.int32)
    kv_cache = place_pages(jnp.clip(source, 0, reqs - 1), arrived, count // PAGE)

    feed = lambda half, heads: ffn(
        half, place, tokens, ffn_gain[None], heads, own_w, mine, other
    )
    R, H = ROWS, ROWS // 2
    own0 = feed(0, heads0)
    own0, *heads1 = tie(own0, *heads1)
    a0, b0 = shift(own0, 1), shift(own0, -1)
    own1 = feed(1, heads1)
    a1, b1 = shift(own1, 1), shift(own1, -1)
    lo0, hi0 = shift(a0[:H], 1), shift(b0[H:], -1)
    joined = join(place, [own0, a0, b0, own1], ((0, 0, R), (3, 0, R), (1, 0, R), (0, R, R)))
    a1, b1, joined, kv_cache = tie(a1, b1, joined, kv_cache)
    lo1, hi1 = shift(a1[:H], 1), shift(b1[H:], -1)
    joined = join(place, [a1, b1, lo0, hi0], ((3, R, R), (1, R, R), (2, 0, H), (2, H, H)), joined)
    lo1, hi1, joined = tie(lo1, hi1, joined)
    layer_out = join(place, [lo1, hi1], ((2, R, H), (2, R + H, H)), joined)
    return layer_out, kv_cache


def solution(mesh):
    return jax.shard_map(
        on_device,
        mesh=mesh,
        in_specs=(
            P("req", None), P(), P(None, "tp"), P(None, "tp"), P(None, "tp"), P(None, "tp"), P(None, "tp"),
            P("req", "tp"), P("tp"), P("tp", None), P(), P(None, "tp"), P(None, "tp"), P("tp", None),
            P("req"), P("req"), P("req"),
        ),
        out_specs=(P("req", None), P("req", None, "tp")),
        check_vma=False,
    )
```

```python
import functools
import math

import jax
import jax.numpy as jnp
from jax import lax
from jax.experimental import pallas as pl
from jax.experimental.pallas import tpu as pltpu
from jax.sharding import PartitionSpec as P

HD = 128
SEG = 1024
PAGE = 128
CH = 256
ROWS = 256
F32 = jnp.float32
BF = jnp.bfloat16
ANY = pl.ANY


def rms(x, eps):
    return x * lax.rsqrt(jnp.mean(x * x, axis=-1, keepdims=True) + eps)


def dot(a, b):
    return jnp.dot(a, b, preferred_element_type=F32)


def dot_t(a, b):
    return lax.dot_general(a, b, (((1,), (1,)), ((), ())), preferred_element_type=F32)


def dot_l(a, b):
    return lax.dot_general(a, b, (((0,), (0,)), ((), ())), preferred_element_type=F32)


def tri(n, lower=True):
    r = lax.broadcasted_iota(jnp.int32, (n, n), 0)
    c = lax.broadcasted_iota(jnp.int32, (n, n), 1)
    return (r >= c) if lower else (r <= c)


def split3(x):
    hi = x.astype(BF).astype(F32)
    mid = (x - hi).astype(BF).astype(F32)
    return hi, mid, x - hi - mid


def running(info):
    parts = jnp.concatenate(split3(info), axis=0).astype(BF)
    c = dot(parts, tri(info.shape[1], False).astype(F32).astype(BF))
    c = c[0:8] + c[8:16] + c[16:24]
    return jnp.where(lax.broadcasted_iota(jnp.int32, info.shape, 0) == 0, info, c)


def normed(tok, gain, out):
    g = gain[...].astype(F32)
    for b in range(CH // 32):
        r = slice(b * 32, (b + 1) * 32)
        out[r, :] = (rms(tok[r, :].astype(F32), 1e-5) * g).astype(BF)


def project_kernel(owner, slot, tok0, tok1, tok2, gain, wq, wk, wv, row, q_out, kv_out, ku_out, min_out, pay_out, cr_out, cc_out, sent, st, misc, buf, n0, n1, codes, sem):
    i = pl.program_id(0)
    here = CH // PAGE
    last_sem = 2 * here

    @pl.when(i == 0)
    def _():
        st[...] = jnp.zeros_like(st)
        misc[...] = jnp.full_like(misc, -1.0)
        misc[0:2, :] = jnp.zeros((2, 128), F32)
        codes[...] = jnp.zeros_like(codes)
        for p in range(owner.shape[0]):
            codes[owner[p]] = jnp.broadcast_to((slot[p] + 1).astype(F32), codes.shape[1:]).astype(BF)
        pltpu.make_async_copy(codes, sent.at[:, pl.ds(PAGE, 8), :], sem.at[last_sem]).start()
        normed(tok0, gain, n0)

    copies = []
    for j, (now, tok, later) in enumerate(((n0, tok1, n1), (n1, tok2, n0))):
        r = slice(j * CH, (j + 1) * CH)
        n = now[...]
        k = dot(n, wk[...]).astype(BF)
        v = dot(n, wv[...]).astype(BF)
        q_out[r, :] = dot(n, wq[...]).astype(BF)
        for h in range(2):
            s = slice(h * HD, (h + 1) * HD)
            kv_out[r, 2 * h * HD : (2 * h + 1) * HD] = k[:, s]
            kv_out[r, (2 * h + 1) * HD : (2 * h + 2) * HD] = v[:, s]
            for p in range(here):
                w = slice(p * PAGE, (p + 1) * PAGE)
                buf[j * here + p, :, 2 * h * HD : (2 * h + 1) * HD] = k[w, s]
                buf[j * here + p, :, (2 * h + 1) * HD : (2 * h + 2) * HD] = v[w, s]
        for p in range(here):
            m = j * here + p
            c = pltpu.make_async_copy(buf.at[m], sent.at[owner[i * 2 * here + m], pl.ds(0, PAGE), :], sem.at[m])
            c.start()
            copies.append(c)
        normed(tok, gain, later)
        cr = running(row[:, r])
        cc = cr.T
        cr_out[:, r] = cr
        cc_out[r, :] = cc
        last = cr[0:1, CH - 1 : CH]
        same = (cc[:, 0:1] == last).astype(F32)
        last_row = jnp.broadcast_to(last, (1, 128))
        cont = (last_row == misc[2:3, :]).astype(F32)
        for h in range(2):
            s = slice(h * HD, (h + 1) * HD)
            ku = rms(k[:, s].astype(F32), 1e-6) * (1.0 / math.sqrt(HD))
            ku_out[r, s] = ku.astype(BF)
            end_h = cr[1 + h : 2 + h, CH - 1 : CH]
            w = jnp.exp(end_h - cc[:, 1 + h : 2 + h]) * same
            add = dot_l((ku * w).astype(BF), v[:, s])
            end_row = jnp.broadcast_to(end_h, (1, 128))
            old = st[h]
            min_out[j, h] = old
            st[h] = old * (jnp.exp(end_row) * cont) + add
            misc[h : h + 1, :] = misc[h : h + 1, :] + end_row
        misc[2:3, :] = last_row

    @pl.when(i == pl.num_programs(0) - 1)
    def _():
        write_payload(pay_out, st, misc[0:1, :], misc[1:2, :], misc[2:3, :])
        pltpu.make_async_copy(codes, sent.at[:, pl.ds(PAGE, 8), :], sem.at[last_sem]).wait()

    for c in copies:
        c.wait()


def write_payload(out, st, l0, l1, last):
    hi = jnp.floor(last * (1.0 / 256.0))
    rows = [*split3(l0), *split3(l1), hi, last - hi * 256.0]
    tail = jnp.concatenate(rows, axis=0).astype(BF)
    for i in range(out.shape[0]):
        for h in range(2):
            out[i, h * HD : (h + 1) * HD, :] = st[h].astype(BF)
        out[i, 2 * HD : 2 * HD + 8, :] = tail


def read_payload(ref, j):
    s = ref[j, 2 * HD : 2 * HD + 8, :].astype(F32)
    l0 = s[0:1] + s[1:2] + s[2:3]
    l1 = s[3:4] + s[4:5] + s[5:6]
    return l0, l1, s[6:7] * 256.0 + s[7:8]


def project(owner, slot, tokens, gain, wq, wk, wv, row, reqs):
    t, d = tokens.shape
    tile = 512
    n = t // tile
    c = tile // CH
    full = lambda a: pl.BlockSpec(a.shape, lambda i, o, l: (0,) * a.ndim)
    rows = lambda w: pl.BlockSpec((tile, w), lambda i, o, l: (i, 0))
    lanes = pl.BlockSpec((8, tile), lambda i, o, l: (0, i))
    gs = pltpu.PrefetchScalarGridSpec(
        num_scalar_prefetch=2,
        grid=(n,),
        in_specs=[
            pl.BlockSpec((CH, d), lambda i, o, l: (0, 0)),
            pl.BlockSpec((CH, d), lambda i, o, l: (2 * i + 1, 0)),
            pl.BlockSpec((CH, d), lambda i, o, l: (jnp.minimum(2 * i + 2, 2 * n - 1), 0)),
            full(gain), full(wq), full(wk), full(wv), lanes,
        ],
        out_specs=[
            rows(256),
            rows(512),
            rows(256),
            pl.BlockSpec((c, 2, HD, HD), lambda i, o, l: (i, 0, 0, 0)),
            pl.BlockSpec((8, 264, 128), lambda i, o, l: (0, 0, 0)),
            lanes,
            rows(8),
            pl.BlockSpec(memory_space=ANY),
        ],
        scratch_shapes=[
            pltpu.VMEM((2, HD, HD), F32),
            pltpu.VMEM((8, 128), F32),
            pltpu.VMEM((tile // PAGE, PAGE, 512), BF),
            pltpu.VMEM((CH, d), BF),
            pltpu.VMEM((CH, d), BF),
            pltpu.VMEM((reqs, 8, 512), BF),
            pltpu.SemaphoreType.DMA((tile // PAGE + 1,)),
        ],
    )
    return pl.pallas_call(
        project_kernel,
        grid_spec=gs,
        out_shape=[
            jax.ShapeDtypeStruct((t, 256), BF),
            jax.ShapeDtypeStruct((t, 512), BF),
            jax.ShapeDtypeStruct((t, 256), BF),
            jax.ShapeDtypeStruct((t // CH, 2, HD, HD), F32),
            jax.ShapeDtypeStruct((8, 264, 128), BF),
            jax.ShapeDtypeStruct((8, t), F32),
            jax.ShapeDtypeStruct((t, 8), F32),
            jax.ShapeDtypeStruct((reqs, PAGE + 8, 512), BF),
        ],
        name="project",
    )(owner, slot, tokens, tokens, tokens, gain, wq, wk, wv, row)


def combine_kernel(place, got, e_out, info_out, pay_out, st):
    g = place[0]
    st[...] = jnp.zeros_like(st)
    e_out[...] = jnp.zeros_like(e_out)
    cur = jnp.full((1, 128), -1.0, F32)
    t0 = t1 = jnp.zeros((1, 128), F32)
    i0, i1, il = t0, t1, cur
    for j in range(8):
        @pl.when(g == j)
        def _():
            e_out[...] = st[...]

        here = g == j
        i0, i1, il = jnp.where(here, t0, i0), jnp.where(here, t1, i1), jnp.where(here, cur, il)
        l0, l1, last = read_payload(got, j)
        cont = (cur == last).astype(F32)
        for h, l in ((0, l0), (1, l1)):
            st[h] = st[h] * (jnp.exp(l) * cont) + got[j, h * HD : (h + 1) * HD, :].astype(F32)
        t0, t1, cur = t0 + l0, t1 + l1, last
    info_out[...] = jnp.concatenate([i0, i1, il, jnp.zeros((5, 128), F32)], axis=0)
    write_payload(pay_out, st, t0, t1, cur)


def combine(place, got):
    vm = pl.BlockSpec(memory_space=pltpu.VMEM)
    return pl.pallas_call(
        combine_kernel,
        in_specs=[pl.BlockSpec(memory_space=pltpu.SMEM), vm],
        out_specs=[vm, vm, vm],
        out_shape=[
            jax.ShapeDtypeStruct((2, HD, HD), F32),
            jax.ShapeDtypeStruct((8, 128), F32),
            jax.ShapeDtypeStruct((4, 264, 128), BF),
        ],
        scratch_shapes=[pltpu.VMEM((2, HD, HD), F32)],
        name="combine",
    )(place, got)


def attend_kernel(q, k, v, pk, pv, col, row, out):
    scale = 1.0 / math.sqrt(HD)
    c = scale * math.log2(math.e)
    mask = tri(CH)
    for i in range(SEG // CH):
        r = slice(i * CH, (i + 1) * CH)
        qi = q[r, :]
        doc = col[r, 0:1]
        sp = dot_t(qi, pk[...])
        sd = dot_t(qi, k[r, :])
        sd = jnp.where(mask & (doc == row[0:1, r]), sd, -1e30)
        m = jnp.maximum(jnp.max(sp, axis=-1, keepdims=True), jnp.max(sd, axis=-1, keepdims=True))
        if i:
            e = slice(0, i * CH)
            so = dot_t(qi, k[e, :])
            so = jnp.where(doc == row[0:1, e], so, -1e30)
            m = jnp.maximum(m, jnp.max(so, axis=-1, keepdims=True))
        wp = jnp.exp2((sp - m) * c)
        wd = jnp.exp2((sd - m) * c)
        total = jnp.sum(wp, axis=-1, keepdims=True) + jnp.sum(wd, axis=-1, keepdims=True)
        acc = dot(wp.astype(BF), pv[...]) + dot(wd.astype(BF), v[r, :])
        if i:
            wo = jnp.exp2((so - m) * c)
            total = total + jnp.sum(wo, axis=-1, keepdims=True)
            acc = acc + dot(wo.astype(BF), v[e, :])
        out[r, :] = acc / total


def attend(q, kv, pk, pv, col, row, seg, h0=0, heads=2):
    return pl.pallas_call(
        attend_kernel,
        grid=(heads,),
        in_specs=[
            pl.BlockSpec((SEG, HD), lambda h: (seg, h + h0)),
            pl.BlockSpec((SEG, HD), lambda h: (seg, 2 * (h + h0))),
            pl.BlockSpec((SEG, HD), lambda h: (seg, 2 * (h + h0) + 1)),
            pl.BlockSpec((16, HD), lambda h: (0, h + h0)),
            pl.BlockSpec((16, HD), lambda h: (0, h + h0)),
            pl.BlockSpec((SEG, 8), lambda h: (seg, 0)),
            pl.BlockSpec((8, SEG), lambda h: (0, seg)),
        ],
        out_specs=pl.BlockSpec((SEG, HD), lambda h: (0, h)),
        out_shape=jax.ShapeDtypeStruct((SEG, heads * HD), F32),
        name="attend",
        cost_estimate=pl.CostEstimate(flops=700_000_000 * heads, transcendentals=0, bytes_accessed=2_000_000 * heads),
    )(q, kv, kv, pk, pv, col, row)


def recall_kernel(half, place, bound, q, ku, kv, mi, e1, info, got, col, row, rows, at0, at1, gain, o0, o1, o2, o3, pst, pdoc):
    b = pl.program_id(0)
    chunk = 2 * b + half

    @pl.when(b == 0)
    def _():
        x, g = place[1], place[0]
        st = [jnp.zeros((HD, HD), F32)] * 2
        cur = jnp.full((1, 128), -1.0, F32)
        pst[...] = jnp.zeros_like(pst)
        il = cur
        for j in range(4):
            here = x == j
            il = jnp.where(here, cur, il)
            for h in range(2):
                pst[h] = jnp.where(here, st[h], pst[h])
            l0, l1, last = read_payload(got, j)
            cont = (cur == last).astype(F32)
            for h, l in ((0, l0), (1, l1)):
                st[h] = st[h] * (jnp.exp(l) * cont) + got[j, h * HD : (h + 1) * HD, :].astype(F32)
            cur = last
        glast = info[2:3, :]
        first = g == 0
        ok = jnp.where(first, 1.0, (il == glast).astype(F32))
        for h in range(2):
            pst[h] = pst[h] * (jnp.exp(info[h : h + 1, :]) * ok) + e1[h]
        pdoc[0:1, :] = jnp.where(first, il, glast)

    mask = tri(CH)
    pos = lax.broadcasted_iota(jnp.int32, rows.shape, 1)
    ends = (pos < chunk * CH) & (lax.rem(pos, CH) == CH - 1)
    pre = jnp.sum(jnp.where(ends, rows[...], 0.0), axis=1, keepdims=True)
    doc = col[:, 0:1]
    pdoc_row = pdoc[0:1, :]
    carried = jnp.where(chunk == 0, pdoc_row, bound[chunk])
    joined = (carried == pdoc_row).astype(F32)
    live = (doc == carried[:, 0:1]).astype(F32)
    ok = mask & (doc == row[0:1, :])
    for h in range(2):
        s = slice(h * HD, (h + 1) * HD)
        qh = q[:, s]
        cc = col[:, 1 + h : 2 + h]
        dec = jnp.exp(jnp.where(ok, cc - row[1 + h : 2 + h, :], -1e30))
        inner = (dot_t(qh, ku[:, s]) * dec).astype(BF)
        rec = dot(inner, kv[:, (2 * h + 1) * HD : (2 * h + 2) * HD])
        f = jnp.exp(jnp.broadcast_to(pre[1 + h : 2 + h, :], (1, 128))) * joined
        m = mi[0, h] + pst[h] * f
        rec = rec + dot(qh, m.astype(BF)) * (jnp.exp(cc) * live)
        qw = qh.astype(F32)
        rec = rec * (lax.rsqrt(jnp.mean(qw * qw, axis=-1, keepdims=True) + 1e-6) * (1.0 / math.sqrt(HD)))
        at = jnp.where(chunk < SEG // CH, at0[:, s], at1[:, s])
        val = (at + rms(rec, 1e-5) * gain[:, s]).astype(BF)
        for d, out in enumerate((o0, o1, o2, o3)):
            @pl.when(lax.rem(b - place[2] + 4, 4) == d)
            def _():
                out[:, s] = val


def recall(half, place, bound, q, ku, kv, mi, e1, info, got, col, row, at0, at1, gain):
    ch = lambda w: pl.BlockSpec((CH, w), lambda b, p, d: (2 * b + half, 0))
    full = lambda a: pl.BlockSpec(a.shape, lambda b, p, d: (0,) * a.ndim)
    per = SEG // CH
    gs = pltpu.PrefetchScalarGridSpec(
        num_scalar_prefetch=2,
        grid=(4,),
        in_specs=[
            ch(256),
            ch(256),
            ch(512),
            pl.BlockSpec((1, 2, HD, HD), lambda b, p, d: (2 * b + half, 0, 0, 0)),
            full(e1),
            full(info),
            full(got),
            ch(8),
            pl.BlockSpec((8, CH), lambda b, p, d: (0, 2 * b + half)),
            full(row),
            pl.BlockSpec((CH, 256), lambda b, p, d: (jnp.minimum(2 * b + half, per - 1), 0)),
            pl.BlockSpec((CH, 256), lambda b, p, d: (jnp.maximum(2 * b + half - per, 0), 0)),
            full(gain),
        ],
        out_specs=[pl.BlockSpec((CH, 256), lambda b, p, d: (0, 0))] * 4,
        scratch_shapes=[pltpu.VMEM((2, HD, HD), F32), pltpu.VMEM((8, 128), F32)],
    )
    return pl.pallas_call(
        functools.partial(recall_kernel, half),
        grid_spec=gs,
        out_shape=[jax.ShapeDtypeStruct((CH, 256), BF)] * 4,
        name="recall",
        cost_estimate=pl.CostEstimate(flops=400_000_000, transcendentals=0, bytes_accessed=4_000_000),
    )(place, bound, q, ku, kv, mi, e1, info, got, col, row, row, at0, at1, gain)


def ffn_kernel(half, place, gain, tokens, *rest):
    y = place[2]
    heads, own = rest[0:4], rest[4:8]
    sets = (rest[8:14], rest[14:20])
    out, tok, hv, wgu, wd, wo, norm, acc, sem = rest[20:]
    core = place[3]
    count = [0]
    waits = {}

    def copy(key, src, dst):
        c = pltpu.make_async_copy(src, dst, sem.at[count[0]])
        count[0] += 1
        waits.setdefault(key, []).append(c)
        c.start()

    def fetch(kind, i):
        key = (kind, i)
        if i == 0:
            if kind == "out":
                copy(key, own[3], wo.at[0])
            elif kind == "up":
                copy(key, own[0], wgu.at[0, 0])
                copy(key, own[1], wgu.at[1, 0])
            else:
                copy(key, own[2], wd.at[0])
            return
        for which in range(2):
            at = core if which == 0 else 1 - core
            p, q = sets[which][2 * i - 2], sets[which][2 * i - 1]
            if kind == "up":
                copy(key, p.at[pl.ds(0, 352), :], wgu.at[0, i, pl.ds(at * 352, 352), :])
                copy(key, p.at[pl.ds(352, 240), :], wgu.at[1, i, pl.ds(at * 352, 240), :])
                copy(key, q.at[pl.ds(0, 112), :], wgu.at[1, i, pl.ds(at * 352 + 240, 112), :])
            elif kind == "down":
                copy(key, q.at[pl.ds(112, 352), :], wd.at[i, pl.ds(at * 352, 352), :])
            else:
                copy(key, q.at[pl.ds(464, 128), :], wo.at[i, pl.ds(at * 128, 128), :])

    def ready(kind, group):
        for c in waits[(kind, group)]:
            c.wait()

    copy(("in", 0), tokens.at[pl.ds((2 * y + half) * ROWS, ROWS), :], tok)
    for i in range(4):
        copy(("in", 0), heads[i], hv.at[i])
    for i in range(4):
        fetch("out", i)
    fetch("up", 0)
    fetch("down", 0)
    ready("in", 0)
    total = tok[...].astype(F32)
    for i in range(4):
        ready("out", i)
        total = total + dot(hv[i], wo[i])
    for i in (1, 2, 3):
        fetch("up", i)
        fetch("down", i)
    resid = total.astype(BF).astype(F32)
    acc[...] = resid
    norm[...] = (rms(resid, 1e-5) * gain[...].astype(F32)).astype(BF)

    def step(i, carry):
        for index in range(4):
            @pl.when(i == index)
            def _():
                ready("up", index)
                ready("down", index)

        n = norm[...]
        g = dot_t(n, wgu[0, i])
        u = dot_t(n, wgu[1, i])
        hid = (g / (1.0 + jnp.exp(-g)) * u).astype(BF)
        acc[...] += dot(hid, wd[i])
        return carry

    lax.fori_loop(0, 4, step, 0)
    out[...] = acc[...].astype(BF)


def ffn(half, place, tokens, gain, heads, own, mine, other):
    d = tokens.shape[1]
    full = lambda a: pl.BlockSpec(a.shape, lambda i, p: (0,) * a.ndim)
    anys = pl.BlockSpec(memory_space=ANY)
    ws = [*own, *mine, *other]
    gs = pltpu.PrefetchScalarGridSpec(
        num_scalar_prefetch=1,
        grid=(1,),
        in_specs=[full(gain)] + [anys] * (1 + len(heads) + len(ws)),
        out_specs=pl.BlockSpec((ROWS, d), lambda i, p: (0, 0)),
        scratch_shapes=[
            pltpu.VMEM((ROWS, d), BF),
            pltpu.VMEM((4, ROWS, 256), BF),
            pltpu.VMEM((2, 4, 704, 1024), BF),
            pltpu.VMEM((4, 704, 1024), BF),
            pltpu.VMEM((4, 256, 1024), BF),
            pltpu.VMEM((ROWS, d), BF),
            pltpu.VMEM((ROWS, d), F32),
            pltpu.SemaphoreType.DMA((39,)),
        ],
    )
    return pl.pallas_call(
        functools.partial(ffn_kernel, half),
        grid_spec=gs,
        out_shape=jax.ShapeDtypeStruct((ROWS, d), BF),
        name="ffn",
    )(place, gain, tokens, *heads, *ws)


def staged(ins, bufs, outs, sem):
    n = len(ins)
    first = [pltpu.make_async_copy(ins[i], bufs[i], sem.at[i]) for i in range(n)]
    second = [pltpu.make_async_copy(bufs[i], outs[i], sem.at[n + i]) for i in range(n)]
    for c in first:
        c.start()
    for a, b in zip(first, second):
        a.wait()
        b.start()
    for c in second:
        c.wait()


def place_kernel(source, got, out, buf, sem):
    n = out.shape[0]
    staged(
        [got.at[source[s], pl.ds(0, PAGE), :] for s in range(n)],
        [buf.at[s] for s in range(n)],
        [out.at[s] for s in range(n)],
        sem,
    )


def place_pages(source, got, count):
    anys = pl.BlockSpec(memory_space=ANY)
    shape = (count, PAGE, got.shape[2])
    return pl.pallas_call(
        place_kernel,
        in_specs=[pl.BlockSpec(memory_space=pltpu.SMEM), anys],
        out_specs=anys,
        out_shape=jax.ShapeDtypeStruct(shape, BF),
        scratch_shapes=[pltpu.VMEM(shape, BF), pltpu.SemaphoreType.DMA((2 * count,))],
        name="place",
    )(source, got)


def join_kernel(spots, place, *refs):
    pieces, out, bufs, sem = refs[: len(spots)], refs[-2 - len(spots)], refs[-1 - len(spots) : -1], refs[-1]
    y = place[2]
    outs = []
    for d, row, n in spots:
        outs.append(out.at[pl.ds(lax.rem(y + d, 4) * (2 * ROWS) + row, n), :])
    staged(pieces, bufs, outs, sem)


def join(place, pieces, spots, into=None):
    anys = pl.BlockSpec(memory_space=ANY)
    rest = [] if into is None else [into]
    width = pieces[0].shape[1]
    return pl.pallas_call(
        functools.partial(join_kernel, spots),
        in_specs=[pl.BlockSpec(memory_space=pltpu.SMEM)] + [anys] * (len(pieces) + len(rest)),
        out_specs=anys,
        out_shape=jax.ShapeDtypeStruct((8 * ROWS, width), BF),
        scratch_shapes=[pltpu.VMEM(p.shape, BF) for p in pieces] + [pltpu.SemaphoreType.DMA((2 * len(pieces),))],
        input_output_aliases={} if into is None else {1 + len(pieces): 0},
        name="join",
    )(place, *pieces, *rest)


def cut_kernel(place, gate, up, down, last, p, q, sem):
    core = place[3]
    copies = [
        pltpu.make_async_copy(gate.at[pl.ds(core * 352, 352), :], p.at[pl.ds(0, 352), :], sem.at[0]),
        pltpu.make_async_copy(up.at[pl.ds(core * 352, 240), :], p.at[pl.ds(352, 240), :], sem.at[1]),
        pltpu.make_async_copy(up.at[pl.ds(core * 352 + 240, 112), :], q.at[pl.ds(0, 112), :], sem.at[2]),
        pltpu.make_async_copy(down.at[pl.ds(core * 352, 352), :], q.at[pl.ds(112, 352), :], sem.at[3]),
        pltpu.make_async_copy(last.at[pl.ds(core * 128, 128), :], q.at[pl.ds(464, 128), :], sem.at[4]),
    ]
    for c in copies:
        c.start()
    for c in copies:
        c.wait()


def cut_weights(place, gate, up, down, last):
    anys = pl.BlockSpec(memory_space=ANY)
    vm = pl.BlockSpec(memory_space=pltpu.VMEM)
    shape = jax.ShapeDtypeStruct((592, gate.shape[1]), BF)
    return pl.pallas_call(
        cut_kernel,
        in_specs=[pl.BlockSpec(memory_space=pltpu.SMEM)] + [anys] * 4,
        out_specs=[vm, vm],
        out_shape=[shape, shape],
        scratch_shapes=[pltpu.SemaphoreType.DMA((5,))],
        name="cut_weights",
    )(place, gate, up, down, last)


def on_device(
    tokens, attn_gain, w_query, w_key, w_value, persist_key, persist_value, log_forget, mem_gain,
    w_out, ffn_gain, w_gate, w_up, w_down, doc_ids, page_owner, page_slot,
):
    count = tokens.shape[0]
    reqs = lax.axis_size("req")
    req, y = lax.axis_index("req"), lax.axis_index("tp")
    core, x, z = req % 2, req // 8, (req // 2) % 4
    place = jnp.stack([req % 8, x, y, core, z]).astype(jnp.int32)
    shift = lambda a, d: lax.ppermute(a, "tp", [(i, (i + d) % 4) for i in range(4)])
    swap = lambda a: lax.ppermute(a, "req", [(i, i ^ 1) for i in range(reqs)])
    tie = lambda *a: lax.optimization_barrier(a)

    gate, up = w_gate.T, w_up.T
    p, qq = cut_weights(place, gate, up, w_down, w_out)
    p1, q3, q1w, p3 = shift(p, 1), shift(qq, -1), shift(qq, 1), shift(p, -1)

    doc = doc_ids.astype(F32)
    row = jnp.concatenate([doc[None], log_forget.T, jnp.zeros((5, count), F32)])
    bound = jnp.concatenate([jnp.full((1,), -1.0, F32), doc[CH - 1 : -1 : CH]])

    q, kv, ku, mi, pay, row, col, outgoing = project(
        page_owner, page_slot, tokens, attn_gain[None], w_query, w_key, w_value, row, reqs
    )

    group8 = [[i * 8 + k for k in range(8)] for i in range(reqs // 8)]
    group4 = [[i * 8 + k for i in range(reqs // 8)] for k in range(8)]
    spread = lambda a, g: lax.all_to_all(a, "req", 0, 0, tiled=True, axis_index_groups=g)
    got8 = spread(pay, group8)

    at0 = attend(q, kv, persist_key, persist_value, col, row, 0)
    at0, got8, bound, ffn_gain = tie(at0, got8, bound, ffn_gain[None])
    e1, info, pay4 = combine(place, got8)
    got4 = spread(pay4, group4)
    q1, at0, _ = tie(q, at0, pay4)
    at1 = attend(q1, kv, persist_key, persist_value, col, row, 1)
    at1, got4, outgoing = tie(at1, got4, outgoing)
    arrived = lax.all_to_all(outgoing, "req", 0, 0, tiled=True)
    at1, p1, q3, q1w, p3 = tie(at1, p1, q3, q1w, p3)
    p2, q2 = shift(p1, 1), shift(q3, -1)

    gain = mem_gain[None]
    own_w = (gate, up, w_down, w_out)
    mem = lambda half: recall(half, place, bound, q, ku, kv, mi, e1, info, got4, col, row, at0, at1, gain)
    send = lambda out: [out[0]] + [shift(out[d], d) for d in (1, 3, 2)]
    p1x, q3x, q1x, p3x = swap(p1), swap(q3), swap(q1w), swap(p3)
    out0 = mem(0)
    tied = tie(*out0, p1x, q3x, q1x, p3x)
    out0, (p1x, q3x, q1x, p3x) = tied[:4], tied[4:]
    heads0 = send(out0)
    out1 = mem(1)
    tied = tie(*out1, *heads0)
    p2, q2, _ = tie(p2, q2, tied[0])
    out1, heads0 = tied[:4], tied[4:]
    heads1 = send(out1)
    p2x, q2x = swap(p2), swap(q2)
    mine, other = [p1, q1w, p3, q3, p2, q2], [p1x, q1x, p3x, q3x, p2x, q2x]

    slots = arrived[:, PAGE, 0].astype(F32)
    wanted = slots[None, :] == (jnp.arange(count // PAGE) + 1).astype(F32)[:, None]
    source = jnp.sum(jnp.where(wanted, jnp.arange(reqs)[None, :], 0), axis=1).astype(jnp.int32)
    kv_cache = place_pages(jnp.clip(source, 0, reqs - 1), arrived, count // PAGE)

    feed = lambda half, heads: ffn(
        half, place, tokens, ffn_gain, heads, own_w, mine, other
    )
    R, H = ROWS, ROWS // 2
    own0 = feed(0, heads0)
    own0, *heads1 = tie(own0, *heads1)
    a0, b0 = shift(own0, 1), shift(own0, -1)
    own1 = feed(1, heads1)
    a1, b1 = shift(own1, 1), shift(own1, -1)
    lo0, hi0 = shift(a0[:H], 1), shift(b0[H:], -1)
    joined = join(place, [own0, a0, b0, own1], ((0, 0, R), (3, 0, R), (1, 0, R), (0, R, R)))
    a1, b1, joined, kv_cache = tie(a1, b1, joined, kv_cache)
    lo1, hi1 = shift(a1[:H], 1), shift(b1[H:], -1)
    joined = join(place, [a1, b1, lo0, hi0], ((3, R, R), (1, R, R), (2, 0, H), (2, H, H)), joined)
    lo1, hi1, joined = tie(lo1, hi1, joined)
    at = (y + 2) % 4 * (2 * R) + R
    layer_out = lax.dynamic_update_slice(joined, lo1, (at, 0))
    layer_out = lax.dynamic_update_slice(layer_out, hi1, (at + H, 0))
    return layer_out, kv_cache


def solution(mesh):
    return jax.shard_map(
        on_device,
        mesh=mesh,
        in_specs=(
            P("req", None), P(), P(None, "tp"), P(None, "tp"), P(None, "tp"), P(None, "tp"), P(None, "tp"),
            P("req", "tp"), P("tp"), P("tp", None), P(), P(None, "tp"), P(None, "tp"), P("tp", None),
            P("req"), P("req"), P("req"),
        ),
        out_specs=(P("req", None), P("req", None, "tp")),
        check_vma=False,
    )
```

```python
import functools
import math

import jax
import jax.numpy as jnp
from jax import lax
from jax.experimental import pallas as pl
from jax.experimental.pallas import tpu as pltpu
from jax.sharding import PartitionSpec as P

HD = 128
SEG = 1024
PAGE = 128
CH = 256
ROWS = 256
F32 = jnp.float32
BF = jnp.bfloat16
ANY = pl.ANY


def rms(x, eps):
    return x * lax.rsqrt(jnp.mean(x * x, axis=-1, keepdims=True) + eps)


def dot(a, b):
    return jnp.dot(a, b, preferred_element_type=F32)


def dot_t(a, b):
    return lax.dot_general(a, b, (((1,), (1,)), ((), ())), preferred_element_type=F32)


def dot_l(a, b):
    return lax.dot_general(a, b, (((0,), (0,)), ((), ())), preferred_element_type=F32)


def tri(n, lower=True):
    r = lax.broadcasted_iota(jnp.int32, (n, n), 0)
    c = lax.broadcasted_iota(jnp.int32, (n, n), 1)
    return (r >= c) if lower else (r <= c)


def split3(x):
    hi = x.astype(BF).astype(F32)
    mid = (x - hi).astype(BF).astype(F32)
    return hi, mid, x - hi - mid


def running(info):
    parts = jnp.concatenate(split3(info), axis=0).astype(BF)
    c = dot(parts, tri(info.shape[1], False).astype(F32).astype(BF))
    c = c[0:8] + c[8:16] + c[16:24]
    return jnp.where(lax.broadcasted_iota(jnp.int32, info.shape, 0) == 0, info, c)


def normed(tok, gain, out):
    g = gain[...].astype(F32)
    for b in range(CH // 32):
        r = slice(b * 32, (b + 1) * 32)
        out[r, :] = (rms(tok[r, :].astype(F32), 1e-5) * g).astype(BF)


def project_kernel(owner, slot, tok0, tok1, tok2, gain, wq, wk, wv, row, q_out, kv_out, ku_out, min_out, pay_out, cr_out, cc_out, sent, st, misc, buf, n0, n1, codes, sem):
    i = pl.program_id(0)
    here = CH // PAGE
    last_sem = 2 * here

    @pl.when(i == 0)
    def _():
        st[...] = jnp.zeros_like(st)
        misc[...] = jnp.full_like(misc, -1.0)
        misc[0:2, :] = jnp.zeros((2, 128), F32)
        codes[...] = jnp.zeros_like(codes)
        for p in range(owner.shape[0]):
            codes[owner[p]] = jnp.broadcast_to((slot[p] + 1).astype(F32), codes.shape[1:]).astype(BF)
        pltpu.make_async_copy(codes, sent.at[:, pl.ds(PAGE, 8), :], sem.at[last_sem]).start()
        normed(tok0, gain, n0)

    copies = []
    for j, (now, tok, later) in enumerate(((n0, tok1, n1), (n1, tok2, n0))):
        r = slice(j * CH, (j + 1) * CH)
        n = now[...]
        k = dot(n, wk[...]).astype(BF)
        v = dot(n, wv[...]).astype(BF)
        q_out[r, :] = dot(n, wq[...]).astype(BF)
        for h in range(2):
            s = slice(h * HD, (h + 1) * HD)
            kv_out[r, 2 * h * HD : (2 * h + 1) * HD] = k[:, s]
            kv_out[r, (2 * h + 1) * HD : (2 * h + 2) * HD] = v[:, s]
            for p in range(here):
                w = slice(p * PAGE, (p + 1) * PAGE)
                buf[j * here + p, :, 2 * h * HD : (2 * h + 1) * HD] = k[w, s]
                buf[j * here + p, :, (2 * h + 1) * HD : (2 * h + 2) * HD] = v[w, s]
        for p in range(here):
            m = j * here + p
            c = pltpu.make_async_copy(buf.at[m], sent.at[owner[i * 2 * here + m], pl.ds(0, PAGE), :], sem.at[m])
            c.start()
            copies.append(c)
        normed(tok, gain, later)
        cr = running(row[:, r])
        cc = cr.T
        cr_out[:, r] = cr
        cc_out[r, :] = cc
        last = cr[0:1, CH - 1 : CH]
        same = (cc[:, 0:1] == last).astype(F32)
        last_row = jnp.broadcast_to(last, (1, 128))
        cont = (last_row == misc[2:3, :]).astype(F32)
        for h in range(2):
            s = slice(h * HD, (h + 1) * HD)
            ku = rms(k[:, s].astype(F32), 1e-6) * (1.0 / math.sqrt(HD))
            ku_out[r, s] = ku.astype(BF)
            end_h = cr[1 + h : 2 + h, CH - 1 : CH]
            w = jnp.exp(end_h - cc[:, 1 + h : 2 + h]) * same
            add = dot_l((ku * w).astype(BF), v[:, s])
            end_row = jnp.broadcast_to(end_h, (1, 128))
            old = st[h]
            min_out[j, h] = old
            st[h] = old * (jnp.exp(end_row) * cont) + add
            misc[h : h + 1, :] = misc[h : h + 1, :] + end_row
        misc[2:3, :] = last_row

    @pl.when(i == pl.num_programs(0) - 1)
    def _():
        write_payload(pay_out, st, misc[0:1, :], misc[1:2, :], misc[2:3, :])
        pltpu.make_async_copy(codes, sent.at[:, pl.ds(PAGE, 8), :], sem.at[last_sem]).wait()

    for c in copies:
        c.wait()


def write_payload(out, st, l0, l1, last):
    hi = jnp.floor(last * (1.0 / 256.0))
    rows = [*split3(l0), *split3(l1), hi, last - hi * 256.0]
    tail = jnp.concatenate(rows, axis=0).astype(BF)
    for i in range(out.shape[0]):
        for h in range(2):
            out[i, h * HD : (h + 1) * HD, :] = st[h].astype(BF)
        out[i, 2 * HD : 2 * HD + 8, :] = tail


def read_payload(ref, j):
    s = ref[j, 2 * HD : 2 * HD + 8, :].astype(F32)
    l0 = s[0:1] + s[1:2] + s[2:3]
    l1 = s[3:4] + s[4:5] + s[5:6]
    return l0, l1, s[6:7] * 256.0 + s[7:8]


def project(owner, slot, tokens, gain, wq, wk, wv, row, reqs):
    t, d = tokens.shape
    tile = 512
    n = t // tile
    c = tile // CH
    full = lambda a: pl.BlockSpec(a.shape, lambda i, o, l: (0,) * a.ndim)
    rows = lambda w: pl.BlockSpec((tile, w), lambda i, o, l: (i, 0))
    lanes = pl.BlockSpec((8, tile), lambda i, o, l: (0, i))
    gs = pltpu.PrefetchScalarGridSpec(
        num_scalar_prefetch=2,
        grid=(n,),
        in_specs=[
            pl.BlockSpec((CH, d), lambda i, o, l: (0, 0)),
            pl.BlockSpec((CH, d), lambda i, o, l: (2 * i + 1, 0)),
            pl.BlockSpec((CH, d), lambda i, o, l: (jnp.minimum(2 * i + 2, 2 * n - 1), 0)),
            full(gain), full(wq), full(wk), full(wv), lanes,
        ],
        out_specs=[
            rows(256),
            rows(512),
            rows(256),
            pl.BlockSpec((c, 2, HD, HD), lambda i, o, l: (i, 0, 0, 0)),
            pl.BlockSpec((8, 264, 128), lambda i, o, l: (0, 0, 0)),
            lanes,
            rows(8),
            pl.BlockSpec(memory_space=ANY),
        ],
        scratch_shapes=[
            pltpu.VMEM((2, HD, HD), F32),
            pltpu.VMEM((8, 128), F32),
            pltpu.VMEM((tile // PAGE, PAGE, 512), BF),
            pltpu.VMEM((CH, d), BF),
            pltpu.VMEM((CH, d), BF),
            pltpu.VMEM((reqs, 8, 512), BF),
            pltpu.SemaphoreType.DMA((tile // PAGE + 1,)),
        ],
    )
    return pl.pallas_call(
        project_kernel,
        grid_spec=gs,
        out_shape=[
            jax.ShapeDtypeStruct((t, 256), BF),
            jax.ShapeDtypeStruct((t, 512), BF),
            jax.ShapeDtypeStruct((t, 256), BF),
            jax.ShapeDtypeStruct((t // CH, 2, HD, HD), F32),
            jax.ShapeDtypeStruct((8, 264, 128), BF),
            jax.ShapeDtypeStruct((8, t), F32),
            jax.ShapeDtypeStruct((t, 8), F32),
            jax.ShapeDtypeStruct((reqs, PAGE + 8, 512), BF),
        ],
        name="project",
    )(owner, slot, tokens, tokens, tokens, gain, wq, wk, wv, row)


def combine_kernel(place, got, e_out, info_out, pay_out, st):
    g = place[0]
    st[...] = jnp.zeros_like(st)
    e_out[...] = jnp.zeros_like(e_out)
    cur = jnp.full((1, 128), -1.0, F32)
    t0 = t1 = jnp.zeros((1, 128), F32)
    i0, i1, il = t0, t1, cur
    for j in range(8):
        @pl.when(g == j)
        def _():
            e_out[...] = st[...]

        here = g == j
        i0, i1, il = jnp.where(here, t0, i0), jnp.where(here, t1, i1), jnp.where(here, cur, il)
        l0, l1, last = read_payload(got, j)
        cont = (cur == last).astype(F32)
        for h, l in ((0, l0), (1, l1)):
            st[h] = st[h] * (jnp.exp(l) * cont) + got[j, h * HD : (h + 1) * HD, :].astype(F32)
        t0, t1, cur = t0 + l0, t1 + l1, last
    info_out[...] = jnp.concatenate([i0, i1, il, jnp.zeros((5, 128), F32)], axis=0)
    write_payload(pay_out, st, t0, t1, cur)


def combine(place, got):
    vm = pl.BlockSpec(memory_space=pltpu.VMEM)
    return pl.pallas_call(
        combine_kernel,
        in_specs=[pl.BlockSpec(memory_space=pltpu.SMEM), vm],
        out_specs=[vm, vm, vm],
        out_shape=[
            jax.ShapeDtypeStruct((2, HD, HD), F32),
            jax.ShapeDtypeStruct((8, 128), F32),
            jax.ShapeDtypeStruct((4, 264, 128), BF),
        ],
        scratch_shapes=[pltpu.VMEM((2, HD, HD), F32)],
        name="combine",
    )(place, got)


def attend_kernel(q, k, v, pk, pv, col, row, out):
    scale = 1.0 / math.sqrt(HD)
    c = scale * math.log2(math.e)
    mask = tri(CH)
    for i in range(SEG // CH):
        r = slice(i * CH, (i + 1) * CH)
        qi = q[r, :]
        doc = col[r, 0:1]
        sp = dot_t(qi, pk[...])
        sd = dot_t(qi, k[r, :])
        sd = jnp.where(mask & (doc == row[0:1, r]), sd, -1e30)
        m = jnp.maximum(jnp.max(sp, axis=-1, keepdims=True), jnp.max(sd, axis=-1, keepdims=True))
        if i:
            e = slice(0, i * CH)
            so = dot_t(qi, k[e, :])
            so = jnp.where(doc == row[0:1, e], so, -1e30)
            m = jnp.maximum(m, jnp.max(so, axis=-1, keepdims=True))
        wp = jnp.exp2((sp - m) * c)
        wd = jnp.exp2((sd - m) * c)
        total = jnp.sum(wp, axis=-1, keepdims=True) + jnp.sum(wd, axis=-1, keepdims=True)
        acc = dot(wp.astype(BF), pv[...]) + dot(wd.astype(BF), v[r, :])
        if i:
            wo = jnp.exp2((so - m) * c)
            total = total + jnp.sum(wo, axis=-1, keepdims=True)
            acc = acc + dot(wo.astype(BF), v[e, :])
        out[r, :] = acc / total


def attend(q, kv, pk, pv, col, row, seg, h0=0, heads=2):
    return pl.pallas_call(
        attend_kernel,
        grid=(heads,),
        in_specs=[
            pl.BlockSpec((SEG, HD), lambda h: (seg, h + h0)),
            pl.BlockSpec((SEG, HD), lambda h: (seg, 2 * (h + h0))),
            pl.BlockSpec((SEG, HD), lambda h: (seg, 2 * (h + h0) + 1)),
            pl.BlockSpec((16, HD), lambda h: (0, h + h0)),
            pl.BlockSpec((16, HD), lambda h: (0, h + h0)),
            pl.BlockSpec((SEG, 8), lambda h: (seg, 0)),
            pl.BlockSpec((8, SEG), lambda h: (0, seg)),
        ],
        out_specs=pl.BlockSpec((SEG, HD), lambda h: (0, h)),
        out_shape=jax.ShapeDtypeStruct((SEG, heads * HD), F32),
        name="attend",
        cost_estimate=pl.CostEstimate(flops=700_000_000 * heads, transcendentals=0, bytes_accessed=2_000_000 * heads),
    )(q, kv, kv, pk, pv, col, row)


def recall_kernel(half, place, bound, q, ku, kv, mi, e1, info, got, col, row, rows, at0, at1, gain, o0, o1, o2, o3, pst, pdoc):
    b = pl.program_id(0)
    chunk = 2 * b + half

    @pl.when(b == 0)
    def _():
        x, g = place[1], place[0]
        st = [jnp.zeros((HD, HD), F32)] * 2
        cur = jnp.full((1, 128), -1.0, F32)
        pst[...] = jnp.zeros_like(pst)
        il = cur
        for j in range(4):
            here = x == j
            il = jnp.where(here, cur, il)
            for h in range(2):
                pst[h] = jnp.where(here, st[h], pst[h])
            l0, l1, last = read_payload(got, j)
            cont = (cur == last).astype(F32)
            for h, l in ((0, l0), (1, l1)):
                st[h] = st[h] * (jnp.exp(l) * cont) + got[j, h * HD : (h + 1) * HD, :].astype(F32)
            cur = last
        glast = info[2:3, :]
        first = g == 0
        ok = jnp.where(first, 1.0, (il == glast).astype(F32))
        for h in range(2):
            pst[h] = pst[h] * (jnp.exp(info[h : h + 1, :]) * ok) + e1[h]
        pdoc[0:1, :] = jnp.where(first, il, glast)

    mask = tri(CH)
    pos = lax.broadcasted_iota(jnp.int32, rows.shape, 1)
    ends = (pos < chunk * CH) & (lax.rem(pos, CH) == CH - 1)
    pre = jnp.sum(jnp.where(ends, rows[...], 0.0), axis=1, keepdims=True)
    doc = col[:, 0:1]
    pdoc_row = pdoc[0:1, :]
    carried = jnp.where(chunk == 0, pdoc_row, bound[chunk])
    joined = (carried == pdoc_row).astype(F32)
    live = (doc == carried[:, 0:1]).astype(F32)
    ok = mask & (doc == row[0:1, :])
    for h in range(2):
        s = slice(h * HD, (h + 1) * HD)
        qh = q[:, s]
        cc = col[:, 1 + h : 2 + h]
        dec = jnp.exp(jnp.where(ok, cc - row[1 + h : 2 + h, :], -1e30))
        inner = (dot_t(qh, ku[:, s]) * dec).astype(BF)
        rec = dot(inner, kv[:, (2 * h + 1) * HD : (2 * h + 2) * HD])
        f = jnp.exp(jnp.broadcast_to(pre[1 + h : 2 + h, :], (1, 128))) * joined
        m = mi[0, h] + pst[h] * f
        rec = rec + dot(qh, m.astype(BF)) * (jnp.exp(cc) * live)
        qw = qh.astype(F32)
        rec = rec * (lax.rsqrt(jnp.mean(qw * qw, axis=-1, keepdims=True) + 1e-6) * (1.0 / math.sqrt(HD)))
        at = jnp.where(chunk < SEG // CH, at0[:, s], at1[:, s])
        val = (at + rms(rec, 1e-5) * gain[:, s]).astype(BF)
        for d, out in enumerate((o0, o1, o2, o3)):
            @pl.when(lax.rem(b - place[2] + 4, 4) == d)
            def _():
                out[:, s] = val


def recall(half, place, bound, q, ku, kv, mi, e1, info, got, col, row, at0, at1, gain):
    ch = lambda w: pl.BlockSpec((CH, w), lambda b, p, d: (2 * b + half, 0))
    full = lambda a: pl.BlockSpec(a.shape, lambda b, p, d: (0,) * a.ndim)
    per = SEG // CH
    gs = pltpu.PrefetchScalarGridSpec(
        num_scalar_prefetch=2,
        grid=(4,),
        in_specs=[
            ch(256),
            ch(256),
            ch(512),
            pl.BlockSpec((1, 2, HD, HD), lambda b, p, d: (2 * b + half, 0, 0, 0)),
            full(e1),
            full(info),
            full(got),
            ch(8),
            pl.BlockSpec((8, CH), lambda b, p, d: (0, 2 * b + half)),
            full(row),
            pl.BlockSpec((CH, 256), lambda b, p, d: (jnp.minimum(2 * b + half, per - 1), 0)),
            pl.BlockSpec((CH, 256), lambda b, p, d: (jnp.maximum(2 * b + half - per, 0), 0)),
            full(gain),
        ],
        out_specs=[pl.BlockSpec((CH, 256), lambda b, p, d: (0, 0))] * 4,
        scratch_shapes=[pltpu.VMEM((2, HD, HD), F32), pltpu.VMEM((8, 128), F32)],
    )
    return pl.pallas_call(
        functools.partial(recall_kernel, half),
        grid_spec=gs,
        out_shape=[jax.ShapeDtypeStruct((CH, 256), BF)] * 4,
        name="recall",
        cost_estimate=pl.CostEstimate(flops=400_000_000, transcendentals=0, bytes_accessed=4_000_000),
    )(place, bound, q, ku, kv, mi, e1, info, got, col, row, row, at0, at1, gain)


def ffn_kernel(half, place, gain, tokens, *rest):
    y = place[2]
    heads, own = rest[0:4], rest[4:8]
    sets = (rest[8:14], rest[14:20])
    out, tok, hv, wgu, wd, wo, norm, acc, sem = rest[20:]
    core = place[3]
    count = [0]
    waits = {}

    def copy(key, src, dst):
        c = pltpu.make_async_copy(src, dst, sem.at[count[0]])
        count[0] += 1
        waits.setdefault(key, []).append(c)
        c.start()

    def fetch(kind, i):
        key = (kind, i)
        if i == 0:
            if kind == "out":
                copy(key, own[3], wo.at[0])
            elif kind == "up":
                copy(key, own[0], wgu.at[0, 0])
                copy(key, own[1], wgu.at[1, 0])
            else:
                copy(key, own[2], wd.at[0])
            return
        for which in range(2):
            at = core if which == 0 else 1 - core
            p, q = sets[which][2 * i - 2], sets[which][2 * i - 1]
            if kind == "up":
                copy(key, p.at[pl.ds(0, 352), :], wgu.at[0, i, pl.ds(at * 352, 352), :])
                copy(key, p.at[pl.ds(352, 240), :], wgu.at[1, i, pl.ds(at * 352, 240), :])
                copy(key, q.at[pl.ds(0, 112), :], wgu.at[1, i, pl.ds(at * 352 + 240, 112), :])
            elif kind == "down":
                copy(key, q.at[pl.ds(112, 352), :], wd.at[i, pl.ds(at * 352, 352), :])
            else:
                copy(key, q.at[pl.ds(464, 128), :], wo.at[i, pl.ds(at * 128, 128), :])

    def ready(kind, group):
        for c in waits[(kind, group)]:
            c.wait()

    copy(("in", 0), tokens.at[pl.ds((2 * y + half) * ROWS, ROWS), :], tok)
    for i in range(4):
        copy(("in", 0), heads[i], hv.at[i])
    for i in range(4):
        fetch("out", i)
    fetch("up", 0)
    fetch("down", 0)
    ready("in", 0)
    total = tok[...].astype(F32)
    for i in range(4):
        ready("out", i)
        total = total + dot(hv[i], wo[i])
    for i in (1, 2, 3):
        fetch("up", i)
        fetch("down", i)
    resid = total.astype(BF).astype(F32)
    acc[...] = resid
    norm[...] = (rms(resid, 1e-5) * gain[...].astype(F32)).astype(BF)

    def step(i, carry):
        for index in range(4):
            @pl.when(i == index)
            def _():
                ready("up", index)
                ready("down", index)

        n = norm[...]
        g = dot_t(n, wgu[0, i])
        u = dot_t(n, wgu[1, i])
        hid = (g / (1.0 + jnp.exp(-g)) * u).astype(BF)
        acc[...] += dot(hid, wd[i])
        return carry

    lax.fori_loop(0, 4, step, 0)
    out[...] = acc[...].astype(BF)


def ffn(half, place, tokens, gain, heads, own, mine, other):
    d = tokens.shape[1]
    full = lambda a: pl.BlockSpec(a.shape, lambda i, p: (0,) * a.ndim)
    anys = pl.BlockSpec(memory_space=ANY)
    ws = [*own, *mine, *other]
    gs = pltpu.PrefetchScalarGridSpec(
        num_scalar_prefetch=1,
        grid=(1,),
        in_specs=[full(gain)] + [anys] * (1 + len(heads) + len(ws)),
        out_specs=pl.BlockSpec((ROWS, d), lambda i, p: (0, 0)),
        scratch_shapes=[
            pltpu.VMEM((ROWS, d), BF),
            pltpu.VMEM((4, ROWS, 256), BF),
            pltpu.VMEM((2, 4, 704, 1024), BF),
            pltpu.VMEM((4, 704, 1024), BF),
            pltpu.VMEM((4, 256, 1024), BF),
            pltpu.VMEM((ROWS, d), BF),
            pltpu.VMEM((ROWS, d), F32),
            pltpu.SemaphoreType.DMA((39,)),
        ],
    )
    return pl.pallas_call(
        functools.partial(ffn_kernel, half),
        grid_spec=gs,
        out_shape=jax.ShapeDtypeStruct((ROWS, d), BF),
        name="ffn",
    )(place, gain, tokens, *heads, *ws)


def staged(ins, bufs, outs, sem):
    n = len(ins)
    first = [pltpu.make_async_copy(ins[i], bufs[i], sem.at[i]) for i in range(n)]
    second = [pltpu.make_async_copy(bufs[i], outs[i], sem.at[n + i]) for i in range(n)]
    for c in first:
        c.start()
    for a, b in zip(first, second):
        a.wait()
        b.start()
    for c in second:
        c.wait()


def place_kernel(source, got, out, buf, sem):
    n = out.shape[0]
    staged(
        [got.at[source[s], pl.ds(0, PAGE), :] for s in range(n)],
        [buf.at[s] for s in range(n)],
        [out.at[s] for s in range(n)],
        sem,
    )


def place_pages(source, got, count):
    anys = pl.BlockSpec(memory_space=ANY)
    shape = (count, PAGE, got.shape[2])
    return pl.pallas_call(
        place_kernel,
        in_specs=[pl.BlockSpec(memory_space=pltpu.SMEM), anys],
        out_specs=anys,
        out_shape=jax.ShapeDtypeStruct(shape, BF),
        scratch_shapes=[pltpu.VMEM(shape, BF), pltpu.SemaphoreType.DMA((2 * count,))],
        name="place",
    )(source, got)


def join_kernel(spots, place, *refs):
    pieces, out, bufs, sem = refs[: len(spots)], refs[-2 - len(spots)], refs[-1 - len(spots) : -1], refs[-1]
    y = place[2]
    outs = []
    for d, row, n in spots:
        outs.append(out.at[pl.ds(lax.rem(y + d, 4) * (2 * ROWS) + row, n), :])
    staged(pieces, bufs, outs, sem)


def join(place, pieces, spots, into=None):
    anys = pl.BlockSpec(memory_space=ANY)
    rest = [] if into is None else [into]
    width = pieces[0].shape[1]
    return pl.pallas_call(
        functools.partial(join_kernel, spots),
        in_specs=[pl.BlockSpec(memory_space=pltpu.SMEM)] + [anys] * (len(pieces) + len(rest)),
        out_specs=anys,
        out_shape=jax.ShapeDtypeStruct((8 * ROWS, width), BF),
        scratch_shapes=[pltpu.VMEM(p.shape, BF) for p in pieces] + [pltpu.SemaphoreType.DMA((2 * len(pieces),))],
        input_output_aliases={} if into is None else {1 + len(pieces): 0},
        name="join",
    )(place, *pieces, *rest)


def cut_kernel(first, place, *refs):
    core = place[3]
    if first:
        gate, up, out, sem = refs
        copies = [
            pltpu.make_async_copy(gate.at[pl.ds(core * 352, 352), :], out.at[pl.ds(0, 352), :], sem.at[0]),
            pltpu.make_async_copy(up.at[pl.ds(core * 352, 240), :], out.at[pl.ds(352, 240), :], sem.at[1]),
        ]
    else:
        up, down, last, out, sem = refs
        copies = [
            pltpu.make_async_copy(up.at[pl.ds(core * 352 + 240, 112), :], out.at[pl.ds(0, 112), :], sem.at[0]),
            pltpu.make_async_copy(down.at[pl.ds(core * 352, 352), :], out.at[pl.ds(112, 352), :], sem.at[1]),
            pltpu.make_async_copy(last.at[pl.ds(core * 128, 128), :], out.at[pl.ds(464, 128), :], sem.at[2]),
        ]
    for c in copies:
        c.start()
    for c in copies:
        c.wait()


def cut_weights(first, place, *weights):
    anys = pl.BlockSpec(memory_space=ANY)
    return pl.pallas_call(
        functools.partial(cut_kernel, first),
        in_specs=[pl.BlockSpec(memory_space=pltpu.SMEM)] + [anys] * len(weights),
        out_specs=pl.BlockSpec(memory_space=pltpu.VMEM),
        out_shape=jax.ShapeDtypeStruct((592, weights[0].shape[1]), BF),
        scratch_shapes=[pltpu.SemaphoreType.DMA((3,))],
        name="cut_weights",
    )(place, *weights)


def on_device(
    tokens, attn_gain, w_query, w_key, w_value, persist_key, persist_value, log_forget, mem_gain,
    w_out, ffn_gain, w_gate, w_up, w_down, doc_ids, page_owner, page_slot,
):
    count = tokens.shape[0]
    reqs = lax.axis_size("req")
    req, y = lax.axis_index("req"), lax.axis_index("tp")
    core, x, z = req % 2, req // 8, (req // 2) % 4
    place = jnp.stack([req % 8, x, y, core, z]).astype(jnp.int32)
    shift = lambda a, d: lax.ppermute(a, "tp", [(i, (i + d) % 4) for i in range(4)])
    swap = lambda a: lax.ppermute(a, "req", [(i, i ^ 1) for i in range(reqs)])
    tie = lambda *a: lax.optimization_barrier(a)

    gate, up = w_gate.T, w_up.T
    p = cut_weights(True, place, gate, up)
    p1, p3 = shift(p, 1), shift(p, -1)
    qq = cut_weights(False, place, up, w_down, w_out)
    q3, q1w = shift(qq, -1), shift(qq, 1)

    doc = doc_ids.astype(F32)
    row = jnp.concatenate([doc[None], log_forget.T, jnp.zeros((5, count), F32)])
    bound = jnp.concatenate([jnp.full((1,), -1.0, F32), doc[CH - 1 : -1 : CH]])

    q, kv, ku, mi, pay, row, col, outgoing = project(
        page_owner, page_slot, tokens, attn_gain[None], w_query, w_key, w_value, row, reqs
    )

    group8 = [[i * 8 + k for k in range(8)] for i in range(reqs // 8)]
    group4 = [[i * 8 + k for i in range(reqs // 8)] for k in range(8)]
    spread = lambda a, g: lax.all_to_all(a, "req", 0, 0, tiled=True, axis_index_groups=g)
    got8 = spread(pay, group8)

    at0 = attend(q, kv, persist_key, persist_value, col, row, 0)
    at0, got8, bound, ffn_gain = tie(at0, got8, bound, ffn_gain[None])
    e1, info, pay4 = combine(place, got8)
    got4 = spread(pay4, group4)
    q1, at0, _ = tie(q, at0, pay4)
    at1 = attend(q1, kv, persist_key, persist_value, col, row, 1)
    at1, got4, outgoing = tie(at1, got4, outgoing)
    arrived = lax.all_to_all(outgoing, "req", 0, 0, tiled=True)
    at1, p1, q3, q1w, p3 = tie(at1, p1, q3, q1w, p3)
    p2, q2 = shift(p1, 1), shift(q3, -1)

    gain = mem_gain[None]
    own_w = (gate, up, w_down, w_out)
    mem = lambda half: recall(half, place, bound, q, ku, kv, mi, e1, info, got4, col, row, at0, at1, gain)
    send = lambda out: [out[0]] + [shift(out[d], d) for d in (1, 3, 2)]
    p1x, q3x, q1x, p3x = swap(p1), swap(q3), swap(q1w), swap(p3)
    out0 = mem(0)
    tied = tie(*out0, p1x, q3x, q1x, p3x)
    out0, (p1x, q3x, q1x, p3x) = tied[:4], tied[4:]
    heads0 = send(out0)
    out1 = mem(1)
    tied = tie(*out1, *heads0)
    p2, q2, _ = tie(p2, q2, tied[0])
    out1, heads0 = tied[:4], tied[4:]
    p2x, q2x = swap(p2), swap(q2)
    early = shift(out1[1], 1), shift(out1[3], 3)
    far, p2x, q2x = tie(out1[2], p2x, q2x)
    heads1 = [out1[0], *early, shift(far, 2)]
    mine, other = [p1, q1w, p3, q3, p2, q2], [p1x, q1x, p3x, q3x, p2x, q2x]

    slots = arrived[:, PAGE, 0].astype(F32)
    wanted = slots[None, :] == (jnp.arange(count // PAGE) + 1).astype(F32)[:, None]
    source = jnp.sum(jnp.where(wanted, jnp.arange(reqs)[None, :], 0), axis=1).astype(jnp.int32)
    kv_cache = place_pages(jnp.clip(source, 0, reqs - 1), arrived, count // PAGE)

    feed = lambda half, heads: ffn(
        half, place, tokens, ffn_gain, heads, own_w, mine, other
    )
    R, H = ROWS, ROWS // 2
    own0 = feed(0, heads0)
    own0, *heads1 = tie(own0, *heads1)
    a0, b0 = shift(own0, 1), shift(own0, -1)
    own1 = feed(1, heads1)
    a1, b1 = shift(own1, 1), shift(own1, -1)
    lo0, hi0 = shift(a0[:H], 1), shift(b0[H:], -1)
    joined = join(place, [own0, a0, b0, own1], ((0, 0, R), (3, 0, R), (1, 0, R), (0, R, R)))
    a1, b1, joined, kv_cache = tie(a1, b1, joined, kv_cache)
    lo1, hi1 = shift(a1[:H], 1), shift(b1[H:], -1)
    joined = join(place, [a1, b1, lo0, hi0], ((3, R, R), (1, R, R), (2, 0, H), (2, H, H)), joined)
    lo1, hi1, joined = tie(lo1, hi1, joined)
    at = (y + 2) % 4 * (2 * R) + R
    layer_out = lax.dynamic_update_slice(joined, lo1, (at, 0))
    layer_out = lax.dynamic_update_slice(layer_out, hi1, (at + H, 0))
    return layer_out, kv_cache


def solution(mesh):
    return jax.shard_map(
        on_device,
        mesh=mesh,
        in_specs=(
            P("req", None), P(), P(None, "tp"), P(None, "tp"), P(None, "tp"), P(None, "tp"), P(None, "tp"),
            P("req", "tp"), P("tp"), P("tp", None), P(), P(None, "tp"), P(None, "tp"), P("tp", None),
            P("req"), P("req"), P("req"),
        ),
        out_specs=(P("req", None), P("req", None, "tp")),
        check_vma=False,
    )
```

```python
import functools
import math

import jax
import jax.numpy as jnp
from jax import lax
from jax.experimental import pallas as pl
from jax.experimental.pallas import tpu as pltpu
from jax.sharding import PartitionSpec as P

HD = 128
SEG = 1024
PAGE = 128
CH = 256
ROWS = 256
F32 = jnp.float32
BF = jnp.bfloat16
ANY = pl.ANY


def rms(x, eps):
    return x * lax.rsqrt(jnp.mean(x * x, axis=-1, keepdims=True) + eps)


def dot(a, b):
    return jnp.dot(a, b, preferred_element_type=F32)


def dot_t(a, b):
    return lax.dot_general(a, b, (((1,), (1,)), ((), ())), preferred_element_type=F32)


def dot_l(a, b):
    return lax.dot_general(a, b, (((0,), (0,)), ((), ())), preferred_element_type=F32)


def tri(n, lower=True):
    r = lax.broadcasted_iota(jnp.int32, (n, n), 0)
    c = lax.broadcasted_iota(jnp.int32, (n, n), 1)
    return (r >= c) if lower else (r <= c)


def split3(x):
    hi = x.astype(BF).astype(F32)
    mid = (x - hi).astype(BF).astype(F32)
    return hi, mid, x - hi - mid


def running(info):
    parts = jnp.concatenate(split3(info), axis=0).astype(BF)
    c = dot(parts, tri(info.shape[1], False).astype(F32).astype(BF))
    c = c[0:8] + c[8:16] + c[16:24]
    return jnp.where(lax.broadcasted_iota(jnp.int32, info.shape, 0) == 0, info, c)


def normed(tok, gain, out):
    g = gain[...].astype(F32)
    for b in range(CH // 32):
        r = slice(b * 32, (b + 1) * 32)
        out[r, :] = (rms(tok[r, :].astype(F32), 1e-5) * g).astype(BF)


def project_kernel(owner, slot, tok0, tok1, tok2, gain, wq, wk, wv, row, q_out, kv_out, ku_out, min_out, pay_out, cr_out, cc_out, sent, st, misc, buf, n0, n1, codes, sem):
    i = pl.program_id(0)
    here = CH // PAGE
    last_sem = 2 * here

    @pl.when(i == 0)
    def _():
        st[...] = jnp.zeros_like(st)
        misc[...] = jnp.full_like(misc, -1.0)
        misc[0:2, :] = jnp.zeros((2, 128), F32)
        codes[...] = jnp.zeros_like(codes)
        for p in range(owner.shape[0]):
            codes[owner[p]] = jnp.broadcast_to((slot[p] + 1).astype(F32), codes.shape[1:]).astype(BF)
        pltpu.make_async_copy(codes, sent.at[:, pl.ds(PAGE, 8), :], sem.at[last_sem]).start()
        normed(tok0, gain, n0)

    copies = []
    for j, (now, tok, later) in enumerate(((n0, tok1, n1), (n1, tok2, n0))):
        r = slice(j * CH, (j + 1) * CH)
        n = now[...]
        k = dot(n, wk[...]).astype(BF)
        v = dot(n, wv[...]).astype(BF)
        q_out[r, :] = dot(n, wq[...]).astype(BF)
        for h in range(2):
            s = slice(h * HD, (h + 1) * HD)
            kv_out[r, 2 * h * HD : (2 * h + 1) * HD] = k[:, s]
            kv_out[r, (2 * h + 1) * HD : (2 * h + 2) * HD] = v[:, s]
            for p in range(here):
                w = slice(p * PAGE, (p + 1) * PAGE)
                buf[j * here + p, :, 2 * h * HD : (2 * h + 1) * HD] = k[w, s]
                buf[j * here + p, :, (2 * h + 1) * HD : (2 * h + 2) * HD] = v[w, s]
        for p in range(here):
            m = j * here + p
            c = pltpu.make_async_copy(buf.at[m], sent.at[owner[i * 2 * here + m], pl.ds(0, PAGE), :], sem.at[m])
            c.start()
            copies.append(c)
        normed(tok, gain, later)
        cr = running(row[:, r])
        cc = cr.T
        cr_out[:, r] = cr
        cc_out[r, :] = cc
        last = cr[0:1, CH - 1 : CH]
        same = (cc[:, 0:1] == last).astype(F32)
        last_row = jnp.broadcast_to(last, (1, 128))
        cont = (last_row == misc[2:3, :]).astype(F32)
        for h in range(2):
            s = slice(h * HD, (h + 1) * HD)
            ku = rms(k[:, s].astype(F32), 1e-6) * (1.0 / math.sqrt(HD))
            ku_out[r, s] = ku.astype(BF)
            end_h = cr[1 + h : 2 + h, CH - 1 : CH]
            w = jnp.exp(end_h - cc[:, 1 + h : 2 + h]) * same
            add = dot_l((ku * w).astype(BF), v[:, s])
            end_row = jnp.broadcast_to(end_h, (1, 128))
            old = st[h]
            min_out[j, h] = old
            st[h] = old * (jnp.exp(end_row) * cont) + add
            misc[h : h + 1, :] = misc[h : h + 1, :] + end_row
        misc[2:3, :] = last_row

    @pl.when(i == pl.num_programs(0) - 1)
    def _():
        write_payload(pay_out, st, misc[0:1, :], misc[1:2, :], misc[2:3, :])
        pltpu.make_async_copy(codes, sent.at[:, pl.ds(PAGE, 8), :], sem.at[last_sem]).wait()

    for c in copies:
        c.wait()


def write_payload(out, st, l0, l1, last):
    hi = jnp.floor(last * (1.0 / 256.0))
    rows = [*split3(l0), *split3(l1), hi, last - hi * 256.0]
    tail = jnp.concatenate(rows, axis=0).astype(BF)
    for i in range(out.shape[0]):
        for h in range(2):
            out[i, h * HD : (h + 1) * HD, :] = st[h].astype(BF)
        out[i, 2 * HD : 2 * HD + 8, :] = tail


def read_payload(ref, j):
    s = ref[j, 2 * HD : 2 * HD + 8, :].astype(F32)
    l0 = s[0:1] + s[1:2] + s[2:3]
    l1 = s[3:4] + s[4:5] + s[5:6]
    return l0, l1, s[6:7] * 256.0 + s[7:8]


def project(owner, slot, tokens, gain, wq, wk, wv, row, reqs):
    t, d = tokens.shape
    tile = 512
    n = t // tile
    c = tile // CH
    full = lambda a: pl.BlockSpec(a.shape, lambda i, o, l: (0,) * a.ndim)
    rows = lambda w: pl.BlockSpec((tile, w), lambda i, o, l: (i, 0))
    lanes = pl.BlockSpec((8, tile), lambda i, o, l: (0, i))
    gs = pltpu.PrefetchScalarGridSpec(
        num_scalar_prefetch=2,
        grid=(n,),
        in_specs=[
            pl.BlockSpec((CH, d), lambda i, o, l: (0, 0)),
            pl.BlockSpec((CH, d), lambda i, o, l: (2 * i + 1, 0)),
            pl.BlockSpec((CH, d), lambda i, o, l: (jnp.minimum(2 * i + 2, 2 * n - 1), 0)),
            full(gain), full(wq), full(wk), full(wv), lanes,
        ],
        out_specs=[
            rows(256),
            rows(512),
            rows(256),
            pl.BlockSpec((c, 2, HD, HD), lambda i, o, l: (i, 0, 0, 0)),
            pl.BlockSpec((8, 264, 128), lambda i, o, l: (0, 0, 0)),
            lanes,
            rows(8),
            pl.BlockSpec(memory_space=ANY),
        ],
        scratch_shapes=[
            pltpu.VMEM((2, HD, HD), F32),
            pltpu.VMEM((8, 128), F32),
            pltpu.VMEM((tile // PAGE, PAGE, 512), BF),
            pltpu.VMEM((CH, d), BF),
            pltpu.VMEM((CH, d), BF),
            pltpu.VMEM((reqs, 8, 512), BF),
            pltpu.SemaphoreType.DMA((tile // PAGE + 1,)),
        ],
    )
    return pl.pallas_call(
        project_kernel,
        grid_spec=gs,
        out_shape=[
            jax.ShapeDtypeStruct((t, 256), BF),
            jax.ShapeDtypeStruct((t, 512), BF),
            jax.ShapeDtypeStruct((t, 256), BF),
            jax.ShapeDtypeStruct((t // CH, 2, HD, HD), F32),
            jax.ShapeDtypeStruct((8, 264, 128), BF),
            jax.ShapeDtypeStruct((8, t), F32),
            jax.ShapeDtypeStruct((t, 8), F32),
            jax.ShapeDtypeStruct((reqs, PAGE + 8, 512), BF),
        ],
        name="project",
    )(owner, slot, tokens, tokens, tokens, gain, wq, wk, wv, row)


def combine_kernel(place, got, e_out, info_out, pay_out, st):
    g = place[0]
    st[...] = jnp.zeros_like(st)
    e_out[...] = jnp.zeros_like(e_out)
    cur = jnp.full((1, 128), -1.0, F32)
    t0 = t1 = jnp.zeros((1, 128), F32)
    i0, i1, il = t0, t1, cur
    for j in range(8):
        @pl.when(g == j)
        def _():
            e_out[...] = st[...]

        here = g == j
        i0, i1, il = jnp.where(here, t0, i0), jnp.where(here, t1, i1), jnp.where(here, cur, il)
        l0, l1, last = read_payload(got, j)
        cont = (cur == last).astype(F32)
        for h, l in ((0, l0), (1, l1)):
            st[h] = st[h] * (jnp.exp(l) * cont) + got[j, h * HD : (h + 1) * HD, :].astype(F32)
        t0, t1, cur = t0 + l0, t1 + l1, last
    info_out[...] = jnp.concatenate([i0, i1, il, jnp.zeros((5, 128), F32)], axis=0)
    write_payload(pay_out, st, t0, t1, cur)


def combine(place, got):
    vm = pl.BlockSpec(memory_space=pltpu.VMEM)
    return pl.pallas_call(
        combine_kernel,
        in_specs=[pl.BlockSpec(memory_space=pltpu.SMEM), vm],
        out_specs=[vm, vm, vm],
        out_shape=[
            jax.ShapeDtypeStruct((2, HD, HD), F32),
            jax.ShapeDtypeStruct((8, 128), F32),
            jax.ShapeDtypeStruct((4, 264, 128), BF),
        ],
        scratch_shapes=[pltpu.VMEM((2, HD, HD), F32)],
        name="combine",
    )(place, got)


def attend_kernel(q, k, v, pk, pv, col, row, out):
    scale = 1.0 / math.sqrt(HD)
    c = scale * math.log2(math.e)
    mask = tri(CH)
    for i in range(SEG // CH):
        r = slice(i * CH, (i + 1) * CH)
        qi = q[r, :]
        doc = col[r, 0:1]
        sp = dot_t(qi, pk[...])
        sd = dot_t(qi, k[r, :])
        sd = jnp.where(mask & (doc == row[0:1, r]), sd, -1e30)
        m = jnp.maximum(jnp.max(sp, axis=-1, keepdims=True), jnp.max(sd, axis=-1, keepdims=True))
        if i:
            e = slice(0, i * CH)
            so = dot_t(qi, k[e, :])
            so = jnp.where(doc == row[0:1, e], so, -1e30)
            m = jnp.maximum(m, jnp.max(so, axis=-1, keepdims=True))
        wp = jnp.exp2((sp - m) * c)
        wd = jnp.exp2((sd - m) * c)
        total = jnp.sum(wp, axis=-1, keepdims=True) + jnp.sum(wd, axis=-1, keepdims=True)
        acc = dot(wp.astype(BF), pv[...]) + dot(wd.astype(BF), v[r, :])
        if i:
            wo = jnp.exp2((so - m) * c)
            total = total + jnp.sum(wo, axis=-1, keepdims=True)
            acc = acc + dot(wo.astype(BF), v[e, :])
        out[r, :] = acc / total


def attend(q, kv, pk, pv, col, row, seg, h0=0, heads=2):
    return pl.pallas_call(
        attend_kernel,
        grid=(heads,),
        in_specs=[
            pl.BlockSpec((SEG, HD), lambda h: (seg, h + h0)),
            pl.BlockSpec((SEG, HD), lambda h: (seg, 2 * (h + h0))),
            pl.BlockSpec((SEG, HD), lambda h: (seg, 2 * (h + h0) + 1)),
            pl.BlockSpec((16, HD), lambda h: (0, h + h0)),
            pl.BlockSpec((16, HD), lambda h: (0, h + h0)),
            pl.BlockSpec((SEG, 8), lambda h: (seg, 0)),
            pl.BlockSpec((8, SEG), lambda h: (0, seg)),
        ],
        out_specs=pl.BlockSpec((SEG, HD), lambda h: (0, h)),
        out_shape=jax.ShapeDtypeStruct((SEG, heads * HD), F32),
        name="attend",
        cost_estimate=pl.CostEstimate(flops=700_000_000 * heads, transcendentals=0, bytes_accessed=2_000_000 * heads),
    )(q, kv, kv, pk, pv, col, row)


def recall_kernel(half, place, bound, q, ku, kv, mi, e1, info, got, col, row, rows, at0, at1, gain, o0, o1, o2, o3, pst, pdoc):
    b = pl.program_id(0)
    chunk = 2 * b + half

    @pl.when(b == 0)
    def _():
        x, g = place[1], place[0]
        st = [jnp.zeros((HD, HD), F32)] * 2
        cur = jnp.full((1, 128), -1.0, F32)
        pst[...] = jnp.zeros_like(pst)
        il = cur
        for j in range(4):
            here = x == j
            il = jnp.where(here, cur, il)
            for h in range(2):
                pst[h] = jnp.where(here, st[h], pst[h])
            l0, l1, last = read_payload(got, j)
            cont = (cur == last).astype(F32)
            for h, l in ((0, l0), (1, l1)):
                st[h] = st[h] * (jnp.exp(l) * cont) + got[j, h * HD : (h + 1) * HD, :].astype(F32)
            cur = last
        glast = info[2:3, :]
        first = g == 0
        ok = jnp.where(first, 1.0, (il == glast).astype(F32))
        for h in range(2):
            pst[h] = pst[h] * (jnp.exp(info[h : h + 1, :]) * ok) + e1[h]
        pdoc[0:1, :] = jnp.where(first, il, glast)

    mask = tri(CH)
    pos = lax.broadcasted_iota(jnp.int32, rows.shape, 1)
    ends = (pos < chunk * CH) & (lax.rem(pos, CH) == CH - 1)
    pre = jnp.sum(jnp.where(ends, rows[...], 0.0), axis=1, keepdims=True)
    doc = col[:, 0:1]
    pdoc_row = pdoc[0:1, :]
    carried = jnp.where(chunk == 0, pdoc_row, bound[chunk])
    joined = (carried == pdoc_row).astype(F32)
    live = (doc == carried[:, 0:1]).astype(F32)
    ok = mask & (doc == row[0:1, :])
    for h in range(2):
        s = slice(h * HD, (h + 1) * HD)
        qh = q[:, s]
        cc = col[:, 1 + h : 2 + h]
        dec = jnp.exp(jnp.where(ok, cc - row[1 + h : 2 + h, :], -1e30))
        inner = (dot_t(qh, ku[:, s]) * dec).astype(BF)
        rec = dot(inner, kv[:, (2 * h + 1) * HD : (2 * h + 2) * HD])
        f = jnp.exp(jnp.broadcast_to(pre[1 + h : 2 + h, :], (1, 128))) * joined
        m = mi[0, h] + pst[h] * f
        rec = rec + dot(qh, m.astype(BF)) * (jnp.exp(cc) * live)
        qw = qh.astype(F32)
        rec = rec * (lax.rsqrt(jnp.mean(qw * qw, axis=-1, keepdims=True) + 1e-6) * (1.0 / math.sqrt(HD)))
        at = jnp.where(chunk < SEG // CH, at0[:, s], at1[:, s])
        val = (at + rms(rec, 1e-5) * gain[:, s]).astype(BF)
        for d, out in enumerate((o0, o1, o2, o3)):
            @pl.when(lax.rem(b - place[2] + 4, 4) == d)
            def _():
                out[:, s] = val


def recall(half, place, bound, q, ku, kv, mi, e1, info, got, col, row, at0, at1, gain):
    ch = lambda w: pl.BlockSpec((CH, w), lambda b, p, d: (2 * b + half, 0))
    full = lambda a: pl.BlockSpec(a.shape, lambda b, p, d: (0,) * a.ndim)
    per = SEG // CH
    gs = pltpu.PrefetchScalarGridSpec(
        num_scalar_prefetch=2,
        grid=(4,),
        in_specs=[
            ch(256),
            ch(256),
            ch(512),
            pl.BlockSpec((1, 2, HD, HD), lambda b, p, d: (2 * b + half, 0, 0, 0)),
            full(e1),
            full(info),
            full(got),
            ch(8),
            pl.BlockSpec((8, CH), lambda b, p, d: (0, 2 * b + half)),
            full(row),
            pl.BlockSpec((CH, 256), lambda b, p, d: (jnp.minimum(2 * b + half, per - 1), 0)),
            pl.BlockSpec((CH, 256), lambda b, p, d: (jnp.maximum(2 * b + half - per, 0), 0)),
            full(gain),
        ],
        out_specs=[pl.BlockSpec((CH, 256), lambda b, p, d: (0, 0))] * 4,
        scratch_shapes=[pltpu.VMEM((2, HD, HD), F32), pltpu.VMEM((8, 128), F32)],
    )
    return pl.pallas_call(
        functools.partial(recall_kernel, half),
        grid_spec=gs,
        out_shape=[jax.ShapeDtypeStruct((CH, 256), BF)] * 4,
        name="recall",
        cost_estimate=pl.CostEstimate(flops=400_000_000, transcendentals=0, bytes_accessed=4_000_000),
    )(place, bound, q, ku, kv, mi, e1, info, got, col, row, row, at0, at1, gain)


def ffn_kernel(half, place, gain, tokens, *rest):
    y = place[2]
    heads, own = rest[0:4], rest[4:8]
    sets = (rest[8:14], rest[14:20])
    out, tok, hv, wgu, wd, wo, norm, acc, sem = rest[20:]
    core = place[3]
    count = [0]
    waits = {}

    def copy(key, src, dst):
        c = pltpu.make_async_copy(src, dst, sem.at[count[0]])
        count[0] += 1
        waits.setdefault(key, []).append(c)
        c.start()

    def fetch(kind, i):
        key = (kind, i)
        if i == 0:
            if kind == "out":
                copy(key, own[3], wo.at[0])
            elif kind == "up":
                copy(key, own[0], wgu.at[0, 0])
                copy(key, own[1], wgu.at[1, 0])
            else:
                copy(key, own[2], wd.at[0])
            return
        for which in range(2):
            at = core if which == 0 else 1 - core
            p, q = sets[which][2 * i - 2], sets[which][2 * i - 1]
            if kind == "up":
                copy(key, p.at[pl.ds(0, 352), :], wgu.at[0, i, pl.ds(at * 352, 352), :])
                copy(key, p.at[pl.ds(352, 240), :], wgu.at[1, i, pl.ds(at * 352, 240), :])
                copy(key, q.at[pl.ds(0, 112), :], wgu.at[1, i, pl.ds(at * 352 + 240, 112), :])
            elif kind == "down":
                copy(key, q.at[pl.ds(112, 352), :], wd.at[i, pl.ds(at * 352, 352), :])
            else:
                copy(key, q.at[pl.ds(464, 128), :], wo.at[i, pl.ds(at * 128, 128), :])

    def ready(kind, group):
        for c in waits[(kind, group)]:
            c.wait()

    copy(("in", 0), tokens.at[pl.ds((2 * y + half) * ROWS, ROWS), :], tok)
    for i in range(4):
        copy(("in", 0), heads[i], hv.at[i])
    for i in range(4):
        fetch("out", i)
    fetch("up", 0)
    fetch("down", 0)
    ready("in", 0)
    total = tok[...].astype(F32)
    for i in range(4):
        ready("out", i)
        total = total + dot(hv[i], wo[i])
    for i in (1, 2, 3):
        fetch("up", i)
        fetch("down", i)
    resid = total.astype(BF).astype(F32)
    acc[...] = resid
    norm[...] = (rms(resid, 1e-5) * gain[...].astype(F32)).astype(BF)

    def step(i, carry):
        for index in range(4):
            @pl.when(i == index)
            def _():
                ready("up", index)
                ready("down", index)

        n = norm[...]
        g = dot_t(n, wgu[0, i])
        u = dot_t(n, wgu[1, i])
        hid = (g / (1.0 + jnp.exp(-g)) * u).astype(BF)
        acc[...] += dot(hid, wd[i])
        return carry

    lax.fori_loop(0, 4, step, 0)
    out[...] = acc[...].astype(BF)


def ffn(half, place, tokens, gain, heads, own, mine, other):
    d = tokens.shape[1]
    full = lambda a: pl.BlockSpec(a.shape, lambda i, p: (0,) * a.ndim)
    anys = pl.BlockSpec(memory_space=ANY)
    ws = [*own, *mine, *other]
    gs = pltpu.PrefetchScalarGridSpec(
        num_scalar_prefetch=1,
        grid=(1,),
        in_specs=[full(gain)] + [anys] * (1 + len(heads) + len(ws)),
        out_specs=pl.BlockSpec((ROWS, d), lambda i, p: (0, 0)),
        scratch_shapes=[
            pltpu.VMEM((ROWS, d), BF),
            pltpu.VMEM((4, ROWS, 256), BF),
            pltpu.VMEM((2, 4, 704, 1024), BF),
            pltpu.VMEM((4, 704, 1024), BF),
            pltpu.VMEM((4, 256, 1024), BF),
            pltpu.VMEM((ROWS, d), BF),
            pltpu.VMEM((ROWS, d), F32),
            pltpu.SemaphoreType.DMA((39,)),
        ],
    )
    return pl.pallas_call(
        functools.partial(ffn_kernel, half),
        grid_spec=gs,
        out_shape=jax.ShapeDtypeStruct((ROWS, d), BF),
        name="ffn",
    )(place, gain, tokens, *heads, *ws)


def staged(ins, bufs, outs, sem):
    n = len(ins)
    first = [pltpu.make_async_copy(ins[i], bufs[i], sem.at[i]) for i in range(n)]
    second = [pltpu.make_async_copy(bufs[i], outs[i], sem.at[n + i]) for i in range(n)]
    for c in first:
        c.start()
    for a, b in zip(first, second):
        a.wait()
        b.start()
    for c in second:
        c.wait()


def place_kernel(source, got, out, buf, sem):
    n = out.shape[0]
    staged(
        [got.at[source[s], pl.ds(0, PAGE), :] for s in range(n)],
        [buf.at[s] for s in range(n)],
        [out.at[s] for s in range(n)],
        sem,
    )


def place_pages(source, got, count):
    anys = pl.BlockSpec(memory_space=ANY)
    shape = (count, PAGE, got.shape[2])
    return pl.pallas_call(
        place_kernel,
        in_specs=[pl.BlockSpec(memory_space=pltpu.SMEM), anys],
        out_specs=anys,
        out_shape=jax.ShapeDtypeStruct(shape, BF),
        scratch_shapes=[pltpu.VMEM(shape, BF), pltpu.SemaphoreType.DMA((2 * count,))],
        name="place",
    )(source, got)


def join_kernel(spots, place, *refs):
    pieces, out, bufs, sem = refs[: len(spots)], refs[-2 - len(spots)], refs[-1 - len(spots) : -1], refs[-1]
    y = place[2]
    outs = []
    for d, row, n in spots:
        outs.append(out.at[pl.ds(lax.rem(y + d, 4) * (2 * ROWS) + row, n), :])
    staged(pieces, bufs, outs, sem)


def join(place, pieces, spots, into=None):
    anys = pl.BlockSpec(memory_space=ANY)
    rest = [] if into is None else [into]
    width = pieces[0].shape[1]
    return pl.pallas_call(
        functools.partial(join_kernel, spots),
        in_specs=[pl.BlockSpec(memory_space=pltpu.SMEM)] + [anys] * (len(pieces) + len(rest)),
        out_specs=anys,
        out_shape=jax.ShapeDtypeStruct((8 * ROWS, width), BF),
        scratch_shapes=[pltpu.VMEM(p.shape, BF) for p in pieces] + [pltpu.SemaphoreType.DMA((2 * len(pieces),))],
        input_output_aliases={} if into is None else {1 + len(pieces): 0},
        name="join",
    )(place, *pieces, *rest)


def cut_kernel(place, gate, up, down, last, p, q, sem):
    core = place[3]
    copies = [
        pltpu.make_async_copy(gate.at[pl.ds(core * 352, 352), :], p.at[pl.ds(0, 352), :], sem.at[0]),
        pltpu.make_async_copy(up.at[pl.ds(core * 352, 240), :], p.at[pl.ds(352, 240), :], sem.at[1]),
        pltpu.make_async_copy(up.at[pl.ds(core * 352 + 240, 112), :], q.at[pl.ds(0, 112), :], sem.at[2]),
        pltpu.make_async_copy(down.at[pl.ds(core * 352, 352), :], q.at[pl.ds(112, 352), :], sem.at[3]),
        pltpu.make_async_copy(last.at[pl.ds(core * 128, 128), :], q.at[pl.ds(464, 128), :], sem.at[4]),
    ]
    for c in copies:
        c.start()
    for c in copies:
        c.wait()


def cut_weights(place, gate, up, down, last):
    anys = pl.BlockSpec(memory_space=ANY)
    vm = pl.BlockSpec(memory_space=pltpu.VMEM)
    shape = jax.ShapeDtypeStruct((592, gate.shape[1]), BF)
    return pl.pallas_call(
        cut_kernel,
        in_specs=[pl.BlockSpec(memory_space=pltpu.SMEM)] + [anys] * 4,
        out_specs=[vm, vm],
        out_shape=[shape, shape],
        scratch_shapes=[pltpu.SemaphoreType.DMA((5,))],
        name="cut_weights",
    )(place, gate, up, down, last)


def on_device(
    tokens, attn_gain, w_query, w_key, w_value, persist_key, persist_value, log_forget, mem_gain,
    w_out, ffn_gain, w_gate, w_up, w_down, doc_ids, page_owner, page_slot,
):
    count = tokens.shape[0]
    reqs = lax.axis_size("req")
    req, y = lax.axis_index("req"), lax.axis_index("tp")
    core, x, z = req % 2, req // 8, (req // 2) % 4
    place = jnp.stack([req % 8, x, y, core, z]).astype(jnp.int32)
    shift = lambda a, d: lax.ppermute(a, "tp", [(i, (i + d) % 4) for i in range(4)])
    swap = lambda a: lax.ppermute(a, "req", [(i, i ^ 1) for i in range(reqs)])
    tie = lambda *a: lax.optimization_barrier(a)

    gate, up = w_gate.T, w_up.T
    p, qq = cut_weights(place, gate, up, w_down, w_out)
    p1, q3, q1w, p3 = shift(p, 1), shift(qq, -1), shift(qq, 1), shift(p, -1)

    doc = doc_ids.astype(F32)
    row = jnp.concatenate([doc[None], log_forget.T, jnp.zeros((5, count), F32)])
    bound = jnp.concatenate([jnp.full((1,), -1.0, F32), doc[CH - 1 : -1 : CH]])

    q, kv, ku, mi, pay, row, col, outgoing = project(
        page_owner, page_slot, tokens, attn_gain[None], w_query, w_key, w_value, row, reqs
    )

    group8 = [[i * 8 + k for k in range(8)] for i in range(reqs // 8)]
    group4 = [[i * 8 + k for i in range(reqs // 8)] for k in range(8)]
    spread = lambda a, g: lax.all_to_all(a, "req", 0, 0, tiled=True, axis_index_groups=g)
    got8 = spread(pay, group8)

    at0 = attend(q, kv, persist_key, persist_value, col, row, 0)
    at0, got8, bound, ffn_gain = tie(at0, got8, bound, ffn_gain[None])
    e1, info, pay4 = combine(place, got8)
    got4 = spread(pay4, group4)
    q1, at0, _ = tie(q, at0, pay4)
    at1 = attend(q1, kv, persist_key, persist_value, col, row, 1)
    at1, got4, outgoing = tie(at1, got4, outgoing)
    arrived = lax.all_to_all(outgoing, "req", 0, 0, tiled=True)
    at1, p1, q3, q1w, p3 = tie(at1, p1, q3, q1w, p3)
    p2, q2 = shift(p1, 1), shift(q3, -1)

    gain = mem_gain[None]
    own_w = (gate, up, w_down, w_out)
    mem = lambda half: recall(half, place, bound, q, ku, kv, mi, e1, info, got4, col, row, at0, at1, gain)
    send = lambda out: [out[0]] + [shift(out[d], d) for d in (1, 3, 2)]
    p1x, q3x, q1x, p3x = swap(p1), swap(q3), swap(q1w), swap(p3)
    out0 = mem(0)
    tied = tie(*out0, p1x, q3x, q1x, p3x)
    out0, (p1x, q3x, q1x, p3x) = tied[:4], tied[4:]
    heads0 = send(out0)
    out1 = mem(1)
    tied = tie(*out1, *heads0)
    p2, q2, _ = tie(p2, q2, tied[0])
    out1, heads0 = tied[:4], tied[4:]
    p2x, q2x = swap(p2), swap(q2)
    early = shift(out1[1], 1), shift(out1[3], 3)
    far, p2x, q2x = tie(out1[2], p2x, q2x)
    heads1 = [out1[0], *early, shift(far, 2)]
    mine, other = [p1, q1w, p3, q3, p2, q2], [p1x, q1x, p3x, q3x, p2x, q2x]

    slots = arrived[:, PAGE, 0].astype(F32)
    wanted = slots[None, :] == (jnp.arange(count // PAGE) + 1).astype(F32)[:, None]
    source = jnp.sum(jnp.where(wanted, jnp.arange(reqs)[None, :], 0), axis=1).astype(jnp.int32)
    kv_cache = place_pages(jnp.clip(source, 0, reqs - 1), arrived, count // PAGE)

    feed = lambda half, heads: ffn(
        half, place, tokens, ffn_gain, heads, own_w, mine, other
    )
    R, H = ROWS, ROWS // 2
    own0 = feed(0, heads0)
    own0, *heads1 = tie(own0, *heads1)
    a0, b0 = shift(own0, 1), shift(own0, -1)
    own1 = feed(1, heads1)
    a1, b1 = shift(own1, 1), shift(own1, -1)
    lo0, hi0 = shift(a0[:H], 1), shift(b0[H:], -1)
    joined = join(place, [own0, a0, b0, own1], ((0, 0, R), (3, 0, R), (1, 0, R), (0, R, R)))
    a1, b1, joined, kv_cache = tie(a1, b1, joined, kv_cache)
    lo1, hi1 = shift(a1[:H], 1), shift(b1[H:], -1)
    joined = join(place, [a1, b1, lo0, hi0], ((3, R, R), (1, R, R), (2, 0, H), (2, H, H)), joined)
    lo1, hi1, joined = tie(lo1, hi1, joined)
    at = (y + 2) % 4 * (2 * R) + R
    layer_out = lax.dynamic_update_slice(joined, lo1, (at, 0))
    layer_out = lax.dynamic_update_slice(layer_out, hi1, (at + H, 0))
    return layer_out, kv_cache


def solution(mesh):
    return jax.shard_map(
        on_device,
        mesh=mesh,
        in_specs=(
            P("req", None), P(), P(None, "tp"), P(None, "tp"), P(None, "tp"), P(None, "tp"), P(None, "tp"),
            P("req", "tp"), P("tp"), P("tp", None), P(), P(None, "tp"), P(None, "tp"), P("tp", None),
            P("req"), P("req"), P("req"),
        ),
        out_specs=(P("req", None), P("req", None, "tp")),
        check_vma=False,
    )
```
